128 devices in a mesh: src: 32 (over x, z, core), tgt: 4 (over y).
Axes of the slice: x: 4, y: 4, z: 4, core: 2. Of those that a mesh axis runs over, the one named last changes fastest.
Arguments:
- src_pts: float32 [3, 512, 256], P(None, 'src'), may hold values from -8 to 9
- src_mass: float32 [512, 256], P('src'), may hold values from 0.25 to 4
- tgt_pts: float32 [3, 256, 1024], P(None, None, 'tgt'), may hold values from -6 to 6
- tgt_mass: float32 [256, 1024], P(None, 'tgt'), may hold values from 0.25 to 4
- listed: int32 [512, 4, 8], P('src', 'tgt'), may hold values from 0 to 255, all different within a row
- live: int32 [512, 4], P('src', 'tgt'), may hold values from 1 to 8, 16 in all within a row
Outputs:
- fine_f: float32 [512, 256], P('src')
- fine_g: float32 [256, 1024], P('src', 'tgt')
The draws below stay inside these ranges and needn't reach their ends.
Inputs may be any that keep to these rules, and one draw needn't show every extreme that they name: Within one row listed[c, t, :] the entries are distinct; only the first live[c, t] of them are used. For each source cluster c the counts live[c, :] add up to 16.
All inputs are finite; a program needn't handle non-finite values. No bound on the sum of `live` on one device may be relied on, other than what follows from the above.
Results may differ from the reference program's by a relative error of at most 0.0003.
Values sent between devices are 32-bit elements; how exact they have to be, the bound alone decides.
No kernel may reach another device: no remote copies, remote signals or barrier semaphores. Data moves between devices by JAX's collectives and lax.ppermute only.
A program may use at most 128 MiB of HBM per device.

```python
import math
import jax
import jax.numpy as jnp
import numpy as np
from jax import lax

NT_DEV = 256
PTS = 256
KSH = 8
SRC_CL = 512
TGT_CL = 1024
N_TGT = 4


def draw_src_pts(key, part):
    base_key = jax.random.fold_in(key, 11)
    noise_key, shift_key = jax.random.split(base_key)
    base = jnp.clip(jax.random.normal(noise_key, (3, SRC_CL, PTS), jnp.float32), -6.0, 6.0)
    shift = jax.random.uniform(shift_key, (3, SRC_CL, 1), jnp.float32, -2.0, 3.0)
    return (base + shift).astype(jnp.float32)


def level_of(stream_key, extent, shards, smallest, top_value):
    factor_of, own = 1.0, jax.random.fold_in(stream_key, 6)
    for axis_at, blocks in shards:
        steps = jnp.exp(jax.random.uniform(jax.random.fold_in(own, axis_at), (blocks,), jnp.float32, smallest / len(shards), top_value / len(shards)))
        factor_of = factor_of * jnp.repeat(steps, extent[axis_at] // blocks).reshape([-1 if axis == axis_at else 1 for axis in range(len(extent))])
    return factor_of


def choose_distinct(stream_key, rows, number_of, top, lift):
    ranking = jax.random.permutation(jax.random.fold_in(stream_key, 1), number_of)
    pull = ranking
    for power in range(3):
        pull = pull * pull // number_of
    pull = pull * lift // number_of
    chance = jax.random.randint(jax.random.fold_in(stream_key, 2), (rows, number_of), 0, 4096) + pull
    fixed_rows = jax.random.permutation(jax.random.fold_in(stream_key, 3), rows)[jnp.arange(number_of) % rows]
    chance = jnp.where(jnp.arange(rows)[:, None] == fixed_rows[None, :], 1 << 14, chance)
    score = chance * number_of + jnp.arange(number_of)
    return lax.top_k(score.astype(jnp.int32), top)[1].astype(jnp.int32)


def split_up(number_of, total, reach, skew):
    weights = [(1 << 20) // math.isqrt(rank ** skew) + 1 for rank in range(2, number_of + 1)]
    surplus, given = total - reach - (number_of - 1), [1] * (number_of - 1)
    while surplus > 0:
        movable = [i for i in range(number_of - 1) if given[i] < reach]
        mass, budget = sum([weights[i] for i in movable]), surplus
        for i in movable:
            addition = min(reach - given[i], max(1, budget * weights[i] // mass), surplus)
            given[i] = given[i] + addition
            surplus = surplus - addition
    return np.array([reach] + given)


def ragged(rng, number_of, total, limit, slope):
    if number_of == 2:
        one = jax.random.randint(rng, (), max(1, total - limit), min(limit, total - 1) + 1)
        return jnp.stack([one, total - one])
    tallies = jnp.asarray(split_up(number_of, total, limit, slope), jnp.int32)
    twos = (number_of - 1) // 2
    source_of, taker = tallies[1:1 + 2 * twos:2], tallies[2:2 + 2 * twos:2]
    margin = jnp.minimum(source_of - 1, limit - taker)
    passed = jax.random.randint(jax.random.fold_in(rng, 1), (twos,), 0, 1 << 20) % (margin + 1)
    tallies = tallies.at[1:1 + 2 * twos:2].set(source_of - passed).at[2:2 + 2 * twos:2].set(taker + passed)
    return tallies[jax.random.permutation(jax.random.fold_in(rng, 2), number_of)]


def centred(own_key, shape, scale, reach, cuts=(), held_as=jnp.bfloat16):
    result = jax.random.normal(own_key, shape, jnp.float32) * scale
    if len(cuts) > 0:
        result = level_of(own_key, shape, cuts, -0.22, 0.18) * result
    return jnp.clip(result, min=-reach, max=reach).astype(held_as)


def setup_inputs(seed: int = 0) -> dict:
    key_list = jax.random.split(jax.random.key(seed), 7)
    return {
        "src_pts": draw_src_pts(jax.random.fold_in(key_list[6], 71), 0),
        "src_mass": jnp.clip(jnp.exp(math.log(4.0) - 2.7725887 * jax.random.uniform(key_list[1], (SRC_CL, PTS), jnp.float32) ** level_of(key_list[1], (SRC_CL, PTS), ((0, 32),), -0.2, 0.2)), 0.25, 4.0),
        "tgt_pts": centred(key_list[2], (3, PTS, TGT_CL), 1.0, 6.0, ((2, 4),), jnp.float32),
        "tgt_mass": jnp.clip(jnp.exp(math.log(4.0) - 2.7725887 * jax.random.uniform(key_list[3], (PTS, TGT_CL), jnp.float32) ** level_of(key_list[3], (PTS, TGT_CL), ((1, 4),), -0.2, 0.2)), 0.25, 4.0),
        "listed": choose_distinct(key_list[4], SRC_CL * N_TGT, NT_DEV, KSH, 256).reshape((SRC_CL, N_TGT, KSH)),
        "live": jax.vmap(lambda own: ragged(own, N_TGT, N_TGT * KSH // 2, KSH, 2))(jax.random.split(key_list[5], SRC_CL)).reshape((SRC_CL, N_TGT)).astype(jnp.int32),
    }


EPS = 0.1
NEG = -1.0e30


def half_dist(first_set, second_set):
    cross_term = jnp.dot(first_set.T, second_set, precision=lax.Precision.HIGHEST, preferred_element_type=jnp.float32)
    first_sq = jnp.sum(first_set * first_set, axis=0)
    second_sq = jnp.sum(second_set * second_set, axis=0)
    return 0.5 * (first_sq[:, None] + second_sq[None, :]) - cross_term


def log_sum(values, along):
    top_val = jnp.max(values, axis=along, keepdims=True)
    return jnp.squeeze(top_val, along) + jnp.log(jnp.sum(jnp.exp(values - top_val), axis=along))


def reference(src_pts, src_mass, tgt_pts, tgt_mass, listed, live):
    src_total = jnp.sum(src_mass, axis=1)
    src_cent = jnp.sum(src_pts * src_mass[None], axis=2) / src_total[None]
    tgt_total = jnp.sum(tgt_mass, axis=0)
    tgt_cent = jnp.sum(tgt_pts * tgt_mass[None], axis=1) / tgt_total[None]
    coarse_cost = half_dist(src_cent, tgt_cent)
    coarse_f = -EPS * log_sum(jnp.log(tgt_total)[None, :] - coarse_cost / EPS, 1)
    coarse_g = -EPS * log_sum(jnp.log(src_total)[:, None] + (coarse_f[:, None] - coarse_cost) / EPS, 0)
    shard_base = (jnp.arange(N_TGT, dtype=jnp.int32) * NT_DEV)[:, None]
    slot_ids = jnp.arange(KSH, dtype=jnp.int32)[None, :]

    def one_cluster(cluster):
        columns = (shard_base + listed[cluster]).reshape(-1).astype(jnp.int32)
        alive_slot = (slot_ids < live[cluster][:, None]).reshape(-1)
        blocks = tgt_pts[:, :, columns].reshape(3, -1)
        base_term = jnp.log(tgt_mass[:, columns]) + coarse_g[columns][None, :] / EPS
        base_term = jnp.where(alive_slot[None, :], base_term, NEG).reshape(-1)
        cost_tile = half_dist(src_pts[:, cluster, :], blocks)
        fine_row = -EPS * log_sum(base_term[None, :] - cost_tile / EPS, 1)
        scores = jnp.log(src_mass[cluster])[:, None] + (fine_row[:, None] - cost_tile) / EPS
        col_top = jnp.max(scores, axis=0)
        col_sum = jnp.sum(jnp.exp(scores - col_top[None, :]), axis=0)
        target_ids = jnp.where(alive_slot, columns, TGT_CL).astype(jnp.int32)
        return fine_row, col_top.reshape(PTS, -1), col_sum.reshape(PTS, -1), target_ids

    fine_f, col_top, col_sum, target_ids = lax.map(one_cluster, jnp.arange(SRC_CL, dtype=jnp.int32))
    col_top = jnp.transpose(col_top, (1, 0, 2)).reshape(PTS, -1)
    col_sum = jnp.transpose(col_sum, (1, 0, 2)).reshape(PTS, -1)
    flat_ids = target_ids.reshape(-1)
    top_all = jnp.full((PTS, TGT_CL + 1), NEG, jnp.float32).at[:, flat_ids].max(col_top)
    sum_all = jnp.zeros((PTS, TGT_CL + 1), jnp.float32).at[:, flat_ids].add(col_sum * jnp.exp(col_top - top_all[:, flat_ids]))
    top_all = top_all[:, :TGT_CL]
    sum_all = sum_all[:, :TGT_CL]
    fallback = (-coarse_g / EPS)[None, :]
    joined = jnp.maximum(top_all, fallback)
    grand_total = sum_all * jnp.exp(top_all - joined) + jnp.exp(fallback - joined)
    fine_g = -EPS * (joined + jnp.log(grand_total))
    return fine_f, fine_g
```

```python
import functools
import math

import jax
import jax.numpy as jnp
from jax import lax
from jax.experimental import pallas as pl
from jax.experimental.pallas import tpu as pltpu
from jax.sharding import PartitionSpec as P

EPS = 0.1
NEG = -1e30
ALPHA = math.log2(math.e) / EPS
UNSCALE = EPS * math.log(2.0)
F32 = jnp.float32
VMEM = pl.BlockSpec(memory_space=pltpu.VMEM)
SMEM = pl.BlockSpec(memory_space=pltpu.SMEM)
ANY = pl.BlockSpec(memory_space=pl.ANY)


def lane_iota(shape):
    return lax.broadcasted_iota(jnp.int32, shape, len(shape) - 1)


def centroid_kernel(pos, sp, sm, tp, tm, row_out, own_out):
    s, t = pos[0], pos[1]
    mass = sm[...]
    total = jnp.sum(mass, axis=1, keepdims=True)
    inv = 1.0 / total
    cols = [jnp.sum(sp[d] * mass, axis=1, keepdims=True) * inv for d in range(3)]
    cols.append(jnp.log2(total))
    lane = lane_iota((mass.shape[0], 128))
    z = jnp.zeros((mass.shape[0], 128), F32)
    for q in range(4):
        z = jnp.where(lane == q, cols[q], z)
    zt = jnp.concatenate([z, jnp.zeros((128 - mass.shape[0], 128), F32)], axis=0).T
    lane = lane_iota((1, 128))
    row = jnp.zeros((1, 128), F32)
    for q in range(4):
        piece = pltpu.roll(zt[q : q + 1, :], lax.rem(128 - 4 * t, 128), 1)
        row = row + pltpu.roll(jnp.where(lane < 4, piece, 0.0), 4 * q, 1)
    weight = tm[...]
    total = jnp.sum(weight, axis=0, keepdims=True)
    inv = 1.0 / total
    rows = [jnp.sum(tp[d] * weight, axis=0, keepdims=True) * inv for d in range(3)]
    rows.append(jnp.log2(total))
    for q in range(4):
        own_out[q : q + 1, :] = rows[q]
        half = jnp.where(s >= 16, rows[q][:, 128:], rows[q][:, :128])
        piece = pltpu.roll(half, lax.rem(128 - 8 * lax.rem(s, 16), 128), 1)
        row = row + pltpu.roll(jnp.where(lane < 8, piece, 0.0), 16 + 8 * q, 1)
    row_out[...] = jnp.broadcast_to(row, row_out.shape)


def row_kernel(listed, live, sp, tp, tm, alive, e_out, m_out, r_out, yt, xc, mcol, scol, ebuf, sems):
    clusters, slots = 16, 8
    y = [tp[d] for d in range(3)]
    base = jnp.log2(tm[...]) - (0.5 * ALPHA) * (y[0] * y[0] + y[1] * y[1] + y[2] * y[2])
    for d in range(3):
        yt[d] = y[d].T
    yt[3] = base.T
    lane = lane_iota((16, 128))

    def flush(b, slot):
        return pltpu.make_async_copy(ebuf.at[slot], e_out.at[b], sems.at[slot])

    def cluster(c, count):
        for d in range(3):
            line = sp[d, pl.ds(c, 1), :] * ALPHA
            xc[d] = jnp.broadcast_to(line, (128, 256)).T

        def block(k, count):
            b = c * slots + k
            slot = lax.rem(count, 2)

            @pl.when(count >= 2)
            def _():
                flush(b, slot).wait()

            at = listed[b]
            rows = [yt[q, pl.ds(at, 1), :] for q in range(4)]
            for i in range(0, 256, 16):
                xs = [xc[d, i : i + 16, :] for d in range(3)]
                halves = []
                for h in (0, 128):
                    v = rows[3][:, h : h + 128] + xs[0] * rows[0][:, h : h + 128]
                    v = v + xs[1] * rows[1][:, h : h + 128]
                    halves.append(v + xs[2] * rows[2][:, h : h + 128])
                top = jnp.max(jnp.maximum(*halves), axis=1, keepdims=True)
                es = [jnp.exp2(v - top) for v in halves]
                total = jnp.sum(es[0] + es[1], axis=1, keepdims=True)
                for h in range(2):
                    ebuf[slot, i : i + 16, 128 * h : 128 * h + 128] = es[h].astype(jnp.bfloat16)
                mcol[i : i + 16, :] = jnp.where(lane == b, top, mcol[i : i + 16, :])
                scol[i : i + 16, :] = jnp.where(lane == b, total, scol[i : i + 16, :])
            flush(b, slot).start()
            return count + 1

        return lax.fori_loop(0, live[c], block, count)

    count = lax.fori_loop(0, clusters, cluster, 0)
    flush(0, lax.rem(count, 2)).wait()
    flush(0, lax.rem(count + 1, 2)).wait()
    xn = (-0.5 * ALPHA) * (sp[0] * sp[0] + sp[1] * sp[1] + sp[2] * sp[2])
    ok = alive[...] > 0
    m = jnp.where(ok, mcol[...].T, 0.0).reshape(clusters, slots, 256) + xn[:, None, :]
    m = m.reshape(clusters * slots, 256)
    m_out[...] = m
    r_out[...] = jnp.where(ok, m + jnp.log2(jnp.where(ok, scol[...].T, 1.0)), NEG)


def log2_sum(parts, axis):
    top = functools.reduce(jnp.maximum, [jnp.max(p, axis=axis, keepdims=True) for p in parts])
    total = sum(jnp.sum(jnp.exp2(p - top), axis=axis, keepdims=True) for p in parts)
    return top + jnp.log2(total)


def coarse_kernel(got, own, m_in, r_in, listed, g_out, mg_out, l_out):
    table = got[...]
    turned = table.T
    tgt = [[turned[16 + 8 * q + li : 17 + 8 * q + li, :] for q in range(4)] for li in range(8)]
    src = [[table[:, 4 * q + ci : 4 * q + ci + 1] for q in range(4)] for ci in range(4)]

    def score(x, y):
        gap = [x[d] - y[d] for d in range(3)]
        return (-0.5 * ALPHA) * (gap[0] * gap[0] + gap[1] * gap[1] + gap[2] * gap[2])

    mine = [own[q : q + 1, :] for q in range(4)]
    terms = []
    for x in src:
        f = -log2_sum([score(x, y) + y[3] for y in tgt], 1)
        terms.append(score(x, mine) + (x[3] + f))
    g = -log2_sum(terms, 0)
    g_out[...] = jnp.broadcast_to(g, g_out.shape)
    slots = listed.shape[0]
    hit = lane_iota((slots, 256)) == listed[...]
    picked = jnp.sum(jnp.where(hit, g, 0.0), axis=1, keepdims=True)
    mg_out[...] = m_in[...] + picked
    r = (r_in[...] + picked).reshape(16, 8, 256)
    l_out[...] = log2_sum([r], 1).reshape(16, 256)


def column_kernel(listed, live, sm, mg, l0, l1, l2, l3, e_in, f_out, s_out, w, st, ebuf, sems):
    clusters, slots = 16, 8
    f = -log2_sum([p[...][None] for p in (l0, l1, l2, l3)], 0)[0]
    f_out[...] = f * UNSCALE
    weights = sm[...][:, None, :] * jnp.exp2(mg[...].reshape(clusters, slots, 256) + f[:, None, :])
    high = weights.astype(jnp.bfloat16).astype(F32)
    w[...] = jnp.concatenate([high, weights - high], axis=1).astype(jnp.bfloat16)
    st[...] = jnp.zeros_like(st)

    def fetch(b, side, k):
        return pltpu.make_async_copy(e_in.at[b], ebuf.at[side, k], sems.at[side, k])

    def start(c, side):
        def one(k, _):
            fetch(c * slots + k, side, k).start()
            return 0

        lax.fori_loop(0, live[c], one, 0)

    start(0, 0)
    sub = lax.broadcasted_iota(jnp.int32, (2 * slots, 256), 0)

    def cluster(c, _):
        side = lax.rem(c, 2)

        @pl.when(c + 1 < clusters)
        def _():
            start(c + 1, 1 - side)

        lhs = w[c]

        def block(k, _):
            fetch(c * slots + k, side, k).wait()
            out = jnp.dot(lhs, ebuf[side, k], preferred_element_type=F32)
            out = jnp.sum(jnp.where((sub & 7) == k, out, 0.0), axis=0, keepdims=True)
            at = listed[c * slots + k]
            st[pl.ds(at, 1), :] = st[pl.ds(at, 1), :] + out
            return 0

        return lax.fori_loop(0, live[c], block, 0)

    lax.fori_loop(0, clusters, cluster, 0)
    s_out[...] = st[...].T.reshape(32, 8, 256)


def on_device(src_pts, src_mass, tgt_pts, tgt_mass, listed, live):
    shape = jax.ShapeDtypeStruct
    s, t = lax.axis_index("src"), lax.axis_index("tgt")
    pos = jnp.stack([s, t]).astype(jnp.int32)
    row, own = pl.pallas_call(
        centroid_kernel,
        out_shape=(shape((128, 128), F32), shape((8, 256), F32)),
        in_specs=[SMEM, VMEM, VMEM, VMEM, VMEM],
        out_specs=(VMEM, VMEM),
        name="centroids",
    )(pos, src_pts, src_mass, tgt_pts, tgt_mass)
    got = lax.all_to_all(row, ("src", "tgt"), split_axis=0, concat_axis=0, tiled=True)
    flat = listed.reshape(128)
    counts = live.reshape(16)
    column = listed.reshape(128, 1)
    alive = (jnp.arange(8, dtype=jnp.int32)[None, :] < counts[:, None]).astype(jnp.int32).reshape(128, 1)
    e, m, r = pl.pallas_call(
        row_kernel,
        out_shape=(shape((128, 256, 256), jnp.bfloat16), shape((128, 256), F32), shape((128, 256), F32)),
        in_specs=[SMEM, SMEM, VMEM, VMEM, VMEM, VMEM],
        out_specs=(ANY, VMEM, VMEM),
        scratch_shapes=[
            pltpu.VMEM((4, 256, 256), F32),
            pltpu.VMEM((3, 256, 128), F32),
            pltpu.VMEM((256, 128), F32),
            pltpu.VMEM((256, 128), F32),
            pltpu.VMEM((2, 256, 256), jnp.bfloat16),
            pltpu.SemaphoreType.DMA((2,)),
        ],
        cost_estimate=pl.CostEstimate(flops=100_000_000, bytes_accessed=10_000_000, transcendentals=5_000_000),
        name="rows",
    )(flat, counts, src_pts, tgt_pts, tgt_mass, alive)
    g, mg, part = pl.pallas_call(
        coarse_kernel,
        out_shape=(shape((8, 256), F32), shape((128, 256), F32), shape((16, 256), F32)),
        in_specs=[VMEM] * 5,
        out_specs=(VMEM, VMEM, VMEM),
        name="coarse",
    )(got, own, m, r, column)
    parts = [part] + [
        lax.ppermute(part, "tgt", [(i, (i + k) % 4) for i in range(4)]) for k in (1, 2, 3)
    ]
    fine_f, sums = pl.pallas_call(
        column_kernel,
        out_shape=(shape((16, 256), F32), shape((32, 8, 256), F32)),
        in_specs=[SMEM, SMEM] + [VMEM] * 6 + [ANY],
        out_specs=(VMEM, VMEM),
        scratch_shapes=[
            pltpu.VMEM((16, 16, 256), jnp.bfloat16),
            pltpu.VMEM((256, 256), F32),
            pltpu.VMEM((2, 8, 256, 256), jnp.bfloat16),
            pltpu.SemaphoreType.DMA((2, 8)),
        ],
        name="columns",
    )(flat, counts, src_mass, mg, *parts, e)
    arrived = lax.all_to_all(sums, "src", split_axis=0, concat_axis=0, tiled=True)
    mass = lax.dynamic_slice_in_dim(tgt_mass, s * 8, 8, 0)
    fine_g = (g - jnp.log2(1.0 + arrived.sum(axis=0) / mass)) * UNSCALE
    return fine_f, fine_g


def solution(mesh):
    placed = (
        P(None, "src", None),
        P("src", None),
        P(None, None, "tgt"),
        P(None, "tgt"),
        P("src", "tgt", None),
        P("src", "tgt"),
    )
    return jax.shard_map(
        on_device,
        mesh=mesh,
        in_specs=placed,
        out_specs=(P("src", None), P("src", "tgt")),
        check_vma=False,
    )
```

```python
import functools
import math

import jax
import jax.numpy as jnp
from jax import lax
from jax.experimental import pallas as pl
from jax.experimental.pallas import tpu as pltpu
from jax.sharding import PartitionSpec as P

EPS = 0.1
NEG = -1e30
ALPHA = math.log2(math.e) / EPS
UNSCALE = EPS * math.log(2.0)
F32, BF16, I32 = jnp.float32, jnp.bfloat16, jnp.int32
CL, SLOTS, PTS, TGT = 16, 8, 256, 256
BLOCKS = CL * SLOTS
UNROLL = 4
PAD = 8
VMEM_LIMIT = 24 << 20
VMEM = pl.BlockSpec(memory_space=pltpu.VMEM)
SMEM = pl.BlockSpec(memory_space=pltpu.SMEM)
ANY = pl.BlockSpec(memory_space=pl.ANY)


def iota(shape, dim):
    return lax.broadcasted_iota(I32, shape, dim)


def split3(value):
    high = value.astype(BF16).astype(F32)
    rest = value - high
    mid = rest.astype(BF16).astype(F32)
    return high, mid, rest - mid


def centroid_kernel(sp, sm, tp, tm, row_out, own_out):
    s, t = lax.axis_index("src"), lax.axis_index("tgt")
    mass = sm[...]
    total = jnp.sum(mass, axis=1, keepdims=True)
    inv = 1.0 / total
    cols = [jnp.sum(sp[d] * mass, axis=1, keepdims=True) * inv for d in range(3)]
    cols.append(jnp.log2(total))
    lane = iota((CL, 128), 1)
    z = jnp.zeros((CL, 128), F32)
    for q in range(4):
        z = jnp.where(lane == q, cols[q], z)
    zt = jnp.concatenate([z, jnp.zeros((128 - CL, 128), F32)], axis=0).T
    lane = iota((1, 128), 1)
    row = jnp.zeros((1, 128), F32)
    for q in range(4):
        piece = pltpu.roll(zt[q : q + 1, :], lax.rem(128 - 4 * t, 128), 1)
        row = row + pltpu.roll(jnp.where(lane < 4, piece, 0.0), 4 * q, 1)
    weight = tm[...]
    total = jnp.sum(weight, axis=0, keepdims=True)
    inv = 1.0 / total
    rows = [jnp.sum(tp[d] * weight, axis=0, keepdims=True) * inv for d in range(3)]
    rows.append(jnp.log2(total))
    for q in range(4):
        own_out[q : q + 1, :] = rows[q]
        half = jnp.where(s >= 16, rows[q][:, 128:], rows[q][:, :128])
        piece = pltpu.roll(half, lax.rem(128 - 8 * lax.rem(s, 16), 128), 1)
        row = row + pltpu.roll(jnp.where(lane < 8, piece, 0.0), 16 + 8 * q, 1)
    row_out[...] = jnp.broadcast_to(row, row_out.shape)


def row_kernel(listed, live, sp, tp, tm, e_out, m_out, r_out, l_out, order, gt, gf, tab, lhs_a, lhs_b, score_a, score_b, tops_a, tops_b, scol, lrow):
    n = 0
    for c in range(CL):
        for k in range(SLOTS):
            order[n + k] = k * CL + c
        n = n + live[0, c]
    for u in range(PAD):
        order[n + u] = order[0]
    order[BLOCKS + PAD] = n

    for d in range(3):
        a, b, _ = split3(sp[d] * ALPHA)
        for r, piece in enumerate((a, b, a, b)):
            for h in range(2):
                gf[h, pl.ds(4 * d + r, CL, stride=16), :] = piece[:, 128 * h : 128 * h + 128]
    for r in range(12, 16):
        for h in range(2):
            gf[h, pl.ds(r, CL, stride=16), :] = jnp.full((CL, 128), 1.0 if r < 15 else 0.0, F32)
    for c in range(CL):
        gt[c] = jnp.concatenate([gf[h, 16 * c : 16 * c + 16, :] for h in range(2)], axis=1).astype(BF16)
    for d in range(3):
        a, b, _ = split3(tp[d].T)
        tab[2 * d] = a
        tab[2 * d + 1] = b
    base = -(0.5 * ALPHA) * (tp[0] * tp[0] + tp[1] * tp[1] + tp[2] * tp[2]) + jnp.log2(tm[...])
    for r, piece in enumerate(split3(base.T)):
        tab[6 + r] = piece
    sub = iota((16, PTS), 0)
    source = [0, 0, 1, 1, 2, 2, 3, 3, 4, 4, 5, 5, 6, 7, 8]

    def prepare(i, lhs):
        b = order[i]
        at = listed[b // CL, lax.rem(b, CL)]
        pieces = [tab[q, pl.ds(at, 1), :] for q in range(9)]
        stack = jnp.zeros((16, PTS), F32)
        for r, q in enumerate(source):
            stack = jnp.where(sub == r, pieces[q], stack)
        lhs[...] = stack.T.astype(BF16)
        lrow[pl.ds(b, 1), :] = jnp.broadcast_to(at.astype(F32), (1, 128))

    sets = ((lhs_a, score_a, tops_a), (lhs_b, score_b, tops_b))
    for u in range(2):
        prepare(u, sets[u][0])

    def pair(i, _):
        old = [order[jnp.maximum(2 * i - 2 + u, 0)] for u in range(2)]
        v = [jnp.dot(sets[u][0][...], gt[lax.rem(order[2 * i + u], CL)], preferred_element_type=F32) for u in range(2)]
        top_old = [sets[u][2][...] for u in range(2)]
        total = [jnp.zeros((8, PTS), F32) for u in range(2)]
        top = [jnp.full((8, PTS), NEG, F32) for u in range(2)]
        for u in range(2):
            prepare(2 * i + 2 + u, sets[u][0])
        for j in range(0, TGT, 32):
            for u in range(2):
                score = sets[u][1]
                es = []
                for o in range(j, j + 32, 8):
                    e = jnp.exp2(score[o : o + 8, :] - top_old[u])
                    total[u] = total[u] + e
                    es.append(e)
                e_out[old[u], j : j + 32, :] = jnp.concatenate(es, axis=0).astype(BF16)
                score[j : j + 32, :] = v[u][j : j + 32, :]
                for o in range(j, j + 32, 8):
                    top[u] = jnp.maximum(top[u], v[u][o : o + 8, :])
        for u in range(2):
            sets[u][2][...] = jnp.broadcast_to(jnp.max(top[u], axis=0, keepdims=True), (8, PTS))
            scol[pl.ds(old[u], 1), :] = jnp.sum(total[u], axis=0, keepdims=True)
            m_out[pl.ds(old[u], 1), :] = top_old[u][0:1, :]
        return 0

    lax.fori_loop(0, (n + 1) // 2 + 1, pair, 0)
    xn = (-0.5 * ALPHA) * (sp[0] * sp[0] + sp[1] * sp[1] + sp[2] * sp[2])
    lane = iota((1, 128), 1)
    have = jnp.zeros((1, 128), I32)
    for c in range(CL):
        have = jnp.where((lane & (CL - 1)) == c, live[0, c], have)
    ok = jnp.broadcast_to(jnp.where((lane >> 4) < have, 1.0, 0.0), (128, 128)).T[:, 0:1] > 0.5
    m = (m_out[...].reshape(SLOTS, CL, PTS) + xn[None]).reshape(BLOCKS, PTS)
    m_out[...] = m
    r_out[...] = jnp.where(ok, m + jnp.log2(scol[...]), NEG)
    l_out[...] = jnp.where(ok, lrow[...], -1.0)


def coarse_kernel(got, own, m_in, r_in, l_in, g_out, mg_out, l_out, terms):
    turned = got[...].T

    def side(rows):
        norm = rows[0] * rows[0] + rows[1] * rows[1] + rows[2] * rows[2]
        return [rows[0], rows[1], rows[2], rows[3] - (0.5 * ALPHA) * norm]

    tgt = [side([turned[16 + 8 * q + li : 17 + 8 * q + li, :] for q in range(4)]) for li in range(8)]
    mine = side([own[q : q + 1, :] for q in range(4)])
    top_g = jnp.full((16, TGT), NEG, F32)
    for ci in range(4):
        for i in range(0, 128, 16):
            x = [jnp.broadcast_to(got[i : i + 16, 4 * d + ci : 4 * d + ci + 1], (16, 128)) for d in range(3)]
            mass = got[i : i + 16, 12 + ci : 13 + ci]
            ax = [ALPHA * v for v in x]
            scores = [y[3] + ax[0] * y[0] + ax[1] * y[1] + ax[2] * y[2] for y in tgt]
            top = jnp.max(functools.reduce(jnp.maximum, scores), axis=1, keepdims=True)
            total = jnp.sum(sum(jnp.exp2(v - top) for v in scores), axis=1, keepdims=True)
            const = mass - (top + jnp.log2(total))
            halves = []
            for h in (0, 128):
                y = [row[:, h : h + 128] for row in mine]
                halves.append(const + ax[0] * y[0] + ax[1] * y[1] + ax[2] * y[2])
            v = jnp.concatenate(halves, axis=1)
            terms[128 * ci + i : 128 * ci + i + 16, :] = v
            top_g = jnp.maximum(top_g, v)
    top = jnp.max(top_g, axis=0, keepdims=True)
    total = jnp.zeros((16, TGT), F32)
    for i in range(0, 512, 16):
        total = total + jnp.exp2(terms[i : i + 16, :] - top)
    g = (mine[3] - own[3:4, :]) + top + jnp.log2(jnp.sum(total, axis=0, keepdims=True))
    g = -g
    g_out[...] = jnp.broadcast_to(g, g_out.shape)
    at = l_in[...]
    lane = iota((128, 128), 1).astype(F32)
    hit = jnp.where(at == lane, g[:, :128], 0.0) + jnp.where(at == lane + 128.0, g[:, 128:], 0.0)
    picked = jnp.sum(hit, axis=1, keepdims=True)
    mg_out[...] = m_in[...] + picked
    r = (r_in[...] + picked).reshape(SLOTS, CL, PTS)
    top = jnp.max(r, axis=0)
    l_out[...] = top + jnp.log2(jnp.sum(jnp.exp2(r - top[None]), axis=0))


def column_kernel(order, sm, mg, l0, l1, l2, l3, at, e_in, f_out, s_out, sums):
    n = order[BLOCKS + PAD]
    parts = [p[...] for p in (l0, l1, l2, l3)]
    top = functools.reduce(jnp.maximum, parts)
    f = -(top + jnp.log2(sum(jnp.exp2(p - top) for p in parts)))
    f_out[...] = f * UNSCALE
    weights = sm[...][None] * jnp.exp2(mg[...].reshape(SLOTS, CL, PTS) + f[None])
    alive = at[...][:, 0:1] >= 0.0
    w = jnp.where(alive, weights.reshape(BLOCKS, PTS), 0.0).T
    high = w.astype(BF16)
    w = jnp.concatenate([high, (w - high.astype(F32)).astype(BF16)], axis=1)
    sums[...] = jnp.zeros_like(sums)
    lane = iota((TGT, 128), 1)

    def group(g, _):
        for u in range(UNROLL):
            b = order[g * UNROLL + u]
            out = jnp.dot(e_in[b], w, preferred_element_type=F32)
            pltpu.store(sums, out[:, :128] + out[:, 128:], mask=lane == b)
        return 0

    lax.fori_loop(0, (n + UNROLL - 1) // UNROLL, group, 0)
    lane = iota((128, TGT), 1).astype(F32)
    own = jnp.where(lane == jnp.concatenate([at[...], at[...]], axis=1), 1.0, 0.0).astype(BF16)
    total = jnp.zeros((TGT, TGT), F32)
    for piece in split3(sums[...]):
        total = total + jnp.dot(piece.astype(BF16), own, preferred_element_type=F32)
    s_out[...] = total.reshape(32, 8, TGT)


def on_device(src_pts, src_mass, tgt_pts, tgt_mass, listed, live):
    shape = jax.ShapeDtypeStruct
    row, own = pl.pallas_call(
        centroid_kernel,
        out_shape=(shape((128, 128), F32), shape((8, 256), F32)),
        in_specs=[VMEM] * 4,
        out_specs=(VMEM, VMEM),
        name="centroids",
    )(src_pts, src_mass, tgt_pts, tgt_mass)
    got = lax.all_to_all(row, ("src", "tgt"), split_axis=0, concat_axis=0, tiled=True)
    slots = listed.transpose(1, 2, 0).reshape(SLOTS, CL)
    counts = live.transpose(1, 0)
    e, m, r, where, order = pl.pallas_call(
        row_kernel,
        out_shape=(
            pltpu.VMEM((BLOCKS, TGT, PTS), BF16),
            shape((BLOCKS, PTS), F32),
            shape((BLOCKS, PTS), F32),
            shape((128, 128), F32),
            shape((BLOCKS + 2 * PAD,), I32),
        ),
        in_specs=[SMEM, SMEM, VMEM, VMEM, VMEM],
        out_specs=(VMEM, VMEM, VMEM, VMEM, SMEM),
        scratch_shapes=[
            pltpu.VMEM((CL, 16, PTS), BF16),
            pltpu.VMEM((2, CL * 16, 128), F32),
            pltpu.VMEM((9, TGT, PTS), F32),
            pltpu.VMEM((TGT, 16), BF16),
            pltpu.VMEM((TGT, 16), BF16),
            pltpu.VMEM((TGT, PTS), F32),
            pltpu.VMEM((TGT, PTS), F32),
            pltpu.VMEM((8, PTS), F32),
            pltpu.VMEM((8, PTS), F32),
            pltpu.VMEM((BLOCKS, PTS), F32),
            pltpu.VMEM((BLOCKS, 128), F32),
        ],
        cost_estimate=pl.CostEstimate(flops=100_000_000, bytes_accessed=10_000_000, transcendentals=5_000_000),
        compiler_params=pltpu.CompilerParams(vmem_limit_bytes=VMEM_LIMIT),
        name="rows",
    )(slots, counts, src_pts, tgt_pts, tgt_mass)
    g, mg, part = pl.pallas_call(
        coarse_kernel,
        out_shape=(shape((8, 256), F32), shape((BLOCKS, PTS), F32), shape((CL, PTS), F32)),
        in_specs=[VMEM] * 5,
        out_specs=(VMEM, VMEM, VMEM),
        scratch_shapes=[pltpu.VMEM((512, 256), F32)],
        compiler_params=pltpu.CompilerParams(vmem_limit_bytes=VMEM_LIMIT),
        name="coarse",
    )(got, own, m, r, where)
    parts = [part] + [
        lax.ppermute(part, "tgt", [(i, (i + k) % 4) for i in range(4)]) for k in (1, 2, 3)
    ]
    fine_f, sums = pl.pallas_call(
        column_kernel,
        out_shape=(shape((CL, PTS), F32), shape((32, 8, TGT), F32)),
        in_specs=[SMEM] + [VMEM] * 8,
        out_specs=(VMEM, VMEM),
        scratch_shapes=[pltpu.VMEM((TGT, 128), F32)],
        compiler_params=pltpu.CompilerParams(vmem_limit_bytes=VMEM_LIMIT),
        name="columns",
    )(order, src_mass, mg, *parts, where, e)
    arrived = lax.all_to_all(sums, "src", split_axis=0, concat_axis=0, tiled=True)
    mass = lax.dynamic_slice_in_dim(tgt_mass, lax.axis_index("src") * 8, 8, 0)
    fine_g = (g - jnp.log2(1.0 + arrived.sum(axis=0) / mass)) * UNSCALE
    return fine_f, fine_g


def solution(mesh):
    placed = (
        P(None, "src", None),
        P("src", None),
        P(None, None, "tgt"),
        P(None, "tgt"),
        P("src", "tgt", None),
        P("src", "tgt"),
    )
    return jax.shard_map(
        on_device,
        mesh=mesh,
        in_specs=placed,
        out_specs=(P("src", None), P("src", "tgt")),
        check_vma=False,
    )
```

```python
import functools
import math

import jax
import jax.numpy as jnp
from jax import lax
from jax.experimental import pallas as pl
from jax.experimental.pallas import tpu as pltpu
from jax.sharding import PartitionSpec as P

EPS = 0.1
NEG = -1e30
ALPHA = math.log2(math.e) / EPS
UNSCALE = EPS * math.log(2.0)
F32, BF16, I32 = jnp.float32, jnp.bfloat16, jnp.int32
CL, SLOTS, PTS, TGT = 16, 8, 256, 256
BLOCKS = CL * SLOTS
UNROLL = 4
PAD = 8
VMEM = pl.BlockSpec(memory_space=pltpu.VMEM)
SMEM = pl.BlockSpec(memory_space=pltpu.SMEM)
ANY = pl.BlockSpec(memory_space=pl.ANY)


def iota(shape, dim):
    return lax.broadcasted_iota(I32, shape, dim)


def split3(value):
    high = value.astype(BF16).astype(F32)
    rest = value - high
    mid = rest.astype(BF16).astype(F32)
    return high, mid, rest - mid


def centroid_kernel(sp, sm, tp, tm, row_out, own_out):
    s, t = lax.axis_index("src"), lax.axis_index("tgt")
    mass = sm[...]
    total = jnp.sum(mass, axis=1, keepdims=True)
    inv = 1.0 / total
    cols = [jnp.sum(sp[d] * mass, axis=1, keepdims=True) * inv for d in range(3)]
    cols.append(jnp.log2(total))
    lane = iota((CL, 128), 1)
    z = jnp.zeros((CL, 128), F32)
    for q in range(4):
        z = jnp.where(lane == q, cols[q], z)
    zt = jnp.concatenate([z, jnp.zeros((128 - CL, 128), F32)], axis=0).T
    lane = iota((1, 128), 1)
    row = jnp.zeros((1, 128), F32)
    for q in range(4):
        piece = pltpu.roll(zt[q : q + 1, :], lax.rem(128 - 4 * t, 128), 1)
        row = row + pltpu.roll(jnp.where(lane < 4, piece, 0.0), 4 * q, 1)
    weight = tm[...]
    total = jnp.sum(weight, axis=0, keepdims=True)
    inv = 1.0 / total
    rows = [jnp.sum(tp[d] * weight, axis=0, keepdims=True) * inv for d in range(3)]
    rows.append(jnp.log2(total))
    for q in range(4):
        own_out[q : q + 1, :] = rows[q]
        half = jnp.where(s >= 16, rows[q][:, 128:], rows[q][:, :128])
        piece = pltpu.roll(half, lax.rem(128 - 8 * lax.rem(s, 16), 128), 1)
        row = row + pltpu.roll(jnp.where(lane < 8, piece, 0.0), 16 + 8 * q, 1)
    row_out[...] = jnp.broadcast_to(row, row_out.shape)


def row_kernel(listed, live, sp, tp, tm, e_out, m_out, r_out, l_out, order, gt, gf, tab, lhs_a, lhs_b, score_a, score_b, tops_a, tops_b, scol, lrow, spot, ebuf, sems):
    n = 0
    for c in range(CL):
        for k in range(SLOTS):
            order[n + k] = k * CL + c
            spot[n + k] = listed[k, c]
        n = n + live[0, c]
    for u in range(PAD):
        order[n + u] = order[0]
        spot[n + u] = spot[0]
    order[BLOCKS + PAD] = n

    for d in range(3):
        a, b, _ = split3(sp[d] * ALPHA)
        for r, piece in enumerate((a, b, a, b)):
            for h in range(2):
                gf[h, pl.ds(4 * d + r, CL, stride=16), :] = piece[:, 128 * h : 128 * h + 128]
    for r in range(12, 16):
        for h in range(2):
            gf[h, pl.ds(r, CL, stride=16), :] = jnp.full((CL, 128), 1.0 if r < 15 else 0.0, F32)
    for c in range(CL):
        gt[c] = jnp.concatenate([gf[h, 16 * c : 16 * c + 16, :] for h in range(2)], axis=1).astype(BF16)
    for d in range(3):
        a, b, _ = split3(tp[d].T)
        tab[2 * d] = a
        tab[2 * d + 1] = b
    base = -(0.5 * ALPHA) * (tp[0] * tp[0] + tp[1] * tp[1] + tp[2] * tp[2]) + jnp.log2(tm[...])
    for r, piece in enumerate(split3(base.T)):
        tab[6 + r] = piece
    sub = iota((16, PTS), 0)
    source = [0, 0, 1, 1, 2, 2, 3, 3, 4, 4, 5, 5, 6, 7, 8]

    def prepare(i, lhs):
        b = order[i]
        at = spot[i]
        pieces = [tab[q, pl.ds(at, 1), :] for q in range(9)]
        stack = jnp.zeros((16, PTS), F32)
        for r, q in enumerate(source):
            stack = jnp.where(sub == r, pieces[q], stack)
        lhs[...] = stack.T.astype(BF16)
        lrow[pl.ds(b, 1), :] = jnp.broadcast_to(at.astype(F32), (1, 128))

    def flush(b, side, u):
        return pltpu.make_async_copy(ebuf.at[side, u], e_out.at[b], sems.at[side, u])

    sets = ((lhs_a, score_a, tops_a), (lhs_b, score_b, tops_b))
    for u in range(2):
        prepare(u, sets[u][0])

    def pair(i, _):
        side = i & 1

        @pl.when(i >= 3)
        def _():
            for u in range(2):
                flush(0, side, u).wait()

        old = [order[jnp.maximum(2 * i - 2 + u, 0)] for u in range(2)]
        v = [jnp.dot(sets[u][0][...], gt[order[2 * i + u] & (CL - 1)], preferred_element_type=F32) for u in range(2)]
        top_old = [sets[u][2][...] for u in range(2)]
        total = [jnp.zeros((8, PTS), F32) for u in range(2)]
        top = [jnp.full((8, PTS), NEG, F32) for u in range(2)]
        for u in range(2):
            prepare(2 * i + 2 + u, sets[u][0])
        for j in range(0, TGT, 32):
            for u in range(2):
                score = sets[u][1]
                es = []
                for o in range(j, j + 32, 8):
                    e = jnp.exp2(score[o : o + 8, :] - top_old[u])
                    total[u] = total[u] + e
                    es.append(e)
                ebuf[side, u, j : j + 32, :] = jnp.concatenate(es, axis=0).astype(BF16)
                score[j : j + 32, :] = v[u][j : j + 32, :]
                for o in range(j, j + 32, 8):
                    top[u] = jnp.maximum(top[u], v[u][o : o + 8, :])
        for u in range(2):
            sets[u][2][...] = jnp.broadcast_to(jnp.max(top[u], axis=0, keepdims=True), (8, PTS))
            scol[pl.ds(old[u], 1), :] = jnp.sum(total[u], axis=0, keepdims=True)
            m_out[pl.ds(old[u], 1), :] = top_old[u][0:1, :]

        @pl.when(i >= 1)
        def _():
            for u in range(2):
                flush(old[u], side, u).start()

        return 0

    lax.fori_loop(0, (n + 1) // 2 + 1, pair, 0)
    for side in range(2):
        for u in range(2):
            flush(0, side, u).wait()
    xn = (-0.5 * ALPHA) * (sp[0] * sp[0] + sp[1] * sp[1] + sp[2] * sp[2])
    lane = iota((1, 128), 1)
    have = jnp.zeros((1, 128), I32)
    for c in range(CL):
        have = jnp.where((lane & (CL - 1)) == c, live[0, c], have)
    ok = jnp.broadcast_to(jnp.where((lane >> 4) < have, 1.0, 0.0), (128, 128)).T[:, 0:1] > 0.5
    m = (m_out[...].reshape(SLOTS, CL, PTS) + xn[None]).reshape(BLOCKS, PTS)
    m_out[...] = m
    r_out[...] = jnp.where(ok, m + jnp.log2(scol[...]), NEG)
    l_out[...] = jnp.where(ok, lrow[...], -1.0)


def coarse_kernel(got, own, m_in, r_in, l_in, g_out, mg_out, l_out, terms, scores):
    turned = got[...].T

    def side(rows):
        norm = rows[0] * rows[0] + rows[1] * rows[1] + rows[2] * rows[2]
        return [rows[0], rows[1], rows[2], rows[3] - (0.5 * ALPHA) * norm]

    tgt = [side([turned[16 + 8 * q + li : 17 + 8 * q + li, :] for q in range(4)]) for li in range(8)]
    mine = side([own[q : q + 1, :] for q in range(4)])
    step = 32
    top_g = jnp.full((8, TGT), NEG, F32)
    for ci in range(4):
        for i in range(0, 128, step):
            x = [jnp.broadcast_to(ALPHA * got[i : i + step, 4 * d + ci : 4 * d + ci + 1], (step, 128)) for d in range(3)]
            peak = None
            for li, y in enumerate(tgt):
                v = (y[3] + x[0] * y[0]) + (x[1] * y[1] + x[2] * y[2])
                scores[li] = v
                peak = v if peak is None else jnp.maximum(peak, v)
            peak = jnp.max(peak, axis=1, keepdims=True)
            total = jnp.exp2(scores[0] - peak)
            for li in range(1, 8):
                total = total + jnp.exp2(scores[li] - peak)
            total = jnp.sum(total, axis=1, keepdims=True)
            const = got[i : i + step, 12 + ci : 13 + ci] - (peak + jnp.log2(total))
            const = jnp.broadcast_to(const, (step, 128))
            for h in (0, 128):
                y = [row[:, h : h + 128] for row in mine]
                v = (const + x[0] * y[0]) + (x[1] * y[1] + x[2] * y[2])
                terms[128 * ci + i : 128 * ci + i + step, h : h + 128] = v
    for i in range(0, 512, 8):
        top_g = jnp.maximum(top_g, terms[i : i + 8, :])
    top = jnp.max(top_g, axis=0, keepdims=True)
    total = jnp.zeros((8, TGT), F32)
    for i in range(0, 512, 8):
        total = total + jnp.exp2(terms[i : i + 8, :] - top)
    g = (mine[3] - own[3:4, :]) + top + jnp.log2(jnp.sum(total, axis=0, keepdims=True))
    g = -g
    g_out[...] = jnp.broadcast_to(g, g_out.shape)
    at = l_in[...]
    lane = iota((128, 128), 1).astype(F32)
    hit = jnp.where(at == lane, g[:, :128], 0.0) + jnp.where(at == lane + 128.0, g[:, 128:], 0.0)
    picked = jnp.sum(hit, axis=1, keepdims=True)
    mg_out[...] = m_in[...] + picked
    r = (r_in[...] + picked).reshape(SLOTS, CL, PTS)
    top = jnp.max(r, axis=0)
    l_out[...] = top + jnp.log2(jnp.sum(jnp.exp2(r - top[None]), axis=0))


def column_kernel(order, sm, mg, l0, l1, l2, l3, at, e_in, f_out, s_out, sums, ebuf, sems):
    groups = (order[BLOCKS + PAD] + UNROLL - 1) // UNROLL

    def fetch(b, side, u):
        return pltpu.make_async_copy(e_in.at[b], ebuf.at[side, u], sems.at[side, u])

    def start(g, side):
        for u in range(UNROLL):
            fetch(order[g * UNROLL + u], side, u).start()

    start(0, 0)
    parts = [p[...] for p in (l0, l1, l2, l3)]
    top = functools.reduce(jnp.maximum, parts)
    f = -(top + jnp.log2(sum(jnp.exp2(p - top) for p in parts)))
    f_out[...] = f * UNSCALE
    weights = sm[...][None] * jnp.exp2(mg[...].reshape(SLOTS, CL, PTS) + f[None])
    alive = at[...][:, 0:1] >= 0.0
    w = jnp.where(alive, weights.reshape(BLOCKS, PTS), 0.0).T
    w = w.astype(BF16)
    sums[...] = jnp.zeros_like(sums)
    lane = iota((128, 128), 1)

    def group(g, _):
        side = g & 1

        @pl.when(g + 1 < groups)
        def _():
            start(g + 1, 1 - side)

        for u in range(UNROLL):
            fetch(0, side, u).wait()
        for u in range(UNROLL):
            mask = lane == order[g * UNROLL + u]
            for j in range(0, TGT, 128):
                out = jnp.dot(ebuf[side, u, j : j + 128, :], w, preferred_element_type=F32)
                pltpu.store(sums.at[j : j + 128, :], out, mask=mask)
        return 0

    lax.fori_loop(0, groups, group, 0)
    lane = iota((128, TGT), 1).astype(F32)
    own = jnp.where(lane == jnp.concatenate([at[...], at[...]], axis=1), 1.0, 0.0).astype(BF16)
    total = jnp.zeros((TGT, TGT), F32)
    for piece in split3(sums[...]):
        total = total + jnp.dot(piece.astype(BF16), own, preferred_element_type=F32)
    s_out[...] = total.reshape(32, 8, TGT)


def on_device(src_pts, src_mass, tgt_pts, tgt_mass, listed, live):
    shape = jax.ShapeDtypeStruct
    row, own = pl.pallas_call(
        centroid_kernel,
        out_shape=(shape((128, 128), F32), shape((8, 256), F32)),
        in_specs=[VMEM] * 4,
        out_specs=(VMEM, VMEM),
        name="centroids",
    )(src_pts, src_mass, tgt_pts, tgt_mass)
    got = lax.all_to_all(row, ("src", "tgt"), split_axis=0, concat_axis=0, tiled=True)
    slots = listed.transpose(1, 2, 0).reshape(SLOTS, CL)
    counts = live.transpose(1, 0)
    e, m, r, where, order = pl.pallas_call(
        row_kernel,
        out_shape=(
            shape((BLOCKS, TGT, PTS), BF16),
            shape((BLOCKS, PTS), F32),
            shape((BLOCKS, PTS), F32),
            shape((128, 128), F32),
            shape((BLOCKS + 2 * PAD,), I32),
        ),
        in_specs=[SMEM, SMEM, VMEM, VMEM, VMEM],
        out_specs=(ANY, VMEM, VMEM, VMEM, SMEM),
        scratch_shapes=[
            pltpu.VMEM((CL, 16, PTS), BF16),
            pltpu.VMEM((2, CL * 16, 128), F32),
            pltpu.VMEM((9, TGT, PTS), F32),
            pltpu.VMEM((TGT, 16), BF16),
            pltpu.VMEM((TGT, 16), BF16),
            pltpu.VMEM((TGT, PTS), F32),
            pltpu.VMEM((TGT, PTS), F32),
            pltpu.VMEM((8, PTS), F32),
            pltpu.VMEM((8, PTS), F32),
            pltpu.VMEM((BLOCKS, PTS), F32),
            pltpu.VMEM((BLOCKS, 128), F32),
            pltpu.SMEM((BLOCKS + 2 * PAD,), I32),
            pltpu.VMEM((2, 2, TGT, PTS), BF16),
            pltpu.SemaphoreType.DMA((2, 2)),
        ],
        cost_estimate=pl.CostEstimate(flops=100_000_000, bytes_accessed=10_000_000, transcendentals=5_000_000),
        name="rows",
    )(slots, counts, src_pts, tgt_pts, tgt_mass)
    g, mg, part = pl.pallas_call(
        coarse_kernel,
        out_shape=(shape((8, 256), F32), shape((BLOCKS, PTS), F32), shape((CL, PTS), F32)),
        in_specs=[VMEM] * 5,
        out_specs=(VMEM, VMEM, VMEM),
        scratch_shapes=[pltpu.VMEM((512, 256), F32), pltpu.VMEM((8, 32, 128), F32)],
        name="coarse",
    )(got, own, m, r, where)
    parts = [part] + [
        lax.ppermute(part, "tgt", [(i, (i + k) % 4) for i in range(4)]) for k in (1, 2, 3)
    ]
    fine_f, sums = pl.pallas_call(
        column_kernel,
        out_shape=(shape((CL, PTS), F32), shape((32, 8, TGT), F32)),
        in_specs=[SMEM] + [VMEM] * 7 + [ANY],
        out_specs=(VMEM, VMEM),
        scratch_shapes=[
            pltpu.VMEM((TGT, 128), F32),
            pltpu.VMEM((2, UNROLL, TGT, PTS), BF16),
            pltpu.SemaphoreType.DMA((2, UNROLL)),
        ],
        name="columns",
    )(order, src_mass, mg, *parts, where, e)
    arrived = lax.all_to_all(sums, "src", split_axis=0, concat_axis=0, tiled=True)
    mass = lax.dynamic_slice_in_dim(tgt_mass, lax.axis_index("src") * 8, 8, 0)
    fine_g = (g - jnp.log2(1.0 + arrived.sum(axis=0) / mass)) * UNSCALE
    return fine_f, fine_g


def solution(mesh):
    placed = (
        P(None, "src", None),
        P("src", None),
        P(None, None, "tgt"),
        P(None, "tgt"),
        P("src", "tgt", None),
        P("src", "tgt"),
    )
    return jax.shard_map(
        on_device,
        mesh=mesh,
        in_specs=placed,
        out_specs=(P("src", None), P("src", "tgt")),
        check_vma=False,
    )
```

```python
import functools
import math

import jax
import jax.numpy as jnp
from jax import lax
from jax.experimental import pallas as pl
from jax.experimental.pallas import tpu as pltpu
from jax.sharding import PartitionSpec as P

EPS = 0.1
NEG = -1e30
ALPHA = math.log2(math.e) / EPS
UNSCALE = EPS * math.log(2.0)
F32, BF16, I32 = jnp.float32, jnp.bfloat16, jnp.int32
CL, SLOTS, PTS, TGT = 16, 8, 256, 256
BLOCKS = CL * SLOTS
UNROLL = 4
AHEAD = 2
PAD = 8
VMEM = pl.BlockSpec(memory_space=pltpu.VMEM)
SMEM = pl.BlockSpec(memory_space=pltpu.SMEM)
ANY = pl.BlockSpec(memory_space=pl.ANY)


def iota(shape, dim):
    return lax.broadcasted_iota(I32, shape, dim)


def split3(value):
    high = value.astype(BF16).astype(F32)
    rest = value - high
    mid = rest.astype(BF16).astype(F32)
    return high, mid, rest - mid


def centroid_kernel(sp, sm, tp, tm, row_out, own_out):
    s, t = lax.axis_index("src"), lax.axis_index("tgt")
    mass = sm[...]
    total = jnp.sum(mass, axis=1, keepdims=True)
    inv = 1.0 / total
    cols = [jnp.sum(sp[d] * mass, axis=1, keepdims=True) * inv for d in range(3)]
    cols.append(jnp.log2(total))
    lane = iota((CL, 128), 1)
    z = jnp.zeros((CL, 128), F32)
    for q in range(4):
        z = jnp.where(lane == q, cols[q], z)
    zt = jnp.concatenate([z, jnp.zeros((128 - CL, 128), F32)], axis=0).T
    lane = iota((1, 128), 1)
    row = jnp.zeros((1, 128), F32)
    for q in range(4):
        piece = pltpu.roll(zt[q : q + 1, :], lax.rem(128 - 4 * t, 128), 1)
        row = row + pltpu.roll(jnp.where(lane < 4, piece, 0.0), 4 * q, 1)
    weight = tm[...]
    total = jnp.sum(weight, axis=0, keepdims=True)
    inv = 1.0 / total
    rows = [jnp.sum(tp[d] * weight, axis=0, keepdims=True) * inv for d in range(3)]
    rows.append(jnp.log2(total))
    for q in range(4):
        own_out[q : q + 1, :] = rows[q]
        half = jnp.where(s >= 16, rows[q][:, 128:], rows[q][:, :128])
        piece = pltpu.roll(half, lax.rem(128 - 8 * lax.rem(s, 16), 128), 1)
        row = row + pltpu.roll(jnp.where(lane < 8, piece, 0.0), 16 + 8 * q, 1)
    row_out[...] = jnp.broadcast_to(row, row_out.shape)


def dup(table, r, piece):
    for h in range(2):
        table[h, pl.ds(r, CL, stride=16), :] = piece[:, 128 * h : 128 * h + 128]


def own_terms(tp, tm):
    return jnp.log2(tm[...]) - (0.5 * ALPHA) * (tp[0] * tp[0] + tp[1] * tp[1] + tp[2] * tp[2])


def fill_order(order, spot, listed, live):
    n = 0
    for c in range(CL):
        for k in range(SLOTS):
            order[n + k] = k * CL + c
            spot[n + k] = listed[k, c]
        n = n + live[0, c]
    for u in range(PAD):
        order[n + u] = order[0]
        spot[n + u] = spot[0]
    return n


def target_tables(tab, tp, base):
    for d in range(3):
        a, b, _ = split3(tp[d].T)
        tab[2 * d] = a
        tab[2 * d + 1] = b
    for r, piece in enumerate(split3(base)):
        tab[6 + r] = piece


def target_factors(tab, at):
    sub = iota((16, PTS), 0)
    stack = jnp.ones((16, PTS), F32)
    for r, q in enumerate((0, 0, 1, 2, 2, 3, 4, 4, 5, 6, 7, 8)):
        stack = jnp.where(sub == r, tab[q, pl.ds(at, 1), :], stack)
    return stack


def source_factors(table, x, own):
    for d in range(3):
        a, b, _ = split3(x[d])
        for r, piece in enumerate((a, b, a)):
            dup(table, 3 * d + r, piece)
    for r in range(9, 12):
        dup(table, r, jnp.ones((CL, PTS), F32))
    for r, piece in enumerate(own):
        dup(table, 12 + r, piece)


def row_kernel(listed, live, sp, tp, tm, r_out, l_out, order, spot, gt, gf, tab, scol, lrow, *sets):
    sets = [sets[3 * u : 3 * u + 3] for u in range(AHEAD)]
    n = fill_order(order, spot, listed, live)
    order[BLOCKS + PAD] = n
    zero = jnp.zeros((CL, PTS), F32)
    source_factors(gf, [sp[d] * ALPHA for d in range(3)], [zero] * 4)
    for c in range(CL):
        gt[c] = jnp.concatenate([gf[h, 16 * c : 16 * c + 16, :] for h in range(2)], axis=1).astype(BF16)
    target_tables(tab, tp, own_terms(tp, tm).T)

    def prepare(i, lhs):
        lhs[...] = target_factors(tab, spot[i]).T.astype(BF16)
        lrow[pl.ds(order[i], 1), :] = jnp.broadcast_to(spot[i].astype(F32), (1, 128))

    for u in range(AHEAD):
        prepare(u, sets[u][0])

    def batch(i, _):
        at = AHEAD * i
        v = [jnp.dot(sets[u][0][...], gt[order[at + u] & (CL - 1)], preferred_element_type=F32) for u in range(AHEAD)]
        for u in range(AHEAD):
            prepare(at + AHEAD + u, sets[u][0])
        for u in range(AHEAD):
            lhs, score, tops = sets[u]
            top_old = tops[...]
            total = jnp.zeros((8, PTS), F32)
            top = jnp.full((8, PTS), NEG, F32)
            for j in range(0, TGT, 8):
                total = total + jnp.exp2(score[j : j + 8, :] - top_old)
                score[j : j + 8, :] = v[u][j : j + 8, :]
                top = jnp.maximum(top, v[u][j : j + 8, :])
            tops[...] = jnp.broadcast_to(jnp.max(top, axis=0, keepdims=True), (8, PTS))
            old = order[jnp.maximum(at - AHEAD + u, 0)]
            r_out[pl.ds(old, 1), :] = top_old[0:1, :]
            scol[pl.ds(old, 1), :] = jnp.sum(total, axis=0, keepdims=True)
        return 0

    lax.fori_loop(0, (n + AHEAD - 1) // AHEAD + 1, batch, 0)
    xn = (-0.5 * ALPHA) * (sp[0] * sp[0] + sp[1] * sp[1] + sp[2] * sp[2])
    lane = iota((1, 128), 1)
    have = jnp.zeros((1, 128), I32)
    for c in range(CL):
        have = jnp.where((lane & (CL - 1)) == c, live[0, c], have)
    ok = jnp.broadcast_to(jnp.where((lane >> 4) < have, 1.0, 0.0), (128, 128)).T[:, 0:1] > 0.5
    r = r_out[...] + jnp.log2(scol[...])
    r = (r.reshape(SLOTS, CL, PTS) + xn[None]).reshape(BLOCKS, PTS)
    r_out[...] = jnp.where(ok, r, NEG)
    l_out[...] = jnp.where(ok, lrow[...], -1.0)


def coarse_kernel(got, own, r_in, l_in, g_out, l_out, terms, scores):
    turned = got[...].T

    def side(rows):
        norm = rows[0] * rows[0] + rows[1] * rows[1] + rows[2] * rows[2]
        return [rows[0], rows[1], rows[2], rows[3] - (0.5 * ALPHA) * norm]

    tgt = [side([turned[16 + 8 * q + li : 17 + 8 * q + li, :] for q in range(4)]) for li in range(8)]
    mine = side([own[q : q + 1, :] for q in range(4)])
    step = 32
    top_g = jnp.full((8, TGT), NEG, F32)
    for ci in range(4):
        for i in range(0, 128, step):
            x = [jnp.broadcast_to(ALPHA * got[i : i + step, 4 * d + ci : 4 * d + ci + 1], (step, 128)) for d in range(3)]
            peak = None
            for li, y in enumerate(tgt):
                v = (y[3] + x[0] * y[0]) + (x[1] * y[1] + x[2] * y[2])
                scores[li] = v
                peak = v if peak is None else jnp.maximum(peak, v)
            peak = jnp.max(peak, axis=1, keepdims=True)
            total = jnp.exp2(scores[0] - peak)
            for li in range(1, 8):
                total = total + jnp.exp2(scores[li] - peak)
            total = jnp.sum(total, axis=1, keepdims=True)
            const = got[i : i + step, 12 + ci : 13 + ci] - (peak + jnp.log2(total))
            const = jnp.broadcast_to(const, (step, 128))
            for h in (0, 128):
                y = [row[:, h : h + 128] for row in mine]
                v = (const + x[0] * y[0]) + (x[1] * y[1] + x[2] * y[2])
                terms[128 * ci + i : 128 * ci + i + step, h : h + 128] = v
    for i in range(0, 512, 8):
        top_g = jnp.maximum(top_g, terms[i : i + 8, :])
    top = jnp.max(top_g, axis=0, keepdims=True)
    total = jnp.zeros((8, TGT), F32)
    for i in range(0, 512, 8):
        total = total + jnp.exp2(terms[i : i + 8, :] - top)
    g = (mine[3] - own[3:4, :]) + top + jnp.log2(jnp.sum(total, axis=0, keepdims=True))
    g = -g
    g_out[...] = jnp.broadcast_to(g, g_out.shape)
    at = l_in[...]
    lane = iota((128, 128), 1).astype(F32)
    hit = jnp.where(at == lane, g[:, :128], 0.0) + jnp.where(at == lane + 128.0, g[:, 128:], 0.0)
    picked = jnp.sum(hit, axis=1, keepdims=True)
    r = (r_in[...] + picked).reshape(SLOTS, CL, PTS)
    top = jnp.max(r, axis=0)
    l_out[...] = top + jnp.log2(jnp.sum(jnp.exp2(r - top[None]), axis=0))


def column_kernel(listed, live, sp, sm, tp, tm, g, l0, l1, l2, l3, f_out, s_out, order, spot, gt, gf, tab, st):
    n = fill_order(order, spot, listed, live)
    target_tables(tab, tp, (own_terms(tp, tm) + g[0:1, :]).T)
    parts = [p[...] for p in (l0, l1, l2, l3)]
    top = functools.reduce(jnp.maximum, parts)
    f = -(top + jnp.log2(sum(jnp.exp2(p - top) for p in parts)))
    f_out[...] = f * UNSCALE
    own = f + jnp.log2(sm[...]) - (0.5 * ALPHA) * (sp[0] * sp[0] + sp[1] * sp[1] + sp[2] * sp[2])
    zero = jnp.zeros((CL, PTS), F32)
    source_factors(gf, [sp[d] * ALPHA for d in range(3)], (*split3(own), zero))
    for c in range(CL):
        gt[c] = jnp.concatenate([gf[h, 16 * c : 16 * c + 16, :] for h in range(2)], axis=1).T.astype(BF16)
    st[...] = jnp.zeros_like(st)

    def batch(i, _):
        at = i * UNROLL
        v = [
            jnp.dot(gt[order[at + u] & (CL - 1)], target_factors(tab, spot[at + u]).astype(BF16), preferred_element_type=F32)
            for u in range(UNROLL)
        ]
        lines = []
        for u in range(UNROLL):
            total = jnp.zeros((8, TGT), F32)
            for o in range(0, PTS, 8):
                total = total + jnp.exp2(v[u][o : o + 8, :])
            line = jnp.sum(total, axis=0, keepdims=True)
            lines.append(jnp.where(at + u < n, line, 0.0))
        for u in range(UNROLL):
            to = pl.ds(spot[at + u], 1)
            st[to, :] = st[to, :] + lines[u]
        return 0

    lax.fori_loop(0, (n + UNROLL - 1) // UNROLL, batch, 0)
    s_out[...] = st[...].T.reshape(32, 8, TGT)


def on_device(src_pts, src_mass, tgt_pts, tgt_mass, listed, live):
    shape = jax.ShapeDtypeStruct
    row, own = pl.pallas_call(
        centroid_kernel,
        out_shape=(shape((128, 128), F32), shape((8, 256), F32)),
        in_specs=[VMEM] * 4,
        out_specs=(VMEM, VMEM),
        name="centroids",
    )(src_pts, src_mass, tgt_pts, tgt_mass)
    got = lax.all_to_all(row, ("src", "tgt"), split_axis=0, concat_axis=0, tiled=True)
    slots = listed.transpose(1, 2, 0).reshape(SLOTS, CL)
    counts = live.transpose(1, 0)
    r, where = pl.pallas_call(
        row_kernel,
        out_shape=(shape((BLOCKS, PTS), F32), shape((128, 128), F32)),
        in_specs=[SMEM, SMEM, VMEM, VMEM, VMEM],
        out_specs=(VMEM, VMEM),
        scratch_shapes=[
            pltpu.SMEM((BLOCKS + 2 * PAD,), I32),
            pltpu.SMEM((BLOCKS + 2 * PAD,), I32),
            pltpu.VMEM((CL, 16, PTS), BF16),
            pltpu.VMEM((2, CL * 16, 128), F32),
            pltpu.VMEM((9, TGT, PTS), F32),
            pltpu.VMEM((BLOCKS, PTS), F32),
            pltpu.VMEM((BLOCKS, 128), F32),
        ]
        + [pltpu.VMEM((TGT, 16), BF16), pltpu.VMEM((TGT, PTS), F32), pltpu.VMEM((8, PTS), F32)] * AHEAD,
        cost_estimate=pl.CostEstimate(flops=100_000_000, bytes_accessed=10_000_000, transcendentals=5_000_000),
        name="rows",
    )(slots, counts, src_pts, tgt_pts, tgt_mass)
    g, part = pl.pallas_call(
        coarse_kernel,
        out_shape=(shape((8, 256), F32), shape((CL, PTS), F32)),
        in_specs=[VMEM] * 4,
        out_specs=(VMEM, VMEM),
        scratch_shapes=[pltpu.VMEM((512, 256), F32), pltpu.VMEM((8, 32, 128), F32)],
        name="coarse",
    )(got, own, r, where)
    parts = [part] + [
        lax.ppermute(part, "tgt", [(i, (i + k) % 4) for i in range(4)]) for k in (1, 2, 3)
    ]
    fine_f, sums = pl.pallas_call(
        column_kernel,
        out_shape=(shape((CL, PTS), F32), shape((32, 8, TGT), F32)),
        in_specs=[SMEM, SMEM] + [VMEM] * 9,
        out_specs=(VMEM, VMEM),
        scratch_shapes=[
            pltpu.SMEM((BLOCKS + 2 * PAD,), I32),
            pltpu.SMEM((BLOCKS + 2 * PAD,), I32),
            pltpu.VMEM((CL, PTS, 16), BF16),
            pltpu.VMEM((2, CL * 16, 128), F32),
            pltpu.VMEM((9, TGT, PTS), F32),
            pltpu.VMEM((TGT, PTS), F32),
        ],
        name="columns",
    )(slots, counts, src_pts, src_mass, tgt_pts, tgt_mass, g, *parts)
    arrived = lax.all_to_all(sums, "src", split_axis=0, concat_axis=0, tiled=True)
    mass = lax.dynamic_slice_in_dim(tgt_mass, lax.axis_index("src") * 8, 8, 0)
    fine_g = (g - jnp.log2(1.0 + arrived.sum(axis=0) / mass)) * UNSCALE
    return fine_f, fine_g


def solution(mesh):
    placed = (
        P(None, "src", None),
        P("src", None),
        P(None, None, "tgt"),
        P(None, "tgt"),
        P("src", "tgt", None),
        P("src", "tgt"),
    )
    return jax.shard_map(
        on_device,
        mesh=mesh,
        in_specs=placed,
        out_specs=(P("src", None), P("src", "tgt")),
        check_vma=False,
    )
```

```python
import functools
import math

import jax
import jax.numpy as jnp
from jax import lax
from jax.experimental import pallas as pl
from jax.experimental.pallas import tpu as pltpu
from jax.sharding import PartitionSpec as P

EPS = 0.1
NEG = -1e30
ALPHA = math.log2(math.e) / EPS
UNSCALE = EPS * math.log(2.0)
F32, BF16, I32 = jnp.float32, jnp.bfloat16, jnp.int32
CL, SLOTS, PTS, TGT = 16, 8, 256, 256
BLOCKS = CL * SLOTS
UNROLL = 8
AHEAD = 4
PAD = 16
LIST = BLOCKS + 2 * PAD
LIMIT = 16 << 20
VMEM = pl.BlockSpec(memory_space=pltpu.VMEM)
SMEM = pl.BlockSpec(memory_space=pltpu.SMEM)


def iota(shape, dim):
    return lax.broadcasted_iota(I32, shape, dim)


def bf16_part(value):
    big = value * 65537.0
    return big - (big - value)


def split3(value):
    high = bf16_part(value)
    rest = value - high
    mid = bf16_part(rest)
    return high, mid, rest - mid


def centroid_kernel(sp, sm, tp, tm, row_out, own_out, slice_out):
    s, t = lax.axis_index("src"), lax.axis_index("tgt")
    mass = sm[...]
    total = jnp.sum(mass, axis=1, keepdims=True)
    inv = 1.0 / total
    cols = [jnp.sum(sp[d] * mass, axis=1, keepdims=True) * inv for d in range(3)]
    cols.append(jnp.log2(total))
    lane = iota((CL, 128), 1)
    z = jnp.zeros((CL, 128), F32)
    for q in range(4):
        z = jnp.where(lane == q, cols[q], z)
    zt = jnp.concatenate([z, jnp.zeros((128 - CL, 128), F32)], axis=0).T
    lane = iota((1, 128), 1)
    row = jnp.zeros((1, 128), F32)
    for q in range(4):
        piece = pltpu.roll(zt[q : q + 1, :], lax.rem(128 - 4 * t, 128), 1)
        row = row + pltpu.roll(jnp.where(lane < 4, piece, 0.0), 4 * q, 1)
    slice_out[...] = tm[pl.ds(pl.multiple_of(8 * s, 8), 8), :]
    weight = tm[...]
    total = jnp.sum(weight, axis=0, keepdims=True)
    inv = 1.0 / total
    rows = [jnp.sum(tp[d] * weight, axis=0, keepdims=True) * inv for d in range(3)]
    rows.append(jnp.log2(total))
    for q in range(4):
        own_out[q : q + 1, :] = rows[q]
        half = jnp.where(s >= 16, rows[q][:, 128:], rows[q][:, :128])
        piece = pltpu.roll(half, lax.rem(128 - 8 * lax.rem(s, 16), 128), 1)
        row = row + pltpu.roll(jnp.where(lane < 8, piece, 0.0), 16 + 8 * q, 1)
    row_out[...] = jnp.broadcast_to(row, row_out.shape)


def dup(table, r, piece):
    for h in range(2):
        table[h, pl.ds(r, CL, stride=16), :] = piece[:, 128 * h : 128 * h + 128]


def own_terms(tp, tm):
    return jnp.log2(tm[...]) - (0.5 * ALPHA) * (tp[0] * tp[0] + tp[1] * tp[1] + tp[2] * tp[2])


def fill_order(order, listed, live):
    n = 0
    for c in range(CL):
        for k in range(SLOTS):
            order[n + k] = (k * CL + c) * TGT + listed[k, c]
        n = n + live[0, c]
    for u in range(PAD):
        order[n + u] = order[0]
    order[LIST - 1] = n
    return n


def target_tables(tab, tp, base):
    for d in range(3):
        a, b, _ = split3(tp[d].T)
        tab[2 * d] = a
        tab[2 * d + 1] = b
    for r, piece in enumerate(split3(base)):
        tab[6 + r] = piece


def target_factors(tab, at):
    sub = iota((16, PTS), 0)
    stack = jnp.ones((16, PTS), F32)
    for r, q in enumerate((0, 0, 1, 2, 2, 3, 4, 4, 5, 6, 7, 8)):
        stack = jnp.where(sub == r, tab[q, pl.ds(at, 1), :], stack)
    return stack


def source_factors(table, x, own):
    for d in range(3):
        a, b, _ = split3(x[d])
        for r, piece in enumerate((a, b, a)):
            dup(table, 3 * d + r, piece)
    for r in range(9, 12):
        dup(table, r, jnp.ones((CL, PTS), F32))
    for r, piece in enumerate(own):
        dup(table, 12 + r, piece)


def row_kernel(listed, live, sp, tp, tm, r_out, l_out, order, gt, gf, tab, scol, lrow, *sets):
    sets = [sets[3 * u : 3 * u + 3] for u in range(AHEAD)]
    n = fill_order(order, listed, live)
    zero = jnp.zeros((CL, PTS), F32)
    source_factors(gf, [sp[d] * ALPHA for d in range(3)], [zero] * 4)
    for c in range(CL):
        gt[c] = jnp.concatenate([gf[h, 16 * c : 16 * c + 16, :] for h in range(2)], axis=1).astype(BF16)
    target_tables(tab, tp, own_terms(tp, tm).T)

    def prepare(i, lhs):
        at = order[i] & (TGT - 1)
        lhs[...] = target_factors(tab, at).astype(BF16).T
        lrow[pl.ds(order[i] >> 8, 1), :] = jnp.broadcast_to(at.astype(F32), (1, 128))

    for u in range(AHEAD):
        prepare(u, sets[u][0])

    def batch(i, _):
        at = AHEAD * i
        v = [jnp.dot(sets[u][0][...], gt[(order[at + u] >> 8) & (CL - 1)], preferred_element_type=F32) for u in range(AHEAD)]
        for u in range(AHEAD):
            prepare(at + AHEAD + u, sets[u][0])
        for u in range(AHEAD):
            lhs, score, tops = sets[u]
            top_old = tops[...]
            total = jnp.zeros((8, PTS), F32)
            top = jnp.full((8, PTS), NEG, F32)
            for j in range(0, TGT, 8):
                total = total + jnp.exp2(score[j : j + 8, :] - top_old)
                score[j : j + 8, :] = v[u][j : j + 8, :]
                top = jnp.maximum(top, v[u][j : j + 8, :])
            tops[...] = jnp.broadcast_to(jnp.max(top, axis=0, keepdims=True), (8, PTS))
            old = order[jnp.maximum(at - AHEAD + u, 0)] >> 8
            r_out[pl.ds(old, 1), :] = top_old[0:1, :]
            scol[pl.ds(old, 1), :] = jnp.sum(total, axis=0, keepdims=True)
        return 0

    lax.fori_loop(0, (n + AHEAD - 1) // AHEAD + 1, batch, 0)
    xn = (-0.5 * ALPHA) * (sp[0] * sp[0] + sp[1] * sp[1] + sp[2] * sp[2])
    lane = iota((1, 128), 1)
    have = jnp.zeros((1, 128), I32)
    for c in range(CL):
        have = jnp.where((lane & (CL - 1)) == c, live[0, c], have)
    ok = jnp.broadcast_to(jnp.where((lane >> 4) < have, 1.0, 0.0), (128, 128)).T[:, 0:1] > 0.5
    r = r_out[...] + jnp.log2(scol[...])
    r = (r.reshape(SLOTS, CL, PTS) + xn[None]).reshape(BLOCKS, PTS)
    r_out[...] = jnp.where(ok, r, NEG)
    l_out[...] = jnp.where(ok, lrow[...], -1.0)


def coarse_kernel(got, own, r_in, l_in, g_out, l_out, terms, scores):
    turned = got[...].T

    def side(rows):
        norm = rows[0] * rows[0] + rows[1] * rows[1] + rows[2] * rows[2]
        return [rows[0], rows[1], rows[2], rows[3] - (0.5 * ALPHA) * norm]

    tgt = [side([turned[16 + 8 * q + li : 17 + 8 * q + li, :] for q in range(4)]) for li in range(8)]
    mine = side([own[q : q + 1, :] for q in range(4)])
    step = 32
    top_g = jnp.full((8, TGT), NEG, F32)
    for ci in range(4):
        for i in range(0, 128, step):
            x = [jnp.broadcast_to(ALPHA * got[i : i + step, 4 * d + ci : 4 * d + ci + 1], (step, 128)) for d in range(3)]
            peak = None
            for li, y in enumerate(tgt):
                v = (y[3] + x[0] * y[0]) + (x[1] * y[1] + x[2] * y[2])
                scores[li] = v
                peak = v if peak is None else jnp.maximum(peak, v)
            peak = jnp.max(peak, axis=1, keepdims=True)
            total = jnp.exp2(scores[0] - peak)
            for li in range(1, 8):
                total = total + jnp.exp2(scores[li] - peak)
            total = jnp.sum(total, axis=1, keepdims=True)
            const = got[i : i + step, 12 + ci : 13 + ci] - (peak + jnp.log2(total))
            const = jnp.broadcast_to(const, (step, 128))
            for h in (0, 128):
                y = [row[:, h : h + 128] for row in mine]
                v = (const + x[0] * y[0]) + (x[1] * y[1] + x[2] * y[2])
                terms[128 * ci + i : 128 * ci + i + step, h : h + 128] = v
    for i in range(0, 512, 8):
        top_g = jnp.maximum(top_g, terms[i : i + 8, :])
    top = jnp.max(top_g, axis=0, keepdims=True)
    total = jnp.zeros((8, TGT), F32)
    for i in range(0, 512, 8):
        total = total + jnp.exp2(terms[i : i + 8, :] - top)
    g = (mine[3] - own[3:4, :]) + top + jnp.log2(jnp.sum(total, axis=0, keepdims=True))
    g = -g
    g_out[...] = jnp.broadcast_to(g, g_out.shape)
    at = l_in[...]
    lane = iota((128, 128), 1).astype(F32)
    hit = jnp.where(at == lane, g[:, :128], 0.0) + jnp.where(at == lane + 128.0, g[:, 128:], 0.0)
    picked = jnp.sum(hit, axis=1, keepdims=True)
    r = (r_in[...] + picked).reshape(SLOTS, CL, PTS)
    top = jnp.max(r, axis=0)
    l_out[...] = top + jnp.log2(jnp.sum(jnp.exp2(r - top[None]), axis=0))


def column_kernel(order, sp, sm, tp, tm, g, l0, l1, l2, l3, f_out, s_out, gt, gf, tab, st):
    parts = [p[...] for p in (l0, l1, l2, l3)]
    top = functools.reduce(jnp.maximum, parts)
    f = -(top + jnp.log2(sum(jnp.exp2(p - top) for p in parts)))
    f_out[...] = f * UNSCALE
    st[...] = jnp.zeros_like(st)
    own = f + jnp.log2(sm[...]) - (0.5 * ALPHA) * (sp[0] * sp[0] + sp[1] * sp[1] + sp[2] * sp[2])
    zero = jnp.zeros((CL, PTS), F32)
    source_factors(gf, [sp[d] * ALPHA for d in range(3)], (*split3(own), zero))
    for c in range(CL):
        gt[c] = jnp.concatenate([gf[h, 16 * c : 16 * c + 16, :] for h in range(2)], axis=1).astype(BF16).T
    target_tables(tab, tp, (own_terms(tp, tm) + g[0:1, :]).T)
    n = order[LIST - 1]

    def batch(i, _):
        at = i * UNROLL
        v = []
        for u in range(UNROLL):
            left = gt[(order[at + u] >> 8) & (CL - 1)]
            right = target_factors(tab, order[at + u] & (TGT - 1)).astype(BF16)
            v.append(jnp.dot(left, right, preferred_element_type=F32))
        lines = []
        for u in range(UNROLL):
            total = jnp.zeros((8, TGT), F32)
            for o in range(0, PTS, 8):
                total = total + jnp.exp2(v[u][o : o + 8, :])
            line = jnp.sum(total, axis=0, keepdims=True)
            lines.append(jnp.where(at + u < n, line, 0.0))
        for u in range(UNROLL):
            to = pl.ds(order[at + u] & (TGT - 1), 1)
            st[to, :] = st[to, :] + lines[u]
        return 0

    lax.fori_loop(0, (n + UNROLL - 1) // UNROLL, batch, 0)
    s_out[...] = st[...].T.reshape(32, 8, TGT)


def final_kernel(arrived, mass, g, out):
    total = jnp.sum(arrived[...], axis=0)
    out[...] = (g[...] - jnp.log2(1.0 + total / mass[...])) * UNSCALE


def on_device(src_pts, src_mass, tgt_pts, tgt_mass, listed, live):
    shape = jax.ShapeDtypeStruct
    params = pltpu.CompilerParams(vmem_limit_bytes=LIMIT)
    row, own, mass = pl.pallas_call(
        centroid_kernel,
        out_shape=(shape((128, 128), F32), shape((8, 256), F32), shape((8, 256), F32)),
        in_specs=[VMEM] * 4,
        out_specs=(VMEM, VMEM, VMEM),
        name="centroids",
    )(src_pts, src_mass, tgt_pts, tgt_mass)
    got = lax.all_to_all(row, ("src", "tgt"), split_axis=0, concat_axis=0, tiled=True)
    slots = listed.transpose(1, 2, 0).reshape(SLOTS, CL)
    counts = live.transpose(1, 0)
    r, where, order = pl.pallas_call(
        row_kernel,
        out_shape=(shape((BLOCKS, PTS), F32), shape((128, 128), F32), shape((LIST,), I32)),
        in_specs=[SMEM, SMEM, VMEM, VMEM, VMEM],
        out_specs=(VMEM, VMEM, SMEM),
        scratch_shapes=[
            pltpu.VMEM((CL, 16, PTS), BF16),
            pltpu.VMEM((2, CL * 16, 128), F32),
            pltpu.VMEM((9, TGT, PTS), F32),
            pltpu.VMEM((BLOCKS, PTS), F32),
            pltpu.VMEM((BLOCKS, 128), F32),
        ]
        + [pltpu.VMEM((TGT, 16), BF16), pltpu.VMEM((TGT, PTS), F32), pltpu.VMEM((8, PTS), F32)] * AHEAD,
        cost_estimate=pl.CostEstimate(flops=100_000_000, bytes_accessed=10_000_000, transcendentals=5_000_000),
        compiler_params=params,
        name="rows",
    )(slots, counts, src_pts, tgt_pts, tgt_mass)
    g, part = pl.pallas_call(
        coarse_kernel,
        out_shape=(shape((8, 256), F32), shape((CL, PTS), F32)),
        in_specs=[VMEM] * 4,
        out_specs=(VMEM, VMEM),
        scratch_shapes=[pltpu.VMEM((512, 256), F32), pltpu.VMEM((8, 32, 128), F32)],
        compiler_params=params,
        name="coarse",
    )(got, own, r, where)
    parts = [part] + [
        lax.ppermute(part, "tgt", [(i, (i + k) % 4) for i in range(4)]) for k in (1, 2, 3)
    ]
    fine_f, sums = pl.pallas_call(
        column_kernel,
        out_shape=(shape((CL, PTS), F32), shape((32, 8, TGT), F32)),
        in_specs=[SMEM] + [VMEM] * 9,
        out_specs=(VMEM, VMEM),
        scratch_shapes=[
            pltpu.VMEM((CL, PTS, 16), BF16),
            pltpu.VMEM((2, CL * 16, 128), F32),
            pltpu.VMEM((9, TGT, PTS), F32),
            pltpu.VMEM((TGT, PTS), F32),
        ],
        compiler_params=params,
        name="columns",
    )(order, src_pts, src_mass, tgt_pts, tgt_mass, g, *parts)
    arrived = lax.all_to_all(sums, "src", split_axis=0, concat_axis=0, tiled=True)
    fine_g = pl.pallas_call(
        final_kernel,
        out_shape=shape((8, TGT), F32),
        in_specs=[VMEM] * 3,
        out_specs=VMEM,
        compiler_params=params,
        name="final",
    )(arrived, mass, g)
    return fine_f, fine_g


def solution(mesh):
    placed = (
        P(None, "src", None),
        P("src", None),
        P(None, None, "tgt"),
        P(None, "tgt"),
        P("src", "tgt", None),
        P("src", "tgt"),
    )
    return jax.shard_map(
        on_device,
        mesh=mesh,
        in_specs=placed,
        out_specs=(P("src", None), P("src", "tgt")),
        check_vma=False,
    )
```

```python
import functools
import math

import jax
import jax.numpy as jnp
from jax import lax
from jax.experimental import pallas as pl
from jax.experimental.pallas import tpu as pltpu
from jax.sharding import PartitionSpec as P

EPS = 0.1
NEG = -1e30
ALPHA = math.log2(math.e) / EPS
UNSCALE = EPS * math.log(2.0)
F32, BF16, I32 = jnp.float32, jnp.bfloat16, jnp.int32
CL, SLOTS, PTS, TGT = 16, 8, 256, 256
BLOCKS = CL * SLOTS
UNROLL = 8
AHEAD = 4
PAD = 16
LIST = BLOCKS + 2 * PAD
LIMIT = 16 << 20
VMEM = pl.BlockSpec(memory_space=pltpu.VMEM)
SMEM = pl.BlockSpec(memory_space=pltpu.SMEM)
ANY = pl.BlockSpec(memory_space=pl.ANY)


def iota(shape, dim):
    return lax.broadcasted_iota(I32, shape, dim)


def bf16_part(value):
    big = value * 65537.0
    return big - (big - value)


def split3(value):
    high = bf16_part(value)
    rest = value - high
    mid = bf16_part(rest)
    return high, mid, rest - mid


def fill_order(order, listed, live):
    n = 0
    for c in range(CL):
        for k in range(SLOTS):
            order[n + k] = (k * CL + c) * TGT + listed[k, c]
        n = n + live[0, c]
    for u in range(PAD):
        order[n + u] = order[0]
    order[LIST - 1] = n


def centroid_kernel(listed, live, sp, sm, tp, tm, row_out, own_out, slice_out, order):
    s, t = lax.axis_index("src"), lax.axis_index("tgt")
    fill_order(order, listed, live)
    mass = sm[...]
    total = jnp.sum(mass, axis=1, keepdims=True)
    inv = 1.0 / total
    cols = [jnp.sum(sp[d] * mass, axis=1, keepdims=True) * inv for d in range(3)]
    cols.append(jnp.log2(total))
    lane = iota((CL, 128), 1)
    z = jnp.zeros((CL, 128), F32)
    for q in range(4):
        z = jnp.where(lane == q, cols[q], z)
    zt = jnp.concatenate([z, jnp.zeros((128 - CL, 128), F32)], axis=0).T
    lane = iota((1, 128), 1)
    row = jnp.zeros((1, 128), F32)
    for q in range(4):
        piece = pltpu.roll(zt[q : q + 1, :], lax.rem(128 - 4 * t, 128), 1)
        row = row + pltpu.roll(jnp.where(lane < 4, piece, 0.0), 4 * q, 1)
    slice_out[...] = tm[pl.ds(pl.multiple_of(8 * s, 8), 8), :]
    weight = tm[...]
    total = jnp.sum(weight, axis=0, keepdims=True)
    inv = 1.0 / total
    rows = [jnp.sum(tp[d] * weight, axis=0, keepdims=True) * inv for d in range(3)]
    rows.append(jnp.log2(total))
    for q in range(4):
        own_out[q : q + 1, :] = rows[q]
        half = jnp.where(s >= 16, rows[q][:, 128:], rows[q][:, :128])
        piece = pltpu.roll(half, lax.rem(128 - 8 * lax.rem(s, 16), 128), 1)
        row = row + pltpu.roll(jnp.where(lane < 8, piece, 0.0), 16 + 8 * q, 1)
    row_out[...] = jnp.broadcast_to(row, row_out.shape)


def dup(table, r, piece):
    for h in range(2):
        table[h, pl.ds(r, CL, stride=16), :] = piece[:, 128 * h : 128 * h + 128]


def own_terms(tp, tm):
    return jnp.log2(tm[...]) - (0.5 * ALPHA) * (tp[0] * tp[0] + tp[1] * tp[1] + tp[2] * tp[2])


def fill_tables(tab, tp, tm):
    for d in range(3):
        y = tp[d].T
        high = bf16_part(y)
        tab[2 * d] = high
        tab[2 * d + 1] = bf16_part(y - high)
    tab[6] = own_terms(tp, tm).T


def target_factors(tab, at, extra):
    sub = iota((16, PTS), 0)
    stack = jnp.ones((16, PTS), F32)
    rows = [tab[q, pl.ds(at, 1), :] for q in (0, 0, 1, 2, 2, 3, 4, 4, 5)]
    own = tab[6, pl.ds(at, 1), :]
    for r, row in enumerate((*rows, *split3(own if extra is None else own + extra))):
        stack = jnp.where(sub == r, row, stack)
    return stack.astype(BF16)


def source_factors(table, x, own):
    for d in range(3):
        a, b, _ = split3(x[d])
        for r, piece in enumerate((a, b, a)):
            dup(table, 3 * d + r, piece)
    for r in range(9, 12):
        dup(table, r, jnp.ones((CL, PTS), F32))
    for r, piece in enumerate(own):
        dup(table, 12 + r, piece)


def row_kernel(order, sp, tp, tm, r_out, l_out, tab, gt, gf, scol, lrow, *sets):
    sets = [sets[3 * u : 3 * u + 3] for u in range(AHEAD)]
    n = order[LIST - 1]
    zero = jnp.zeros((CL, PTS), F32)
    source_factors(gf, [sp[d] * ALPHA for d in range(3)], [zero] * 4)
    for c in range(CL):
        gt[c] = jnp.concatenate([gf[h, 16 * c : 16 * c + 16, :] for h in range(2)], axis=1).astype(BF16)
    fill_tables(tab, tp, tm)
    lrow[...] = jnp.full((BLOCKS, 128), -1.0, F32)

    def prepare(i, lhs):
        at = order[i] & (TGT - 1)
        lhs[...] = target_factors(tab, at, None).T
        lrow[pl.ds(order[i] >> 8, 1), :] = jnp.broadcast_to(at.astype(F32), (1, 128))

    for u in range(AHEAD):
        prepare(u, sets[u][0])

    def batch(i, _):
        at = AHEAD * i
        v = [jnp.dot(sets[u][0][...], gt[(order[at + u] >> 8) & (CL - 1)], preferred_element_type=F32) for u in range(AHEAD)]
        for u in range(AHEAD):
            prepare(at + AHEAD + u, sets[u][0])
        for u in range(AHEAD):
            lhs, score, tops = sets[u]
            top_old = tops[...]
            total = jnp.zeros((8, PTS), F32)
            top = jnp.full((8, PTS), NEG, F32)
            for j in range(0, TGT, 8):
                total = total + jnp.exp2(score[j : j + 8, :] - top_old)
                score[j : j + 8, :] = v[u][j : j + 8, :]
                top = jnp.maximum(top, v[u][j : j + 8, :])
            tops[...] = jnp.broadcast_to(jnp.max(top, axis=0, keepdims=True), (8, PTS))
            old = order[jnp.maximum(at - AHEAD + u, 0)] >> 8
            r_out[pl.ds(old, 1), :] = top_old[0:1, :]
            scol[pl.ds(old, 1), :] = jnp.sum(total, axis=0, keepdims=True)
        return 0

    lax.fori_loop(0, (n + AHEAD - 1) // AHEAD + 1, batch, 0)
    xn = (-0.5 * ALPHA) * (sp[0] * sp[0] + sp[1] * sp[1] + sp[2] * sp[2])
    r = r_out[...] + jnp.log2(scol[...])
    r = (r.reshape(SLOTS, CL, PTS) + xn[None]).reshape(BLOCKS, PTS)
    r_out[...] = jnp.where(lrow[:, 0:1] >= 0.0, r, NEG)
    l_out[...] = lrow[...]


def coarse_kernel(got, own, r_in, l_in, g_out, l_out, terms, scores):
    turned = got[...].T

    def side(rows):
        norm = rows[0] * rows[0] + rows[1] * rows[1] + rows[2] * rows[2]
        return [rows[0], rows[1], rows[2], rows[3] - (0.5 * ALPHA) * norm]

    tgt = [side([turned[16 + 8 * q + li : 17 + 8 * q + li, :] for q in range(4)]) for li in range(8)]
    mine = side([own[q : q + 1, :] for q in range(4)])
    step = 32
    top_g = jnp.full((8, TGT), NEG, F32)
    for ci in range(4):
        for i in range(0, 128, step):
            x = [jnp.broadcast_to(ALPHA * got[i : i + step, 4 * d + ci : 4 * d + ci + 1], (step, 128)) for d in range(3)]
            peak = None
            for li, y in enumerate(tgt):
                v = (y[3] + x[0] * y[0]) + (x[1] * y[1] + x[2] * y[2])
                scores[li] = v
                peak = v if peak is None else jnp.maximum(peak, v)
            peak = jnp.max(peak, axis=1, keepdims=True)
            total = jnp.exp2(scores[0] - peak)
            for li in range(1, 8):
                total = total + jnp.exp2(scores[li] - peak)
            total = jnp.sum(total, axis=1, keepdims=True)
            const = got[i : i + step, 12 + ci : 13 + ci] - (peak + jnp.log2(total))
            const = jnp.broadcast_to(const, (step, 128))
            for h in (0, 128):
                y = [row[:, h : h + 128] for row in mine]
                v = (const + x[0] * y[0]) + (x[1] * y[1] + x[2] * y[2])
                terms[128 * ci + i : 128 * ci + i + step, h : h + 128] = v
    for i in range(0, 512, 8):
        top_g = jnp.maximum(top_g, terms[i : i + 8, :])
    top = jnp.max(top_g, axis=0, keepdims=True)
    total = jnp.zeros((8, TGT), F32)
    for i in range(0, 512, 8):
        total = total + jnp.exp2(terms[i : i + 8, :] - top)
    g = (mine[3] - own[3:4, :]) + top + jnp.log2(jnp.sum(total, axis=0, keepdims=True))
    g = -g
    g_out[...] = jnp.broadcast_to(g, g_out.shape)
    at = l_in[...]
    lane = iota((128, 128), 1).astype(F32)
    hit = jnp.where(at == lane, g[:, :128], 0.0) + jnp.where(at == lane + 128.0, g[:, 128:], 0.0)
    picked = jnp.sum(hit, axis=1, keepdims=True)
    r = (r_in[...] + picked).reshape(SLOTS, CL, PTS)
    top = jnp.max(r, axis=0)
    l_out[...] = top + jnp.log2(jnp.sum(jnp.exp2(r - top[None]), axis=0))


def column_kernel(order, g, sp, sm, tp, tm, l0, l1, l2, l3, f_out, s_out, tab, gt, gf, st, fbuf, sem):
    parts = [p[...] for p in (l0, l1, l2, l3)]
    top = functools.reduce(jnp.maximum, parts)
    f = -(top + jnp.log2(sum(jnp.exp2(p - top) for p in parts)))
    fbuf[...] = f * UNSCALE
    send = pltpu.make_async_copy(fbuf, f_out, sem)
    send.start()
    st[...] = jnp.zeros_like(st)
    fill_tables(tab, tp, tm)
    own = f + jnp.log2(sm[...]) - (0.5 * ALPHA) * (sp[0] * sp[0] + sp[1] * sp[1] + sp[2] * sp[2])
    zero = jnp.zeros((CL, PTS), F32)
    source_factors(gf, [sp[d] * ALPHA for d in range(3)], (*split3(own), zero))
    for c in range(CL):
        gt[c] = jnp.concatenate([gf[h, 16 * c : 16 * c + 16, :] for h in range(2)], axis=1).astype(BF16).T
    n = order[LIST - 1]

    def batch(i, _):
        at = i * UNROLL
        v = []
        for u in range(UNROLL):
            left = gt[(order[at + u] >> 8) & (CL - 1)]
            to = order[at + u] & (TGT - 1)
            right = target_factors(tab, to, g[0, to])
            v.append(jnp.dot(left, right, preferred_element_type=F32))
        lines = []
        for u in range(UNROLL):
            total = jnp.zeros((8, TGT), F32)
            for o in range(0, PTS, 8):
                total = total + jnp.exp2(v[u][o : o + 8, :])
            line = jnp.sum(total, axis=0, keepdims=True)
            lines.append(jnp.where(at + u < n, line, 0.0))
        for u in range(UNROLL):
            to = pl.ds(order[at + u] & (TGT - 1), 1)
            st[to, :] = st[to, :] + lines[u]
        return 0

    lax.fori_loop(0, (n + UNROLL - 1) // UNROLL, batch, 0)
    s_out[...] = st[...].T.reshape(32, 8, TGT)
    send.wait()


def final_kernel(arrived, mass, g, out):
    total = jnp.sum(arrived[...], axis=0)
    out[...] = (g[...] - jnp.log2(1.0 + total / mass[...])) * UNSCALE


def on_device(src_pts, src_mass, tgt_pts, tgt_mass, listed, live):
    shape = jax.ShapeDtypeStruct
    params = pltpu.CompilerParams(vmem_limit_bytes=LIMIT)
    slots = listed.transpose(1, 2, 0).reshape(SLOTS, CL)
    counts = live.transpose(1, 0)
    row, own, mass, order = pl.pallas_call(
        centroid_kernel,
        out_shape=(shape((128, 128), F32), shape((8, 256), F32), shape((8, 256), F32), shape((LIST,), I32)),
        in_specs=[SMEM, SMEM] + [VMEM] * 4,
        out_specs=(VMEM, VMEM, VMEM, SMEM),
        name="centroids",
    )(slots, counts, src_pts, src_mass, tgt_pts, tgt_mass)
    got = lax.all_to_all(row, ("src", "tgt"), split_axis=0, concat_axis=0, tiled=True)
    r, where = pl.pallas_call(
        row_kernel,
        out_shape=(shape((BLOCKS, PTS), F32), shape((128, 128), F32)),
        in_specs=[SMEM, VMEM, VMEM, VMEM],
        out_specs=(VMEM, VMEM),
        scratch_shapes=[
            pltpu.VMEM((7, TGT, PTS), F32),
            pltpu.VMEM((CL, 16, PTS), BF16),
            pltpu.VMEM((2, CL * 16, 128), F32),
            pltpu.VMEM((BLOCKS, PTS), F32),
            pltpu.VMEM((BLOCKS, 128), F32),
        ]
        + [pltpu.VMEM((TGT, 16), BF16), pltpu.VMEM((TGT, PTS), F32), pltpu.VMEM((8, PTS), F32)] * AHEAD,
        cost_estimate=pl.CostEstimate(flops=100_000_000, bytes_accessed=10_000_000, transcendentals=5_000_000),
        compiler_params=params,
        name="rows",
    )(order, src_pts, tgt_pts, tgt_mass)
    g, part = pl.pallas_call(
        coarse_kernel,
        out_shape=(shape((8, 256), F32), shape((CL, PTS), F32)),
        in_specs=[VMEM] * 4,
        out_specs=(VMEM, VMEM),
        scratch_shapes=[pltpu.VMEM((512, 256), F32), pltpu.VMEM((8, 32, 128), F32)],
        compiler_params=params,
        name="coarse",
    )(got, own, r, where)
    parts = [part] + [
        lax.ppermute(part, "tgt", [(i, (i + k) % 4) for i in range(4)]) for k in (1, 2, 3)
    ]
    fine_f, sums = pl.pallas_call(
        column_kernel,
        out_shape=(shape((CL, PTS), F32), shape((32, 8, TGT), F32)),
        in_specs=[SMEM, SMEM] + [VMEM] * 8,
        out_specs=(ANY, VMEM),
        scratch_shapes=[
            pltpu.VMEM((7, TGT, PTS), F32),
            pltpu.VMEM((CL, PTS, 16), BF16),
            pltpu.VMEM((2, CL * 16, 128), F32),
            pltpu.VMEM((TGT, PTS), F32),
            pltpu.VMEM((CL, PTS), F32),
            pltpu.SemaphoreType.DMA,
        ],
        compiler_params=params,
        name="columns",
    )(order, g, src_pts, src_mass, tgt_pts, tgt_mass, *parts)
    arrived = lax.all_to_all(sums, "src", split_axis=0, concat_axis=0, tiled=True)
    fine_g = pl.pallas_call(
        final_kernel,
        out_shape=shape((8, TGT), F32),
        in_specs=[VMEM] * 3,
        out_specs=VMEM,
        compiler_params=params,
        name="final",
    )(arrived, mass, g)
    return fine_f, fine_g


def solution(mesh):
    placed = (
        P(None, "src", None),
        P("src", None),
        P(None, None, "tgt"),
        P(None, "tgt"),
        P("src", "tgt", None),
        P("src", "tgt"),
    )
    return jax.shard_map(
        on_device,
        mesh=mesh,
        in_specs=placed,
        out_specs=(P("src", None), P("src", "tgt")),
        check_vma=False,
    )
```

```python
import functools
import math

import jax
import jax.numpy as jnp
from jax import lax
from jax.experimental import pallas as pl
from jax.experimental.pallas import tpu as pltpu
from jax.sharding import PartitionSpec as P

EPS = 0.1
NEG = -1e30
ALPHA = math.log2(math.e) / EPS
UNSCALE = EPS * math.log(2.0)
F32, BF16, I32 = jnp.float32, jnp.bfloat16, jnp.int32
CL, SLOTS, PTS, TGT = 16, 8, 256, 256
BLOCKS = CL * SLOTS
UNROLL = 8
AHEAD = 4
PAD = 16
LIST = BLOCKS + 2 * PAD
LIMIT = 16 << 20
VMEM = pl.BlockSpec(memory_space=pltpu.VMEM)
SMEM = pl.BlockSpec(memory_space=pltpu.SMEM)
ANY = pl.BlockSpec(memory_space=pl.ANY)


def iota(shape, dim):
    return lax.broadcasted_iota(I32, shape, dim)


def bf16_part(value):
    big = value * 65537.0
    return big - (big - value)


def split3(value):
    high = bf16_part(value)
    rest = value - high
    mid = bf16_part(rest)
    return high, mid, rest - mid


def fill_order(order, listed, live):
    n = 0
    for c in range(CL):
        for k in range(SLOTS):
            order[n + k] = (k * CL + c) * TGT + listed[k, c]
        n = n + live[0, c]
    for u in range(PAD):
        order[n + u] = order[0]
    order[LIST - 1] = n


def centroid_kernel(listed, live, sp, sm, tp, tm, row_out, own_out, slice_out, order):
    s = lax.axis_index("src")
    fill_order(order, listed, live)
    mass = sm[...]
    total = jnp.sum(mass, axis=1, keepdims=True)
    inv = 1.0 / total
    cols = [jnp.sum(sp[d] * mass, axis=1, keepdims=True) * inv for d in range(3)]
    cols.append(jnp.log2(total))
    lane = iota((CL, 128), 1)
    z = jnp.zeros((CL, 128), F32)
    for q in range(4):
        z = jnp.where(lane == q, cols[q], z)
    zt = jnp.concatenate([z, jnp.zeros((128 - CL, 128), F32)], axis=0).T
    row = zt[0:1, :]
    for q in range(1, 4):
        row = row + pltpu.roll(zt[q : q + 1, :], CL * q, 1)
    row_out[...] = jnp.broadcast_to(row, row_out.shape)
    slice_out[...] = tm[pl.ds(pl.multiple_of(8 * s, 8), 8), :]
    weight = tm[...]
    total = jnp.sum(weight, axis=0, keepdims=True)
    inv = 1.0 / total
    rows = [jnp.sum(tp[d] * weight, axis=0, keepdims=True) * inv for d in range(3)]
    rows.append(jnp.log2(total))
    for q in range(4):
        own_out[q : q + 1, :] = rows[q]


def dup(table, r, piece):
    for h in range(2):
        table[h, pl.ds(r, CL, stride=16), :] = piece[:, 128 * h : 128 * h + 128]


def own_terms(tp, tm):
    return jnp.log2(tm[...]) - (0.5 * ALPHA) * (tp[0] * tp[0] + tp[1] * tp[1] + tp[2] * tp[2])


def fill_tables(tab, tp, tm):
    for d in range(3):
        y = tp[d].T
        high = bf16_part(y)
        tab[2 * d] = high
        tab[2 * d + 1] = bf16_part(y - high)
    tab[6] = own_terms(tp, tm).T


def target_factors(tab, at, extra):
    sub = iota((16, PTS), 0)
    stack = jnp.ones((16, PTS), F32)
    rows = [tab[q, pl.ds(at, 1), :] for q in (0, 0, 1, 2, 2, 3, 4, 4, 5)]
    own = tab[6, pl.ds(at, 1), :]
    for r, row in enumerate((*rows, *split3(own if extra is None else own + extra))):
        stack = jnp.where(sub == r, row, stack)
    return stack.astype(BF16)


def source_factors(table, x, own):
    for d in range(3):
        a, b, _ = split3(x[d])
        for r, piece in enumerate((a, b, a)):
            dup(table, 3 * d + r, piece)
    for r in range(9, 12):
        dup(table, r, jnp.ones((CL, PTS), F32))
    for r, piece in enumerate(own):
        dup(table, 12 + r, piece)


def row_kernel(order, sp, tp, tm, r_out, l_out, tab, gt, gf, scol, lrow, *sets):
    sets = [sets[3 * u : 3 * u + 3] for u in range(AHEAD)]
    n = order[LIST - 1]
    zero = jnp.zeros((CL, PTS), F32)
    source_factors(gf, [sp[d] * ALPHA for d in range(3)], [zero] * 4)
    for c in range(CL):
        gt[c] = jnp.concatenate([gf[h, 16 * c : 16 * c + 16, :] for h in range(2)], axis=1).astype(BF16)
    fill_tables(tab, tp, tm)
    lrow[...] = jnp.full((BLOCKS, 128), -1.0, F32)

    def prepare(i, lhs):
        at = order[i] & (TGT - 1)
        lhs[...] = target_factors(tab, at, None).T
        lrow[pl.ds(order[i] >> 8, 1), :] = jnp.broadcast_to(at.astype(F32), (1, 128))

    for u in range(AHEAD):
        prepare(u, sets[u][0])

    def batch(i, _):
        at = AHEAD * i
        v = [jnp.dot(sets[u][0][...], gt[(order[at + u] >> 8) & (CL - 1)], preferred_element_type=F32) for u in range(AHEAD)]
        for u in range(AHEAD):
            prepare(at + AHEAD + u, sets[u][0])
        for u in range(AHEAD):
            lhs, score, tops = sets[u]
            top_old = tops[...]
            total = jnp.zeros((8, PTS), F32)
            top = jnp.full((8, PTS), NEG, F32)
            for j in range(0, TGT, 8):
                total = total + jnp.exp2(score[j : j + 8, :] - top_old)
                score[j : j + 8, :] = v[u][j : j + 8, :]
                top = jnp.maximum(top, v[u][j : j + 8, :])
            tops[...] = jnp.broadcast_to(jnp.max(top, axis=0, keepdims=True), (8, PTS))
            old = order[jnp.maximum(at - AHEAD + u, 0)] >> 8
            r_out[pl.ds(old, 1), :] = top_old[0:1, :]
            scol[pl.ds(old, 1), :] = jnp.sum(total, axis=0, keepdims=True)
        return 0

    lax.fori_loop(0, (n + AHEAD - 1) // AHEAD + 1, batch, 0)
    xn = (-0.5 * ALPHA) * (sp[0] * sp[0] + sp[1] * sp[1] + sp[2] * sp[2])
    r = r_out[...] + jnp.log2(scol[...])
    r = (r.reshape(SLOTS, CL, PTS) + xn[None]).reshape(BLOCKS, PTS)
    r_out[...] = jnp.where(lrow[:, 0:1] >= 0.0, r, NEG)
    l_out[...] = lrow[...]


def coarse_kernel(got, own, own1, own2, own3, r_in, l_in, g_out, l_out, terms, scores):
    def side(table, h):
        rows = [table[q : q + 1, h : h + 128] for q in range(4)]
        norm = rows[0] * rows[0] + rows[1] * rows[1] + rows[2] * rows[2]
        return [rows[0], rows[1], rows[2], rows[3] - (0.5 * ALPHA) * norm]

    tgt = [side(table, h) for table in (own, own1, own2, own3) for h in (0, 128)]
    size = got.shape[0]
    for c in range(CL):
        x = [jnp.broadcast_to(ALPHA * got[:, CL * d + c : CL * d + c + 1], (size, 128)) for d in range(3)]
        peak = None
        for li, y in enumerate(tgt):
            v = (y[3] + x[0] * y[0]) + (x[1] * y[1] + x[2] * y[2])
            scores[li] = v
            peak = v if peak is None else jnp.maximum(peak, v)
            if li < 2:
                terms[size * c : size * (c + 1), 128 * li : 128 * li + 128] = v
        peak = jnp.max(peak, axis=1, keepdims=True)
        total = jnp.exp2(scores[0] - peak)
        for li in range(1, 8):
            total = total + jnp.exp2(scores[li] - peak)
        total = jnp.sum(total, axis=1, keepdims=True)
        const = got[:, 3 * CL + c : 3 * CL + c + 1] - (peak + jnp.log2(total))
        for h in (0, 128):
            terms[size * c : size * (c + 1), h : h + 128] += jnp.broadcast_to(const, (size, 128))
    top_g = jnp.full((8, TGT), NEG, F32)
    for i in range(0, size * CL, 8):
        top_g = jnp.maximum(top_g, terms[i : i + 8, :])
    top = jnp.max(top_g, axis=0, keepdims=True)
    total = jnp.zeros((8, TGT), F32)
    for i in range(0, size * CL, 8):
        total = total + jnp.exp2(terms[i : i + 8, :] - top)
    g = own[3:4, :] - top - jnp.log2(jnp.sum(total, axis=0, keepdims=True))
    g_out[...] = jnp.broadcast_to(g, g_out.shape)
    at = l_in[...]
    lane = iota((128, 128), 1).astype(F32)
    hit = jnp.where(at == lane, g[:, :128], 0.0) + jnp.where(at == lane + 128.0, g[:, 128:], 0.0)
    picked = jnp.sum(hit, axis=1, keepdims=True)
    r = (r_in[...] + picked).reshape(SLOTS, CL, PTS)
    top = jnp.max(r, axis=0)
    l_out[...] = top + jnp.log2(jnp.sum(jnp.exp2(r - top[None]), axis=0))


def column_kernel(order, g, sp, sm, tp, tm, l0, l1, l2, l3, f_out, s_out, tab, gt, gf, st, fbuf, sem):
    parts = [p[...] for p in (l0, l1, l2, l3)]
    top = functools.reduce(jnp.maximum, parts)
    f = -(top + jnp.log2(sum(jnp.exp2(p - top) for p in parts)))
    fbuf[...] = f * UNSCALE
    send = pltpu.make_async_copy(fbuf, f_out, sem)
    send.start()
    st[...] = jnp.zeros_like(st)
    fill_tables(tab, tp, tm)
    own = f + jnp.log2(sm[...]) - (0.5 * ALPHA) * (sp[0] * sp[0] + sp[1] * sp[1] + sp[2] * sp[2])
    zero = jnp.zeros((CL, PTS), F32)
    source_factors(gf, [sp[d] * ALPHA for d in range(3)], (*split3(own), zero))
    for c in range(CL):
        gt[c] = jnp.concatenate([gf[h, 16 * c : 16 * c + 16, :] for h in range(2)], axis=1).astype(BF16).T
    n = order[LIST - 1]

    def batch(i, _):
        at = i * UNROLL
        v = []
        for u in range(UNROLL):
            left = gt[(order[at + u] >> 8) & (CL - 1)]
            to = order[at + u] & (TGT - 1)
            right = target_factors(tab, to, g[0, to])
            v.append(jnp.dot(left, right, preferred_element_type=F32))
        lines = []
        for u in range(UNROLL):
            total = jnp.zeros((8, TGT), F32)
            for o in range(0, PTS, 8):
                total = total + jnp.exp2(v[u][o : o + 8, :])
            line = jnp.sum(total, axis=0, keepdims=True)
            lines.append(jnp.where(at + u < n, line, 0.0))
        for u in range(UNROLL):
            to = pl.ds(order[at + u] & (TGT - 1), 1)
            st[to, :] = st[to, :] + lines[u]
        return 0

    lax.fori_loop(0, (n + UNROLL - 1) // UNROLL, batch, 0)
    s_out[...] = st[...].T.reshape(32, 8, TGT)
    send.wait()


def final_kernel(arrived, mass, g, out):
    total = jnp.sum(arrived[...], axis=0)
    out[...] = (g[...] - jnp.log2(1.0 + total / mass[...])) * UNSCALE


def over_tgt(part):
    return [part] + [lax.ppermute(part, "tgt", [(i, (i + k) % 4) for i in range(4)]) for k in (1, 2, 3)]


def on_device(src_pts, src_mass, tgt_pts, tgt_mass, listed, live):
    shape = jax.ShapeDtypeStruct
    params = pltpu.CompilerParams(vmem_limit_bytes=LIMIT)
    slots = listed.transpose(1, 2, 0).reshape(SLOTS, CL)
    counts = live.transpose(1, 0)
    row, own, mass, order = pl.pallas_call(
        centroid_kernel,
        out_shape=(shape((32, 128), F32), shape((8, 256), F32), shape((8, 256), F32), shape((LIST,), I32)),
        in_specs=[SMEM, SMEM] + [VMEM] * 4,
        out_specs=(VMEM, VMEM, VMEM, SMEM),
        name="centroids",
    )(slots, counts, src_pts, src_mass, tgt_pts, tgt_mass)
    got = lax.all_to_all(row, "src", split_axis=0, concat_axis=0, tiled=True)
    owns = over_tgt(own)
    r, where = pl.pallas_call(
        row_kernel,
        out_shape=(shape((BLOCKS, PTS), F32), shape((128, 128), F32)),
        in_specs=[SMEM, VMEM, VMEM, VMEM],
        out_specs=(VMEM, VMEM),
        scratch_shapes=[
            pltpu.VMEM((7, TGT, PTS), F32),
            pltpu.VMEM((CL, 16, PTS), BF16),
            pltpu.VMEM((2, CL * 16, 128), F32),
            pltpu.VMEM((BLOCKS, PTS), F32),
            pltpu.VMEM((BLOCKS, 128), F32),
        ]
        + [pltpu.VMEM((TGT, 16), BF16), pltpu.VMEM((TGT, PTS), F32), pltpu.VMEM((8, PTS), F32)] * AHEAD,
        cost_estimate=pl.CostEstimate(flops=100_000_000, bytes_accessed=10_000_000, transcendentals=5_000_000),
        compiler_params=params,
        name="rows",
    )(order, src_pts, tgt_pts, tgt_mass)
    g, part = pl.pallas_call(
        coarse_kernel,
        out_shape=(shape((8, 256), F32), shape((CL, PTS), F32)),
        in_specs=[VMEM] * 7,
        out_specs=(VMEM, VMEM),
        scratch_shapes=[pltpu.VMEM((512, 256), F32), pltpu.VMEM((8, 32, 128), F32)],
        compiler_params=params,
        name="coarse",
    )(got, *owns, r, where)
    parts = over_tgt(part)
    fine_f, sums = pl.pallas_call(
        column_kernel,
        out_shape=(shape((CL, PTS), F32), shape((32, 8, TGT), F32)),
        in_specs=[SMEM, SMEM] + [VMEM] * 8,
        out_specs=(ANY, VMEM),
        scratch_shapes=[
            pltpu.VMEM((7, TGT, PTS), F32),
            pltpu.VMEM((CL, PTS, 16), BF16),
            pltpu.VMEM((2, CL * 16, 128), F32),
            pltpu.VMEM((TGT, PTS), F32),
            pltpu.VMEM((CL, PTS), F32),
            pltpu.SemaphoreType.DMA,
        ],
        compiler_params=params,
        name="columns",
    )(order, g, src_pts, src_mass, tgt_pts, tgt_mass, *parts)
    arrived = lax.all_to_all(sums, "src", split_axis=0, concat_axis=0, tiled=True)
    fine_g = pl.pallas_call(
        final_kernel,
        out_shape=shape((8, TGT), F32),
        in_specs=[VMEM] * 3,
        out_specs=VMEM,
        compiler_params=params,
        name="final",
    )(arrived, mass, g)
    return fine_f, fine_g


def solution(mesh):
    placed = (
        P(None, "src", None),
        P("src", None),
        P(None, None, "tgt"),
        P(None, "tgt"),
        P("src", "tgt", None),
        P("src", "tgt"),
    )
    return jax.shard_map(
        on_device,
        mesh=mesh,
        in_specs=placed,
        out_specs=(P("src", None), P("src", "tgt")),
        check_vma=False,
    )
```

```python
import functools
import math

import jax
import jax.numpy as jnp
from jax import lax
from jax.experimental import pallas as pl
from jax.experimental.pallas import tpu as pltpu
from jax.sharding import PartitionSpec as P

EPS = 0.1
NEG = -1e30
ALPHA = math.log2(math.e) / EPS
UNSCALE = EPS * math.log(2.0)
F32, BF16, I32 = jnp.float32, jnp.bfloat16, jnp.int32
CL, SLOTS, PTS, TGT = 16, 8, 256, 256
BLOCKS = CL * SLOTS
SAMPLE = 32
MARGIN = 90.0
HUGE = 1e36
BATCH = 8
MANY = 16
FEW = 4
PAD = 16
LIST = BLOCKS + 2 * PAD
LIMIT = 16 << 20
VMEM = pl.BlockSpec(memory_space=pltpu.VMEM)
SMEM = pl.BlockSpec(memory_space=pltpu.SMEM)
ANY = pl.BlockSpec(memory_space=pl.ANY)


def iota(shape, dim):
    return lax.broadcasted_iota(I32, shape, dim)


def bf16_part(value):
    big = value * 65537.0
    return big - (big - value)


def split3(value):
    high = bf16_part(value)
    rest = value - high
    mid = bf16_part(rest)
    return high, mid, rest - mid


def fill_order(order, listed, live):
    n = 0
    for c in range(CL):
        for k in range(SLOTS):
            order[n + k] = (k * CL + c) * TGT + listed[k, c]
        n = n + live[0, c]
    for u in range(PAD):
        order[n + u] = order[0]
    order[LIST - 1] = n


def centroid_kernel(listed, live, sp, sm, tp, tm, row_out, own_out, slice_out, order):
    s, t = lax.axis_index("src"), lax.axis_index("tgt")
    fill_order(order, listed, live)
    mass = sm[...]
    total = jnp.sum(mass, axis=1, keepdims=True)
    inv = 1.0 / total
    cols = [jnp.sum(sp[d] * mass, axis=1, keepdims=True) * inv for d in range(3)]
    cols.append(jnp.log2(total))
    lane = iota((CL, 128), 1)
    z = jnp.zeros((CL, 128), F32)
    for q in range(4):
        z = jnp.where(lane == q, cols[q], z)
    zt = jnp.concatenate([z, jnp.zeros((128 - CL, 128), F32)], axis=0).T
    lane = iota((1, 128), 1)
    row = jnp.zeros((1, 128), F32)
    for q in range(4):
        piece = pltpu.roll(zt[q : q + 1, :], lax.rem(128 - 4 * t, 128), 1)
        row = row + pltpu.roll(jnp.where(lane < 4, piece, 0.0), 4 * q, 1)
    slice_out[...] = tm[pl.ds(pl.multiple_of(8 * s, 8), 8), :]
    weight = tm[...]
    total = jnp.sum(weight, axis=0, keepdims=True)
    inv = 1.0 / total
    rows = [jnp.sum(tp[d] * weight, axis=0, keepdims=True) * inv for d in range(3)]
    rows.append(jnp.log2(total))
    for q in range(4):
        own_out[q : q + 1, :] = rows[q]
        half = jnp.where(s >= 16, rows[q][:, 128:], rows[q][:, :128])
        piece = pltpu.roll(half, lax.rem(128 - 8 * lax.rem(s, 16), 128), 1)
        row = row + pltpu.roll(jnp.where(lane < 8, piece, 0.0), 16 + 8 * q, 1)
    row_out[...] = jnp.broadcast_to(row, row_out.shape)


def dup(table, r, piece):
    for h in range(2):
        table[h, pl.ds(r, CL, stride=16), :] = piece[:, 128 * h : 128 * h + 128]


def own_terms(tp, tm):
    return jnp.log2(tm[...]) - (0.5 * ALPHA) * (tp[0] * tp[0] + tp[1] * tp[1] + tp[2] * tp[2])


def fill_tables(tab, tp, tm):
    for d in range(3):
        y = tp[d].T
        high = bf16_part(y)
        tab[2 * d] = high
        tab[2 * d + 1] = bf16_part(y - high)
    tab[6] = own_terms(tp, tm).T


def target_factors(tab, at, extra):
    sub = iota((16, PTS), 0)
    stack = jnp.ones((16, PTS), F32)
    rows = [tab[q, pl.ds(at, 1), :] for q in (0, 0, 1, 2, 2, 3, 4, 4, 5)]
    own = tab[6, pl.ds(at, 1), :]
    for r, row in enumerate((*rows, *split3(own if extra is None else own + extra))):
        stack = jnp.where(sub == r, row, stack)
    return stack.astype(BF16)


def source_factors(table, x, own):
    for d in range(3):
        a, b, _ = split3(x[d])
        for r, piece in enumerate((a, b, a)):
            dup(table, 3 * d + r, piece)
    for r in range(9, 12):
        dup(table, r, jnp.ones((CL, PTS), F32))
    for r, piece in enumerate(own):
        dup(table, 12 + r, piece)


def exp_sum(score):
    total = jnp.zeros((8, PTS), F32)
    for o in range(0, TGT, 8):
        total = total + jnp.exp2(score[o : o + 8, :])
    return jnp.sum(total, axis=0, keepdims=True)


def row_kernel(order, sp, tp, tm, r_out, l_out, tab, gt, gf, scol, lrow, *scratch):
    factors = [scratch[2 * u : 2 * u + 2] for u in range(BATCH)]
    n = order[LIST - 1]
    zero = jnp.zeros((CL, PTS), F32)
    source_factors(gf, [sp[d] * ALPHA for d in range(3)], [zero] * 4)
    for c in range(CL):
        gt[c] = jnp.concatenate([gf[h, 16 * c : 16 * c + 16, :] for h in range(2)], axis=1)
    fill_tables(tab, tp, tm)
    lrow[...] = jnp.full((BLOCKS, 128), -1.0, F32)
    scol[...] = jnp.zeros((BLOCKS, PTS), F32)
    sub = iota((16, PTS), 0)

    def prepare(i, lhs, rhs):
        b, at = order[i] >> 8, order[i] & (TGT - 1)
        left = target_factors(tab, at, None).T
        right = gt[b & (CL - 1)]
        seen = jnp.dot(left[:SAMPLE, :], right.astype(BF16), preferred_element_type=F32)
        shift = jnp.max(seen, axis=0, keepdims=True) + MARGIN
        for r, piece in enumerate(split3(-shift)):
            right = jnp.where(sub == 12 + r, piece, right)
        lhs[...] = left
        rhs[...] = right.astype(BF16)
        r_out[pl.ds(b, 1), :] = shift
        lrow[pl.ds(b, 1), :] = jnp.broadcast_to(at.astype(F32), (1, 128))

    for u in range(BATCH):
        prepare(u, *factors[u])

    def batch(i, _):
        at = BATCH * i
        scores = [jnp.dot(lhs[...], rhs[...], preferred_element_type=F32) for lhs, rhs in factors]
        for u in range(BATCH):
            prepare(at + BATCH + u, *factors[u])
        for u in range(BATCH):
            scol[pl.ds(order[at + u] >> 8, 1), :] = exp_sum(scores[u])
        return 0

    lax.fori_loop(0, (n + BATCH - 1) // BATCH, batch, 0)

    @pl.when(jnp.max(scol[...]) > HUGE)
    def _():
        def exact(i, _):
            b = order[i] >> 8
            left = target_factors(tab, order[i] & (TGT - 1), None).T
            v = jnp.dot(left, gt[b & (CL - 1)].astype(BF16), preferred_element_type=F32)
            top = jnp.max(v, axis=0, keepdims=True)
            r_out[pl.ds(b, 1), :] = top
            scol[pl.ds(b, 1), :] = jnp.sum(jnp.exp2(v - top), axis=0, keepdims=True)
            return 0

        lax.fori_loop(0, n, exact, 0)

    xn = (-0.5 * ALPHA) * (sp[0] * sp[0] + sp[1] * sp[1] + sp[2] * sp[2])
    r = r_out[...] + jnp.log2(scol[...])
    r = (r.reshape(SLOTS, CL, PTS) + xn[None]).reshape(BLOCKS, PTS)
    r_out[...] = jnp.where(lrow[:, 0:1] >= 0.0, r, NEG)
    l_out[...] = lrow[...]


def coarse_kernel(got, own, r_in, l_in, g_out, l_out, terms, scores):
    turned = got[...].T

    def side(rows):
        norm = rows[0] * rows[0] + rows[1] * rows[1] + rows[2] * rows[2]
        return [rows[0], rows[1], rows[2], rows[3] - (0.5 * ALPHA) * norm]

    tgt = [side([turned[16 + 8 * q + li : 17 + 8 * q + li, :] for q in range(4)]) for li in range(8)]
    mine = side([own[q : q + 1, :] for q in range(4)])
    step = 32
    top_g = jnp.full((8, TGT), NEG, F32)
    for ci in range(4):
        for i in range(0, 128, step):
            x = [jnp.broadcast_to(ALPHA * got[i : i + step, 4 * d + ci : 4 * d + ci + 1], (step, 128)) for d in range(3)]
            peak = None
            for li, y in enumerate(tgt):
                v = (y[3] + x[0] * y[0]) + (x[1] * y[1] + x[2] * y[2])
                scores[li] = v
                peak = v if peak is None else jnp.maximum(peak, v)
            peak = jnp.max(peak, axis=1, keepdims=True)
            total = jnp.exp2(scores[0] - peak)
            for li in range(1, 8):
                total = total + jnp.exp2(scores[li] - peak)
            total = jnp.sum(total, axis=1, keepdims=True)
            const = got[i : i + step, 12 + ci : 13 + ci] - (peak + jnp.log2(total))
            const = jnp.broadcast_to(const, (step, 128))
            for h in (0, 128):
                y = [row[:, h : h + 128] for row in mine]
                v = (const + x[0] * y[0]) + (x[1] * y[1] + x[2] * y[2])
                terms[128 * ci + i : 128 * ci + i + step, h : h + 128] = v
    for i in range(0, 512, 8):
        top_g = jnp.maximum(top_g, terms[i : i + 8, :])
    top = jnp.max(top_g, axis=0, keepdims=True)
    total = jnp.zeros((8, TGT), F32)
    for i in range(0, 512, 8):
        total = total + jnp.exp2(terms[i : i + 8, :] - top)
    g = (mine[3] - own[3:4, :]) + top + jnp.log2(jnp.sum(total, axis=0, keepdims=True))
    g = -g
    g_out[...] = jnp.broadcast_to(g, g_out.shape)
    at = l_in[...]
    lane = iota((128, 128), 1).astype(F32)
    hit = jnp.where(at == lane, g[:, :128], 0.0) + jnp.where(at == lane + 128.0, g[:, 128:], 0.0)
    picked = jnp.sum(hit, axis=1, keepdims=True)
    r = (r_in[...] + picked).reshape(SLOTS, CL, PTS)
    top = jnp.max(r, axis=0)
    l_out[...] = top + jnp.log2(jnp.sum(jnp.exp2(r - top[None]), axis=0))


def column_kernel(order, g, sp, sm, tp, tm, l0, l1, l2, l3, f_out, s_out, tab, gt, gf, st, fbuf, sem):
    parts = [p[...] for p in (l0, l1, l2, l3)]
    top = functools.reduce(jnp.maximum, parts)
    f = -(top + jnp.log2(sum(jnp.exp2(p - top) for p in parts)))
    fbuf[...] = f * UNSCALE
    send = pltpu.make_async_copy(fbuf, f_out, sem)
    send.start()
    st[...] = jnp.zeros_like(st)
    fill_tables(tab, tp, tm)
    own = f + jnp.log2(sm[...]) - (0.5 * ALPHA) * (sp[0] * sp[0] + sp[1] * sp[1] + sp[2] * sp[2])
    zero = jnp.zeros((CL, PTS), F32)
    source_factors(gf, [sp[d] * ALPHA for d in range(3)], (*split3(own), zero))
    for c in range(CL):
        gt[c] = jnp.concatenate([gf[h, 16 * c : 16 * c + 16, :] for h in range(2)], axis=1).astype(BF16).T
    n = order[LIST - 1]

    def batch(at, size):
        scores = []
        for u in range(size):
            left = gt[(order[at + u] >> 8) & (CL - 1)]
            to = order[at + u] & (TGT - 1)
            scores.append(jnp.dot(left, target_factors(tab, to, g[0, to]), preferred_element_type=F32))
        lines = [jnp.where(at + u < n, exp_sum(scores[u]), 0.0) for u in range(size)]
        for u in range(size):
            to = pl.ds(order[at + u] & (TGT - 1), 1)
            st[to, :] = st[to, :] + lines[u]
        return 0

    whole = n // MANY
    lax.fori_loop(0, whole, lambda i, _: batch(MANY * i, MANY), 0)
    lax.fori_loop(0, (n - MANY * whole + FEW - 1) // FEW, lambda i, _: batch(MANY * whole + FEW * i, FEW), 0)
    s_out[...] = st[...].T.reshape(32, 8, TGT)
    send.wait()


def final_kernel(arrived, mass, g, out):
    total = jnp.sum(arrived[...], axis=0)
    out[...] = (g[...] - jnp.log2(1.0 + total / mass[...])) * UNSCALE


def on_device(src_pts, src_mass, tgt_pts, tgt_mass, listed, live):
    shape = jax.ShapeDtypeStruct
    params = pltpu.CompilerParams(vmem_limit_bytes=LIMIT)
    stages = [pltpu.VMEM((TGT, 16), BF16), pltpu.VMEM((16, PTS), BF16)] * BATCH
    slots = listed.transpose(1, 2, 0).reshape(SLOTS, CL)
    counts = live.transpose(1, 0)
    row, own, mass, order = pl.pallas_call(
        centroid_kernel,
        out_shape=(shape((128, 128), F32), shape((8, 256), F32), shape((8, 256), F32), shape((LIST,), I32)),
        in_specs=[SMEM, SMEM] + [VMEM] * 4,
        out_specs=(VMEM, VMEM, VMEM, SMEM),
        name="centroids",
    )(slots, counts, src_pts, src_mass, tgt_pts, tgt_mass)
    got = lax.all_to_all(row, ("src", "tgt"), split_axis=0, concat_axis=0, tiled=True)
    r, where = pl.pallas_call(
        row_kernel,
        out_shape=(shape((BLOCKS, PTS), F32), shape((128, 128), F32)),
        in_specs=[SMEM, VMEM, VMEM, VMEM],
        out_specs=(VMEM, VMEM),
        scratch_shapes=[
            pltpu.VMEM((7, TGT, PTS), F32),
            pltpu.VMEM((CL, 16, PTS), F32),
            pltpu.VMEM((2, CL * 16, 128), F32),
            pltpu.VMEM((BLOCKS, PTS), F32),
            pltpu.VMEM((BLOCKS, 128), F32),
        ]
        + stages,
        cost_estimate=pl.CostEstimate(flops=100_000_000, bytes_accessed=10_000_000, transcendentals=5_000_000),
        compiler_params=params,
        name="rows",
    )(order, src_pts, tgt_pts, tgt_mass)
    g, part = pl.pallas_call(
        coarse_kernel,
        out_shape=(shape((8, 256), F32), shape((CL, PTS), F32)),
        in_specs=[VMEM] * 4,
        out_specs=(VMEM, VMEM),
        scratch_shapes=[pltpu.VMEM((512, 256), F32), pltpu.VMEM((8, 32, 128), F32)],
        compiler_params=params,
        name="coarse",
    )(got, own, r, where)
    parts = [part] + [
        lax.ppermute(part, "tgt", [(i, (i + k) % 4) for i in range(4)]) for k in (1, 2, 3)
    ]
    fine_f, sums = pl.pallas_call(
        column_kernel,
        out_shape=(shape((CL, PTS), F32), shape((32, 8, TGT), F32)),
        in_specs=[SMEM, SMEM] + [VMEM] * 8,
        out_specs=(ANY, VMEM),
        scratch_shapes=[
            pltpu.VMEM((7, TGT, PTS), F32),
            pltpu.VMEM((CL, PTS, 16), BF16),
            pltpu.VMEM((2, CL * 16, 128), F32),
            pltpu.VMEM((TGT, PTS), F32),
            pltpu.VMEM((CL, PTS), F32),
            pltpu.SemaphoreType.DMA,
        ],
        compiler_params=params,
        name="columns",
    )(order, g, src_pts, src_mass, tgt_pts, tgt_mass, *parts)
    arrived = lax.all_to_all(sums, "src", split_axis=0, concat_axis=0, tiled=True)
    fine_g = pl.pallas_call(
        final_kernel,
        out_shape=shape((8, TGT), F32),
        in_specs=[VMEM] * 3,
        out_specs=VMEM,
        compiler_params=params,
        name="final",
    )(arrived, mass, g)
    return fine_f, fine_g


def solution(mesh):
    placed = (
        P(None, "src", None),
        P("src", None),
        P(None, None, "tgt"),
        P(None, "tgt"),
        P("src", "tgt", None),
        P("src", "tgt"),
    )
    return jax.shard_map(
        on_device,
        mesh=mesh,
        in_specs=placed,
        out_specs=(P("src", None), P("src", "tgt")),
        check_vma=False,
    )
```

```python
import functools
import math

import jax
import jax.numpy as jnp
from jax import lax
from jax.experimental import pallas as pl
from jax.experimental.pallas import tpu as pltpu
from jax.sharding import PartitionSpec as P

EPS = 0.1
NEG = -1e30
ALPHA = math.log2(math.e) / EPS
UNSCALE = EPS * math.log(2.0)
F32, BF16, I32 = jnp.float32, jnp.bfloat16, jnp.int32
CL, SLOTS, PTS, TGT = 16, 8, 256, 256
BLOCKS = CL * SLOTS
SAMPLE = 32
MARGIN = 90.0
HUGE = 1e36
BATCH = 8
MANY = 16
FEW = 4
PAD = 16
LIST = BLOCKS + 2 * PAD
LIMIT = 16 << 20
VMEM = pl.BlockSpec(memory_space=pltpu.VMEM)
SMEM = pl.BlockSpec(memory_space=pltpu.SMEM)
ANY = pl.BlockSpec(memory_space=pl.ANY)


def iota(shape, dim):
    return lax.broadcasted_iota(I32, shape, dim)


def bf16_part(value):
    big = value * 65537.0
    return big - (big - value)


def split3(value):
    high = bf16_part(value)
    rest = value - high
    mid = bf16_part(rest)
    return high, mid, rest - mid


def fill_order(order, listed, live):
    n = 0
    for c in range(CL):
        for k in range(SLOTS):
            order[n + k] = (k * CL + c) * TGT + listed[k, c]
        n = n + live[0, c]
    for u in range(PAD):
        order[n + u] = order[0]
    order[LIST - 1] = n


def centroid_kernel(listed, live, sp, sm, tp, tm, row_out, own_out, slice_out, order):
    s, t = lax.axis_index("src"), lax.axis_index("tgt")
    fill_order(order, listed, live)
    mass = sm[...]
    total = jnp.sum(mass, axis=1, keepdims=True)
    inv = 1.0 / total
    cols = [jnp.sum(sp[d] * mass, axis=1, keepdims=True) * inv for d in range(3)]
    cols.append(jnp.log2(total))
    lane = iota((CL, 128), 1)
    z = jnp.zeros((CL, 128), F32)
    for q in range(4):
        z = jnp.where(lane == q, cols[q], z)
    zt = jnp.concatenate([z, jnp.zeros((128 - CL, 128), F32)], axis=0).T
    lane = iota((1, 128), 1)
    row = jnp.zeros((1, 128), F32)
    for q in range(4):
        piece = pltpu.roll(zt[q : q + 1, :], lax.rem(128 - 4 * t, 128), 1)
        row = row + pltpu.roll(jnp.where(lane < 4, piece, 0.0), 4 * q, 1)
    slice_out[...] = tm[pl.ds(pl.multiple_of(8 * s, 8), 8), :]
    weight = tm[...]
    total = jnp.sum(weight, axis=0, keepdims=True)
    inv = 1.0 / total
    rows = [jnp.sum(tp[d] * weight, axis=0, keepdims=True) * inv for d in range(3)]
    rows.append(jnp.log2(total))
    for q in range(4):
        own_out[q : q + 1, :] = rows[q]
        half = jnp.where(s >= 16, rows[q][:, 128:], rows[q][:, :128])
        piece = pltpu.roll(half, lax.rem(128 - 8 * lax.rem(s, 16), 128), 1)
        row = row + pltpu.roll(jnp.where(lane < 8, piece, 0.0), 16 + 8 * q, 1)
    row_out[...] = jnp.broadcast_to(row, row_out.shape)


def dup(table, r, piece):
    for h in range(2):
        table[h, pl.ds(r, CL, stride=16), :] = piece[:, 128 * h : 128 * h + 128]


def own_terms(tp, tm):
    return jnp.log2(tm[...]) - (0.5 * ALPHA) * (tp[0] * tp[0] + tp[1] * tp[1] + tp[2] * tp[2])


def fill_tables(tab, tp, tm):
    for d in range(3):
        y = tp[d].T
        high = bf16_part(y)
        tab[2 * d] = high
        tab[2 * d + 1] = bf16_part(y - high)
    tab[6] = own_terms(tp, tm).T


def target_factors(tab, at, extra):
    sub = iota((16, PTS), 0)
    stack = jnp.ones((16, PTS), F32)
    rows = [tab[q, pl.ds(at, 1), :] for q in (0, 0, 1, 2, 2, 3, 4, 4, 5)]
    own = tab[6, pl.ds(at, 1), :]
    for r, row in enumerate((*rows, *split3(own if extra is None else own + extra))):
        stack = jnp.where(sub == r, row, stack)
    return stack.astype(BF16)


def source_factors(table, x, own):
    for d in range(3):
        a, b, _ = split3(x[d])
        for r, piece in enumerate((a, b, a)):
            dup(table, 3 * d + r, piece)
    for r in range(9, 12):
        dup(table, r, jnp.ones((CL, PTS), F32))
    for r, piece in enumerate(own):
        dup(table, 12 + r, piece)


def exp_sum(score):
    total = jnp.zeros((8, PTS), F32)
    for o in range(0, TGT, 8):
        total = total + jnp.exp2(score[o : o + 8, :])
    return jnp.sum(total, axis=0, keepdims=True)


def row_kernel(order, sp, tp, tm, r_out, l_out, tab, gt, gf, scol, lrow, *scratch):
    factors = [scratch[2 * u : 2 * u + 2] for u in range(BATCH)]
    n = order[LIST - 1]
    zero = jnp.zeros((CL, PTS), F32)
    source_factors(gf, [sp[d] * ALPHA for d in range(3)], [zero] * 4)
    for c in range(CL):
        gt[c] = jnp.concatenate([gf[h, 16 * c : 16 * c + 16, :] for h in range(2)], axis=1)
    fill_tables(tab, tp, tm)
    lrow[...] = jnp.full((BLOCKS, 128), -1.0, F32)
    scol[...] = jnp.zeros((BLOCKS, PTS), F32)
    sub = iota((16, PTS), 0)

    def prepare(i, lhs, rhs):
        b, at = order[i] >> 8, order[i] & (TGT - 1)
        left = target_factors(tab, at, None).T
        right = gt[b & (CL - 1)]
        seen = jnp.dot(left[:SAMPLE, :], right.astype(BF16), preferred_element_type=F32)
        shift = jnp.max(seen, axis=0, keepdims=True) + MARGIN
        for r, piece in enumerate(split3(-shift)):
            right = jnp.where(sub == 12 + r, piece, right)
        lhs[...] = left
        rhs[...] = right.astype(BF16)
        r_out[pl.ds(b, 1), :] = shift
        lrow[pl.ds(b, 1), :] = jnp.broadcast_to(at.astype(F32), (1, 128))

    for u in range(BATCH):
        prepare(u, *factors[u])

    def batch(i, _):
        at = BATCH * i
        scores = [jnp.dot(lhs[...], rhs[...], preferred_element_type=F32) for lhs, rhs in factors]
        for u in range(BATCH):
            prepare(at + BATCH + u, *factors[u])
        for u in range(BATCH):
            scol[pl.ds(order[at + u] >> 8, 1), :] = exp_sum(scores[u])
        return 0

    lax.fori_loop(0, (n + BATCH - 1) // BATCH, batch, 0)

    @pl.when(jnp.max(scol[...]) > HUGE)
    def _():
        def exact(i, _):
            b = order[i] >> 8
            left = target_factors(tab, order[i] & (TGT - 1), None).T
            v = jnp.dot(left, gt[b & (CL - 1)].astype(BF16), preferred_element_type=F32)
            top = jnp.max(v, axis=0, keepdims=True)
            r_out[pl.ds(b, 1), :] = top
            scol[pl.ds(b, 1), :] = jnp.sum(jnp.exp2(v - top), axis=0, keepdims=True)
            return 0

        lax.fori_loop(0, n, exact, 0)

    xn = (-0.5 * ALPHA) * (sp[0] * sp[0] + sp[1] * sp[1] + sp[2] * sp[2])
    r = r_out[...] + jnp.log2(scol[...])
    r = (r.reshape(SLOTS, CL, PTS) + xn[None]).reshape(BLOCKS, PTS)
    r_out[...] = jnp.where(lrow[:, 0:1] >= 0.0, r, NEG)
    l_out[...] = lrow[...]


def coarse_kernel(got, own, r_in, l_in, g_out, l_out, terms, scores):
    table = got[...]
    turned = table.T
    high = bf16_part(ALPHA * table)
    mid = bf16_part(ALPHA * table - high)
    lane = iota((256, 64), 1)
    r = lane & 15
    d = (r >= 3).astype(I32) + (r >= 6).astype(I32)
    wanted = 4 * d + (lane >> 4) + jnp.where(r - 3 * d == 1, 128, 0)
    pick = jnp.where((r < 9) & (iota((256, 64), 0) == wanted), 1.0, 0.0).astype(BF16)
    left = jnp.dot(jnp.concatenate([high, mid], axis=1).astype(BF16), pick, preferred_element_type=F32)
    r = iota((128, 64), 1) & 15
    left = jnp.where((r >= 9) & (r < 12), 1.0, left).astype(BF16)

    def target_rows(y, mass):
        rows = []
        for v in y:
            a = bf16_part(v)
            rows += [a, a, bf16_part(v - a)]
        return rows + list(split3(mass - (0.5 * ALPHA) * (y[0] * y[0] + y[1] * y[1] + y[2] * y[2])))

    def stacked(rows, at):
        stack = jnp.zeros((16, rows[0].shape[1]), F32)
        sub = iota(stack.shape, 0)
        for q, row in enumerate(rows):
            stack = jnp.where(sub == q, row[at : at + 1, :], stack)
        return stack.astype(BF16)

    tiles = target_rows([turned[16 + 8 * d : 24 + 8 * d, :] for d in range(3)], turned[40:48, :])
    rights = [jnp.concatenate([stacked(tiles, 2 * p), stacked(tiles, 2 * p + 1)], axis=1) for p in range(4)]
    mine = stacked(target_rows([own[d : d + 1, :] for d in range(3)], own[3:4, :]), 0)
    zero = jnp.zeros((16, TGT), BF16)
    for ci in range(4):

        def score(right):
            placed = jnp.concatenate([right if k == ci else zero for k in range(4)], axis=0)
            return jnp.dot(left, placed, preferred_element_type=F32)

        peak = None
        for p, right in enumerate(rights):
            v = score(right)
            scores[p] = v
            peak = v if peak is None else jnp.maximum(peak, v)
        terms[128 * ci : 128 * ci + 128, :] = score(mine)
        peak = jnp.max(jnp.maximum(peak[:, :128], peak[:, 128:]), axis=1, keepdims=True)
        total = jnp.exp2(scores[0] - peak)
        for p in range(1, 4):
            total = total + jnp.exp2(scores[p] - peak)
        total = jnp.sum(total[:, :128] + total[:, 128:], axis=1, keepdims=True)
        terms[128 * ci : 128 * ci + 128, :] += table[:, 12 + ci : 13 + ci] - (peak + jnp.log2(total))
    top_g = jnp.full((8, TGT), NEG, F32)
    for i in range(0, 512, 8):
        top_g = jnp.maximum(top_g, terms[i : i + 8, :])
    top = jnp.max(top_g, axis=0, keepdims=True)
    total = jnp.zeros((8, TGT), F32)
    for i in range(0, 512, 8):
        total = total + jnp.exp2(terms[i : i + 8, :] - top)
    g = own[3:4, :] - top - jnp.log2(jnp.sum(total, axis=0, keepdims=True))
    g_out[...] = jnp.broadcast_to(g, g_out.shape)
    at = l_in[...]
    lane = iota((128, 128), 1).astype(F32)
    hit = jnp.where(at == lane, g[:, :128], 0.0) + jnp.where(at == lane + 128.0, g[:, 128:], 0.0)
    picked = jnp.sum(hit, axis=1, keepdims=True)
    r = (r_in[...] + picked).reshape(SLOTS, CL, PTS)
    top = jnp.max(r, axis=0)
    l_out[...] = top + jnp.log2(jnp.sum(jnp.exp2(r - top[None]), axis=0))


def column_kernel(order, g, sp, sm, tp, tm, l0, l1, l2, l3, f_out, s_out, tab, gt, gf, st, fbuf, sem):
    parts = [p[...] for p in (l0, l1, l2, l3)]
    top = functools.reduce(jnp.maximum, parts)
    f = -(top + jnp.log2(sum(jnp.exp2(p - top) for p in parts)))
    fbuf[...] = f * UNSCALE
    send = pltpu.make_async_copy(fbuf, f_out, sem)
    send.start()
    st[...] = jnp.zeros_like(st)
    fill_tables(tab, tp, tm)
    own = f + jnp.log2(sm[...]) - (0.5 * ALPHA) * (sp[0] * sp[0] + sp[1] * sp[1] + sp[2] * sp[2])
    zero = jnp.zeros((CL, PTS), F32)
    source_factors(gf, [sp[d] * ALPHA for d in range(3)], (*split3(own), zero))
    for c in range(CL):
        gt[c] = jnp.concatenate([gf[h, 16 * c : 16 * c + 16, :] for h in range(2)], axis=1).astype(BF16).T
    n = order[LIST - 1]

    def batch(at, size):
        scores = []
        for u in range(size):
            left = gt[(order[at + u] >> 8) & (CL - 1)]
            to = order[at + u] & (TGT - 1)
            scores.append(jnp.dot(left, target_factors(tab, to, g[0, to]), preferred_element_type=F32))
        lines = [jnp.where(at + u < n, exp_sum(scores[u]), 0.0) for u in range(size)]
        for u in range(size):
            to = pl.ds(order[at + u] & (TGT - 1), 1)
            st[to, :] = st[to, :] + lines[u]
        return 0

    whole = n // MANY
    lax.fori_loop(0, whole, lambda i, _: batch(MANY * i, MANY), 0)
    lax.fori_loop(0, (n - MANY * whole + FEW - 1) // FEW, lambda i, _: batch(MANY * whole + FEW * i, FEW), 0)
    s_out[...] = st[...].T.reshape(32, 8, TGT)
    send.wait()


def final_kernel(arrived, mass, g, out):
    total = jnp.sum(arrived[...], axis=0)
    out[...] = (g[...] - jnp.log2(1.0 + total / mass[...])) * UNSCALE


def on_device(src_pts, src_mass, tgt_pts, tgt_mass, listed, live):
    shape = jax.ShapeDtypeStruct
    params = pltpu.CompilerParams(vmem_limit_bytes=LIMIT)
    stages = [pltpu.VMEM((TGT, 16), BF16), pltpu.VMEM((16, PTS), BF16)] * BATCH
    slots = listed.transpose(1, 2, 0).reshape(SLOTS, CL)
    counts = live.transpose(1, 0)
    row, own, mass, order = pl.pallas_call(
        centroid_kernel,
        out_shape=(shape((128, 128), F32), shape((8, 256), F32), shape((8, 256), F32), shape((LIST,), I32)),
        in_specs=[SMEM, SMEM] + [VMEM] * 4,
        out_specs=(VMEM, VMEM, VMEM, SMEM),
        name="centroids",
    )(slots, counts, src_pts, src_mass, tgt_pts, tgt_mass)
    got = lax.all_to_all(row, ("src", "tgt"), split_axis=0, concat_axis=0, tiled=True)
    r, where = pl.pallas_call(
        row_kernel,
        out_shape=(shape((BLOCKS, PTS), F32), shape((128, 128), F32)),
        in_specs=[SMEM, VMEM, VMEM, VMEM],
        out_specs=(VMEM, VMEM),
        scratch_shapes=[
            pltpu.VMEM((7, TGT, PTS), F32),
            pltpu.VMEM((CL, 16, PTS), F32),
            pltpu.VMEM((2, CL * 16, 128), F32),
            pltpu.VMEM((BLOCKS, PTS), F32),
            pltpu.VMEM((BLOCKS, 128), F32),
        ]
        + stages,
        cost_estimate=pl.CostEstimate(flops=100_000_000, bytes_accessed=10_000_000, transcendentals=5_000_000),
        compiler_params=params,
        name="rows",
    )(order, src_pts, tgt_pts, tgt_mass)
    g, part = pl.pallas_call(
        coarse_kernel,
        out_shape=(shape((8, 256), F32), shape((CL, PTS), F32)),
        in_specs=[VMEM] * 4,
        out_specs=(VMEM, VMEM),
        scratch_shapes=[pltpu.VMEM((512, 256), F32), pltpu.VMEM((4, 128, 256), F32)],
        compiler_params=params,
        name="coarse",
    )(got, own, r, where)
    parts = [part] + [
        lax.ppermute(part, "tgt", [(i, (i + k) % 4) for i in range(4)]) for k in (1, 3, 2)
    ]
    fine_f, sums = pl.pallas_call(
        column_kernel,
        out_shape=(shape((CL, PTS), F32), shape((32, 8, TGT), F32)),
        in_specs=[SMEM, SMEM] + [VMEM] * 8,
        out_specs=(ANY, VMEM),
        scratch_shapes=[
            pltpu.VMEM((7, TGT, PTS), F32),
            pltpu.VMEM((CL, PTS, 16), BF16),
            pltpu.VMEM((2, CL * 16, 128), F32),
            pltpu.VMEM((TGT, PTS), F32),
            pltpu.VMEM((CL, PTS), F32),
            pltpu.SemaphoreType.DMA,
        ],
        compiler_params=params,
        name="columns",
    )(order, g, src_pts, src_mass, tgt_pts, tgt_mass, *parts)
    arrived = lax.all_to_all(sums, "src", split_axis=0, concat_axis=0, tiled=True)
    fine_g = pl.pallas_call(
        final_kernel,
        out_shape=shape((8, TGT), F32),
        in_specs=[VMEM] * 3,
        out_specs=VMEM,
        compiler_params=params,
        name="final",
    )(arrived, mass, g)
    return fine_f, fine_g


def solution(mesh):
    placed = (
        P(None, "src", None),
        P("src", None),
        P(None, None, "tgt"),
        P(None, "tgt"),
        P("src", "tgt", None),
        P("src", "tgt"),
    )
    return jax.shard_map(
        on_device,
        mesh=mesh,
        in_specs=placed,
        out_specs=(P("src", None), P("src", "tgt")),
        check_vma=False,
    )
```

```python
import functools
import math

import jax
import jax.numpy as jnp
from jax import lax
from jax.experimental import pallas as pl
from jax.experimental.pallas import tpu as pltpu
from jax.sharding import PartitionSpec as P

EPS = 0.1
NEG = -1e30
ALPHA = math.log2(math.e) / EPS
UNSCALE = EPS * math.log(2.0)
F32, BF16, I32 = jnp.float32, jnp.bfloat16, jnp.int32
CL, SLOTS, PTS, TGT = 16, 8, 256, 256
BLOCKS = CL * SLOTS
SAMPLE = 32
MARGIN = 90.0
HUGE = 1e36
BATCH = 8
MANY = 16
FEW = 4
PAD = 16
LIST = BLOCKS + 2 * PAD
LIMIT = 16 << 20
VMEM = pl.BlockSpec(memory_space=pltpu.VMEM)
SMEM = pl.BlockSpec(memory_space=pltpu.SMEM)
ANY = pl.BlockSpec(memory_space=pl.ANY)


def iota(shape, dim):
    return lax.broadcasted_iota(I32, shape, dim)


def bf16_part(value):
    big = value * 65537.0
    return big - (big - value)


def split3(value):
    high = bf16_part(value)
    rest = value - high
    mid = bf16_part(rest)
    return high, mid, rest - mid


def fill_order(order, listed, live):
    n = 0
    for c in range(CL):
        for k in range(SLOTS):
            order[n + k] = (k * CL + c) * TGT + listed[k, c]
        n = n + live[0, c]
    for u in range(PAD):
        order[n + u] = order[0]
    order[LIST - 1] = n


def centroid_kernel(listed, live, sp, sm, tp, tm, row_out, own_out, slice_out, order):
    s = lax.axis_index("src")
    fill_order(order, listed, live)
    mass = sm[...]
    total = jnp.sum(mass, axis=1, keepdims=True)
    inv = 1.0 / total
    cols = [jnp.sum(sp[d] * mass, axis=1, keepdims=True) * inv for d in range(3)]
    cols.append(jnp.log2(total))
    lane = iota((CL, 128), 1)
    z = jnp.zeros((CL, 128), F32)
    for q in range(4):
        z = jnp.where(lane == q, cols[q], z)
    zt = jnp.concatenate([z, jnp.zeros((128 - CL, 128), F32)], axis=0).T
    row = zt[0:1, :]
    for q in range(1, 4):
        row = row + pltpu.roll(zt[q : q + 1, :], CL * q, 1)
    row_out[...] = jnp.broadcast_to(row, row_out.shape)
    slice_out[...] = tm[pl.ds(pl.multiple_of(8 * s, 8), 8), :]
    weight = tm[...]
    total = jnp.sum(weight, axis=0, keepdims=True)
    inv = 1.0 / total
    rows = [jnp.sum(tp[d] * weight, axis=0, keepdims=True) * inv for d in range(3)]
    rows.append(jnp.log2(total))
    for q in range(4):
        own_out[q : q + 1, :] = rows[q]


def dup(table, r, piece):
    for h in range(2):
        table[h, pl.ds(r, CL, stride=16), :] = piece[:, 128 * h : 128 * h + 128]


def own_terms(tp, tm):
    return jnp.log2(tm[...]) - (0.5 * ALPHA) * (tp[0] * tp[0] + tp[1] * tp[1] + tp[2] * tp[2])


def fill_tables(tab, tp, tm):
    for d in range(3):
        y = tp[d].T
        high = bf16_part(y)
        tab[2 * d] = high
        tab[2 * d + 1] = bf16_part(y - high)
    tab[6] = own_terms(tp, tm).T


def target_factors(tab, at, extra):
    sub = iota((16, PTS), 0)
    stack = jnp.ones((16, PTS), F32)
    rows = [tab[q, pl.ds(at, 1), :] for q in (0, 0, 1, 2, 2, 3, 4, 4, 5)]
    own = tab[6, pl.ds(at, 1), :]
    for r, row in enumerate((*rows, *split3(own if extra is None else own + extra))):
        stack = jnp.where(sub == r, row, stack)
    return stack.astype(BF16)


def source_factors(table, x, own):
    for d in range(3):
        a, b, _ = split3(x[d])
        for r, piece in enumerate((a, b, a)):
            dup(table, 3 * d + r, piece)
    for r in range(9, 12):
        dup(table, r, jnp.ones((CL, PTS), F32))
    for r, piece in enumerate(own):
        dup(table, 12 + r, piece)


def exp_sum(score):
    total = jnp.zeros((8, PTS), F32)
    for o in range(0, TGT, 8):
        total = total + jnp.exp2(score[o : o + 8, :])
    return jnp.sum(total, axis=0, keepdims=True)


def row_kernel(order, sp, tp, tm, r_out, l_out, tab, gt, gf, scol, lrow, *scratch):
    factors = [scratch[2 * u : 2 * u + 2] for u in range(BATCH)]
    n = order[LIST - 1]
    zero = jnp.zeros((CL, PTS), F32)
    source_factors(gf, [sp[d] * ALPHA for d in range(3)], [zero] * 4)
    for c in range(CL):
        gt[c] = jnp.concatenate([gf[h, 16 * c : 16 * c + 16, :] for h in range(2)], axis=1)
    fill_tables(tab, tp, tm)
    lrow[...] = jnp.full((BLOCKS, 128), -1.0, F32)
    scol[...] = jnp.zeros((BLOCKS, PTS), F32)
    sub = iota((16, PTS), 0)

    def prepare(i, lhs, rhs):
        b, at = order[i] >> 8, order[i] & (TGT - 1)
        left = target_factors(tab, at, None).T
        right = gt[b & (CL - 1)]
        seen = jnp.dot(left[:SAMPLE, :], right.astype(BF16), preferred_element_type=F32)
        shift = jnp.max(seen, axis=0, keepdims=True) + MARGIN
        for r, piece in enumerate(split3(-shift)):
            right = jnp.where(sub == 12 + r, piece, right)
        lhs[...] = left
        rhs[...] = right.astype(BF16)
        r_out[pl.ds(b, 1), :] = shift
        lrow[pl.ds(b, 1), :] = jnp.broadcast_to(at.astype(F32), (1, 128))

    for u in range(BATCH):
        prepare(u, *factors[u])

    def batch(i, _):
        at = BATCH * i
        scores = [jnp.dot(lhs[...], rhs[...], preferred_element_type=F32) for lhs, rhs in factors]
        for u in range(BATCH):
            prepare(at + BATCH + u, *factors[u])
        for u in range(BATCH):
            scol[pl.ds(order[at + u] >> 8, 1), :] = exp_sum(scores[u])
        return 0

    lax.fori_loop(0, (n + BATCH - 1) // BATCH, batch, 0)

    @pl.when(jnp.max(scol[...]) > HUGE)
    def _():
        def exact(i, _):
            b = order[i] >> 8
            left = target_factors(tab, order[i] & (TGT - 1), None).T
            v = jnp.dot(left, gt[b & (CL - 1)].astype(BF16), preferred_element_type=F32)
            top = jnp.max(v, axis=0, keepdims=True)
            r_out[pl.ds(b, 1), :] = top
            scol[pl.ds(b, 1), :] = jnp.sum(jnp.exp2(v - top), axis=0, keepdims=True)
            return 0

        lax.fori_loop(0, n, exact, 0)

    xn = (-0.5 * ALPHA) * (sp[0] * sp[0] + sp[1] * sp[1] + sp[2] * sp[2])
    r = r_out[...] + jnp.log2(scol[...])
    r = (r.reshape(SLOTS, CL, PTS) + xn[None]).reshape(BLOCKS, PTS)
    r_out[...] = jnp.where(lrow[:, 0:1] >= 0.0, r, NEG)
    l_out[...] = lrow[...]


def coarse_kernel(got, own, own1, own2, own3, r_in, l_in, g_out, l_out, terms, scores):
    table = got[...]
    size = table.shape[0]
    high = bf16_part(ALPHA * table)
    mid = bf16_part(ALPHA * table - high)
    lane = iota((256, 256), 1)
    r = lane & 15
    d = (r >= 3).astype(I32) + (r >= 6).astype(I32)
    wanted = CL * d + (lane >> 4) + jnp.where(r - 3 * d == 1, 128, 0)
    pick = jnp.where((r < 9) & (iota((256, 256), 0) == wanted), 1.0, 0.0).astype(BF16)
    picked = jnp.dot(jnp.concatenate([high, mid], axis=1).astype(BF16), pick, preferred_element_type=F32)
    r = iota((size, 256), 1) & 15
    picked = jnp.where((r >= 9) & (r < 12), 1.0, picked)

    def source_side(c):
        half = picked[:, 128 * (c // 8) : 128 * (c // 8) + 128]
        return pltpu.roll(half, (128 - 16 * (c % 8)) % 128, 1)[:, :16]

    def target_side(own):
        y = [own[d : d + 1, :] for d in range(3)]
        rows = []
        for v in y:
            a = bf16_part(v)
            rows += [a, a, bf16_part(v - a)]
        rows += split3(own[3:4, :] - (0.5 * ALPHA) * (y[0] * y[0] + y[1] * y[1] + y[2] * y[2]))
        stack = jnp.zeros((16, TGT), F32)
        sub = iota(stack.shape, 0)
        for q, row in enumerate(rows):
            stack = jnp.where(sub == q, row, stack)
        return stack.astype(BF16)

    rights = [target_side(table) for table in (own, own1, own2, own3)]
    many = 4 * size
    for k in range(4):
        left = jnp.concatenate([source_side(4 * k + c) for c in range(4)], axis=0).astype(BF16)
        mass = jnp.concatenate([table[:, 3 * CL + 4 * k + c : 3 * CL + 4 * k + c + 1] for c in range(4)], axis=0)
        peak = None
        for p, right in enumerate(rights):
            v = jnp.dot(left, right, preferred_element_type=F32)
            scores[4 * k + p] = v
            peak = v if peak is None else jnp.maximum(peak, v)
        peak = jnp.max(jnp.maximum(peak[:, :128], peak[:, 128:]), axis=1, keepdims=True)
        total = jnp.exp2(scores[4 * k] - peak)
        for p in range(1, 4):
            total = total + jnp.exp2(scores[4 * k + p] - peak)
        total = jnp.sum(total[:, :128] + total[:, 128:], axis=1, keepdims=True)
        terms[many * k : many * (k + 1), :] = scores[4 * k] + (mass - (peak + jnp.log2(total)))
    top_g = jnp.full((8, TGT), NEG, F32)
    for i in range(0, 4 * many, 8):
        top_g = jnp.maximum(top_g, terms[i : i + 8, :])
    top = jnp.max(top_g, axis=0, keepdims=True)
    total = jnp.zeros((8, TGT), F32)
    for i in range(0, 4 * many, 8):
        total = total + jnp.exp2(terms[i : i + 8, :] - top)
    g = own[3:4, :] - top - jnp.log2(jnp.sum(total, axis=0, keepdims=True))
    g_out[...] = jnp.broadcast_to(g, g_out.shape)
    at = l_in[...]
    lane = iota((128, 128), 1).astype(F32)
    hit = jnp.where(at == lane, g[:, :128], 0.0) + jnp.where(at == lane + 128.0, g[:, 128:], 0.0)
    picked = jnp.sum(hit, axis=1, keepdims=True)
    r = (r_in[...] + picked).reshape(SLOTS, CL, PTS)
    top = jnp.max(r, axis=0)
    l_out[...] = top + jnp.log2(jnp.sum(jnp.exp2(r - top[None]), axis=0))


def column_kernel(order, g, sp, sm, tp, tm, l0, l1, l2, l3, f_out, s_out, tab, gt, gf, st, fbuf, sem):
    parts = [p[...] for p in (l0, l1, l2, l3)]
    top = functools.reduce(jnp.maximum, parts)
    f = -(top + jnp.log2(sum(jnp.exp2(p - top) for p in parts)))
    fbuf[...] = f * UNSCALE
    send = pltpu.make_async_copy(fbuf, f_out, sem)
    send.start()
    st[...] = jnp.zeros_like(st)
    fill_tables(tab, tp, tm)
    own = f + jnp.log2(sm[...]) - (0.5 * ALPHA) * (sp[0] * sp[0] + sp[1] * sp[1] + sp[2] * sp[2])
    zero = jnp.zeros((CL, PTS), F32)
    source_factors(gf, [sp[d] * ALPHA for d in range(3)], (*split3(own), zero))
    for c in range(CL):
        gt[c] = jnp.concatenate([gf[h, 16 * c : 16 * c + 16, :] for h in range(2)], axis=1).astype(BF16).T
    n = order[LIST - 1]

    def batch(at, size):
        scores = []
        for u in range(size):
            left = gt[(order[at + u] >> 8) & (CL - 1)]
            to = order[at + u] & (TGT - 1)
            scores.append(jnp.dot(left, target_factors(tab, to, g[0, to]), preferred_element_type=F32))
        lines = [jnp.where(at + u < n, exp_sum(scores[u]), 0.0) for u in range(size)]
        for u in range(size):
            to = pl.ds(order[at + u] & (TGT - 1), 1)
            st[to, :] = st[to, :] + lines[u]
        return 0

    whole = n // MANY
    lax.fori_loop(0, whole, lambda i, _: batch(MANY * i, MANY), 0)
    lax.fori_loop(0, (n - MANY * whole + FEW - 1) // FEW, lambda i, _: batch(MANY * whole + FEW * i, FEW), 0)
    s_out[...] = st[...].T.reshape(32, 8, TGT)
    send.wait()


def final_kernel(arrived, mass, g, out):
    total = jnp.sum(arrived[...], axis=0)
    out[...] = (g[...] - jnp.log2(1.0 + total / mass[...])) * UNSCALE


def over_tgt(part):
    return [part] + [lax.ppermute(part, "tgt", [(i, (i + k) % 4) for i in range(4)]) for k in (1, 2, 3)]


def program(src_pts, src_mass, tgt_pts, tgt_mass, listed, live):
    shape = jax.ShapeDtypeStruct
    params = pltpu.CompilerParams(vmem_limit_bytes=LIMIT)
    stages = [pltpu.VMEM((TGT, 16), BF16), pltpu.VMEM((16, PTS), BF16)] * BATCH
    slots = listed.transpose(1, 2, 0).reshape(SLOTS, CL)
    counts = live.transpose(1, 0)
    row, own, mass, order = pl.pallas_call(
        centroid_kernel,
        out_shape=(shape((32, 128), F32), shape((8, 256), F32), shape((8, 256), F32), shape((LIST,), I32)),
        in_specs=[SMEM, SMEM] + [VMEM] * 4,
        out_specs=(VMEM, VMEM, VMEM, SMEM),
        name="centroids",
    )(slots, counts, src_pts, src_mass, tgt_pts, tgt_mass)
    owns = over_tgt(own)
    got = lax.all_to_all(row, "src", split_axis=0, concat_axis=0, tiled=True)
    r, where = pl.pallas_call(
        row_kernel,
        out_shape=(shape((BLOCKS, PTS), F32), shape((128, 128), F32)),
        in_specs=[SMEM, VMEM, VMEM, VMEM],
        out_specs=(VMEM, VMEM),
        scratch_shapes=[
            pltpu.VMEM((7, TGT, PTS), F32),
            pltpu.VMEM((CL, 16, PTS), F32),
            pltpu.VMEM((2, CL * 16, 128), F32),
            pltpu.VMEM((BLOCKS, PTS), F32),
            pltpu.VMEM((BLOCKS, 128), F32),
        ]
        + stages,
        cost_estimate=pl.CostEstimate(flops=100_000_000, bytes_accessed=10_000_000, transcendentals=5_000_000),
        compiler_params=params,
        name="rows",
    )(order, src_pts, tgt_pts, tgt_mass)
    g, part = pl.pallas_call(
        coarse_kernel,
        out_shape=(shape((8, 256), F32), shape((CL, PTS), F32)),
        in_specs=[VMEM] * 7,
        out_specs=(VMEM, VMEM),
        scratch_shapes=[pltpu.VMEM((512, 256), F32), pltpu.VMEM((16, 128, 256), F32)],
        compiler_params=params,
        name="coarse",
    )(got, *owns, r, where)
    parts = over_tgt(part)
    fine_f, sums = pl.pallas_call(
        column_kernel,
        out_shape=(shape((CL, PTS), F32), shape((32, 8, TGT), F32)),
        in_specs=[SMEM, SMEM] + [VMEM] * 8,
        out_specs=(ANY, VMEM),
        scratch_shapes=[
            pltpu.VMEM((7, TGT, PTS), F32),
            pltpu.VMEM((CL, PTS, 16), BF16),
            pltpu.VMEM((2, CL * 16, 128), F32),
            pltpu.VMEM((TGT, PTS), F32),
            pltpu.VMEM((CL, PTS), F32),
            pltpu.SemaphoreType.DMA,
        ],
        compiler_params=params,
        name="columns",
    )(order, g, src_pts, src_mass, tgt_pts, tgt_mass, *parts)
    arrived = lax.all_to_all(sums, "src", split_axis=0, concat_axis=0, tiled=True)
    fine_g = pl.pallas_call(
        final_kernel,
        out_shape=shape((8, TGT), F32),
        in_specs=[VMEM] * 3,
        out_specs=VMEM,
        compiler_params=params,
        name="final",
    )(arrived, mass, g)
    return fine_f, fine_g


def solution(mesh):
    placed = (
        P(None, "src", None),
        P("src", None),
        P(None, None, "tgt"),
        P(None, "tgt"),
        P("src", "tgt", None),
        P("src", "tgt"),
    )
    return jax.shard_map(
        program,
        mesh=mesh,
        in_specs=placed,
        out_specs=(P("src", None), P("src", "tgt")),
        check_vma=False,
    )
```

```python
import functools
import math

import jax
import jax.numpy as jnp
from jax import lax
from jax.experimental import pallas as pl
from jax.experimental.pallas import tpu as pltpu
from jax.sharding import PartitionSpec as P

EPS = 0.1
NEG = -1e30
ALPHA = math.log2(math.e) / EPS
UNSCALE = EPS * math.log(2.0)
F32, BF16, I32 = jnp.float32, jnp.bfloat16, jnp.int32
CL, SLOTS, PTS, TGT = 16, 8, 256, 256
BLOCKS = CL * SLOTS
SAMPLE = 32
MARGIN = 90.0
HUGE = 1e36
BATCH = 8
MANY = 16
FEW = 4
PAD = 16
LIST = BLOCKS + 2 * PAD
LIMIT = 16 << 20
VMEM = pl.BlockSpec(memory_space=pltpu.VMEM)
SMEM = pl.BlockSpec(memory_space=pltpu.SMEM)
ANY = pl.BlockSpec(memory_space=pl.ANY)


def iota(shape, dim):
    return lax.broadcasted_iota(I32, shape, dim)


def bf16_part(value):
    big = value * 65537.0
    return big - (big - value)


def split3(value):
    high = bf16_part(value)
    rest = value - high
    mid = bf16_part(rest)
    return high, mid, rest - mid


def fill_order(order, listed, live):
    n = 0
    for c in range(CL):
        for k in range(SLOTS):
            order[n + k] = (k * CL + c) * TGT + listed[k, c]
        n = n + live[0, c]
    for u in range(PAD):
        order[n + u] = order[0]
    order[LIST - 1] = n


def centroid_kernel(listed, live, sp, sm, tp, tm, row_out, own_out, slice_out, order):
    s, t = lax.axis_index("src"), lax.axis_index("tgt")
    fill_order(order, listed, live)
    mass = sm[...]
    total = jnp.sum(mass, axis=1, keepdims=True)
    inv = 1.0 / total
    cols = [jnp.sum(sp[d] * mass, axis=1, keepdims=True) * inv for d in range(3)]
    cols.append(jnp.log2(total))
    lane = iota((CL, 128), 1)
    z = jnp.zeros((CL, 128), F32)
    for q in range(4):
        z = jnp.where(lane == q, cols[q], z)
    zt = jnp.concatenate([z, jnp.zeros((128 - CL, 128), F32)], axis=0).T
    lane = iota((1, 128), 1)
    row = jnp.zeros((1, 128), F32)
    for q in range(4):
        piece = pltpu.roll(zt[q : q + 1, :], lax.rem(128 - 4 * t, 128), 1)
        row = row + pltpu.roll(jnp.where(lane < 4, piece, 0.0), 4 * q, 1)
    slice_out[...] = tm[pl.ds(pl.multiple_of(8 * s, 8), 8), :]
    weight = tm[...]
    total = jnp.sum(weight, axis=0, keepdims=True)
    inv = 1.0 / total
    rows = [jnp.sum(tp[d] * weight, axis=0, keepdims=True) * inv for d in range(3)]
    rows.append(jnp.log2(total))
    for q in range(4):
        own_out[q : q + 1, :] = rows[q]
        half = jnp.where(s >= 16, rows[q][:, 128:], rows[q][:, :128])
        piece = pltpu.roll(half, lax.rem(128 - 8 * lax.rem(s, 16), 128), 1)
        row = row + pltpu.roll(jnp.where(lane < 8, piece, 0.0), 16 + 8 * q, 1)
    row_out[...] = jnp.broadcast_to(row, row_out.shape)


def dup(table, r, piece):
    for h in range(2):
        table[h, pl.ds(r, CL, stride=16), :] = piece[:, 128 * h : 128 * h + 128]


def own_terms(tp, tm):
    return jnp.log2(tm[...]) - (0.5 * ALPHA) * (tp[0] * tp[0] + tp[1] * tp[1] + tp[2] * tp[2])


def fill_tables(tab, tp, tm):
    for d in range(3):
        y = tp[d].T
        high = bf16_part(y)
        tab[2 * d] = high
        tab[2 * d + 1] = bf16_part(y - high)
    tab[6] = own_terms(tp, tm).T


def target_factors(tab, at, extra):
    sub = iota((16, PTS), 0)
    stack = jnp.ones((16, PTS), F32)
    rows = [tab[q, pl.ds(at, 1), :] for q in (0, 0, 1, 2, 2, 3, 4, 4, 5)]
    own = tab[6, pl.ds(at, 1), :]
    for r, row in enumerate((*rows, *split3(own if extra is None else own + extra))):
        stack = jnp.where(sub == r, row, stack)
    return stack.astype(BF16)


def source_factors(table, x, own):
    for d in range(3):
        a, b, _ = split3(x[d])
        for r, piece in enumerate((a, b, a)):
            dup(table, 3 * d + r, piece)
    for r in range(9, 12):
        dup(table, r, jnp.ones((CL, PTS), F32))
    for r, piece in enumerate(own):
        dup(table, 12 + r, piece)


def exp_sum(score):
    total = jnp.zeros((8, PTS), F32)
    for o in range(0, TGT, 8):
        total = total + jnp.exp2(score[o : o + 8, :])
    return jnp.sum(total, axis=0, keepdims=True)


def row_kernel(order, sp, tp, tm, r_out, l_out, tab, gt, gf, scol, lrow, *scratch):
    factors = [scratch[2 * u : 2 * u + 2] for u in range(BATCH)]
    n = order[LIST - 1]
    zero = jnp.zeros((CL, PTS), F32)
    source_factors(gf, [sp[d] * ALPHA for d in range(3)], [zero] * 4)
    for c in range(CL):
        gt[c] = jnp.concatenate([gf[h, 16 * c : 16 * c + 16, :] for h in range(2)], axis=1)
    fill_tables(tab, tp, tm)
    lrow[...] = jnp.full((BLOCKS, 128), -1.0, F32)
    scol[...] = jnp.zeros((BLOCKS, PTS), F32)
    sub = iota((16, PTS), 0)

    def prepare(i, lhs, rhs):
        b, at = order[i] >> 8, order[i] & (TGT - 1)
        left = target_factors(tab, at, None).T
        right = gt[b & (CL - 1)]
        seen = jnp.dot(left[:SAMPLE, :], right.astype(BF16), preferred_element_type=F32)
        shift = jnp.max(seen, axis=0, keepdims=True) + MARGIN
        for r, piece in enumerate(split3(-shift)):
            right = jnp.where(sub == 12 + r, piece, right)
        lhs[...] = left
        rhs[...] = right.astype(BF16)
        r_out[pl.ds(b, 1), :] = shift
        lrow[pl.ds(b, 1), :] = jnp.broadcast_to(at.astype(F32), (1, 128))

    for u in range(BATCH):
        prepare(u, *factors[u])

    def batch(i, _):
        at = BATCH * i
        scores = [jnp.dot(lhs[...], rhs[...], preferred_element_type=F32) for lhs, rhs in factors]
        for u in range(BATCH):
            prepare(at + BATCH + u, *factors[u])
        for u in range(BATCH):
            scol[pl.ds(order[at + u] >> 8, 1), :] = exp_sum(scores[u])
        return 0

    lax.fori_loop(0, (n + BATCH - 1) // BATCH, batch, 0)

    @pl.when(jnp.max(scol[...]) > HUGE)
    def _():
        def exact(i, _):
            b = order[i] >> 8
            left = target_factors(tab, order[i] & (TGT - 1), None).T
            v = jnp.dot(left, gt[b & (CL - 1)].astype(BF16), preferred_element_type=F32)
            top = jnp.max(v, axis=0, keepdims=True)
            r_out[pl.ds(b, 1), :] = top
            scol[pl.ds(b, 1), :] = jnp.sum(jnp.exp2(v - top), axis=0, keepdims=True)
            return 0

        lax.fori_loop(0, n, exact, 0)

    xn = (-0.5 * ALPHA) * (sp[0] * sp[0] + sp[1] * sp[1] + sp[2] * sp[2])
    r = r_out[...] + jnp.log2(scol[...])
    r = (r.reshape(SLOTS, CL, PTS) + xn[None]).reshape(BLOCKS, PTS)
    r_out[...] = jnp.where(lrow[:, 0:1] >= 0.0, r, NEG)
    l_out[...] = lrow[...]


def coarse_kernel(got, own, r_in, l_in, g_out, l_out, terms, scores):
    table = got[...]
    turned = table.T
    high = bf16_part(ALPHA * table)
    mid = bf16_part(ALPHA * table - high)
    lane = iota((256, 64), 1)
    r = lane & 15
    d = (r >= 3).astype(I32) + (r >= 6).astype(I32)
    wanted = 4 * d + (lane >> 4) + jnp.where(r - 3 * d == 1, 128, 0)
    pick = jnp.where((r < 9) & (iota((256, 64), 0) == wanted), 1.0, 0.0).astype(BF16)
    left = jnp.dot(jnp.concatenate([high, mid], axis=1).astype(BF16), pick, preferred_element_type=F32)
    r = iota((128, 64), 1) & 15
    left = jnp.where((r >= 9) & (r < 12), 1.0, left).astype(BF16)

    def target_rows(y, mass):
        rows = []
        for v in y:
            a = bf16_part(v)
            rows += [a, a, bf16_part(v - a)]
        return rows + list(split3(mass - (0.5 * ALPHA) * (y[0] * y[0] + y[1] * y[1] + y[2] * y[2])))

    def stacked(rows, at):
        stack = jnp.zeros((16, rows[0].shape[1]), F32)
        sub = iota(stack.shape, 0)
        for q, row in enumerate(rows):
            stack = jnp.where(sub == q, row[at : at + 1, :], stack)
        return stack.astype(BF16)

    tiles = target_rows([turned[16 + 8 * d : 24 + 8 * d, :] for d in range(3)], turned[40:48, :])
    rights = [jnp.concatenate([stacked(tiles, 2 * p), stacked(tiles, 2 * p + 1)], axis=1) for p in range(4)]
    mine = stacked(target_rows([own[d : d + 1, :] for d in range(3)], own[3:4, :]), 0)
    zero = jnp.zeros((16, TGT), BF16)
    for ci in range(4):

        def score(right):
            placed = jnp.concatenate([right if k == ci else zero for k in range(4)], axis=0)
            return jnp.dot(left, placed, preferred_element_type=F32)

        peak = None
        for p, right in enumerate(rights):
            v = score(right)
            scores[p] = v
            peak = v if peak is None else jnp.maximum(peak, v)
        terms[128 * ci : 128 * ci + 128, :] = score(mine)
        peak = jnp.max(jnp.maximum(peak[:, :128], peak[:, 128:]), axis=1, keepdims=True)
        total = jnp.exp2(scores[0] - peak)
        for p in range(1, 4):
            total = total + jnp.exp2(scores[p] - peak)
        total = jnp.sum(total[:, :128] + total[:, 128:], axis=1, keepdims=True)
        terms[128 * ci : 128 * ci + 128, :] += table[:, 12 + ci : 13 + ci] - (peak + jnp.log2(total))
    top_g = jnp.full((8, TGT), NEG, F32)
    for i in range(0, 512, 8):
        top_g = jnp.maximum(top_g, terms[i : i + 8, :])
    top = jnp.max(top_g, axis=0, keepdims=True)
    total = jnp.zeros((8, TGT), F32)
    for i in range(0, 512, 8):
        total = total + jnp.exp2(terms[i : i + 8, :] - top)
    g = own[3:4, :] - top - jnp.log2(jnp.sum(total, axis=0, keepdims=True))
    g_out[...] = jnp.broadcast_to(g, g_out.shape)
    at = l_in[...]
    lane = iota((128, 128), 1).astype(F32)
    hit = jnp.where(at == lane, g[:, :128], 0.0) + jnp.where(at == lane + 128.0, g[:, 128:], 0.0)
    picked = jnp.sum(hit, axis=1, keepdims=True)
    r = (r_in[...] + picked).reshape(SLOTS, CL, PTS)
    top = jnp.max(r, axis=0)
    l_out[...] = top + jnp.log2(jnp.sum(jnp.exp2(r - top[None]), axis=0))


def column_kernel(order, g, sp, sm, tp, tm, l0, l1, l2, l3, f_out, s_out, tab, gt, gf, st, fbuf, sem):
    parts = [p[...] for p in (l0, l1, l2, l3)]
    top = functools.reduce(jnp.maximum, parts)
    f = -(top + jnp.log2(sum(jnp.exp2(p - top) for p in parts)))
    fbuf[...] = f * UNSCALE
    send = pltpu.make_async_copy(fbuf, f_out, sem)
    send.start()
    st[...] = jnp.zeros_like(st)
    fill_tables(tab, tp, tm)
    own = f + jnp.log2(sm[...]) - (0.5 * ALPHA) * (sp[0] * sp[0] + sp[1] * sp[1] + sp[2] * sp[2])
    zero = jnp.zeros((CL, PTS), F32)
    source_factors(gf, [sp[d] * ALPHA for d in range(3)], (*split3(own), zero))
    for c in range(CL):
        gt[c] = jnp.concatenate([gf[h, 16 * c : 16 * c + 16, :] for h in range(2)], axis=1).astype(BF16).T
    n = order[LIST - 1]

    def batch(at, size):
        scores = []
        for u in range(size):
            left = gt[(order[at + u] >> 8) & (CL - 1)]
            to = order[at + u] & (TGT - 1)
            scores.append(jnp.dot(left, target_factors(tab, to, g[0, to]), preferred_element_type=F32))
        lines = [jnp.where(at + u < n, exp_sum(scores[u]), 0.0) for u in range(size)]
        for u in range(size):
            to = pl.ds(order[at + u] & (TGT - 1), 1)
            st[to, :] = st[to, :] + lines[u]
        return 0

    whole = n // MANY
    lax.fori_loop(0, whole, lambda i, _: batch(MANY * i, MANY), 0)
    lax.fori_loop(0, (n - MANY * whole + FEW - 1) // FEW, lambda i, _: batch(MANY * whole + FEW * i, FEW), 0)
    s_out[...] = st[...].T.reshape(32, 8, TGT)
    send.wait()


def final_kernel(arrived, mass, g, out):
    total = jnp.sum(arrived[...], axis=0)
    out[...] = (g[...] - jnp.log2(1.0 + total / mass[...])) * UNSCALE


def on_device(src_pts, src_mass, tgt_pts, tgt_mass, listed, live):
    shape = jax.ShapeDtypeStruct
    params = pltpu.CompilerParams(vmem_limit_bytes=LIMIT)
    stages = [pltpu.VMEM((TGT, 16), BF16), pltpu.VMEM((16, PTS), BF16)] * BATCH
    slots = listed.transpose(1, 2, 0).reshape(SLOTS, CL)
    counts = live.transpose(1, 0)
    row, own, mass, order = pl.pallas_call(
        centroid_kernel,
        out_shape=(shape((128, 128), F32), shape((8, 256), F32), shape((8, 256), F32), shape((LIST,), I32)),
        in_specs=[SMEM, SMEM] + [VMEM] * 4,
        out_specs=(VMEM, VMEM, VMEM, SMEM),
        name="centroids",
    )(slots, counts, src_pts, src_mass, tgt_pts, tgt_mass)
    got = lax.all_to_all(row, ("src", "tgt"), split_axis=0, concat_axis=0, tiled=True)
    r, where = pl.pallas_call(
        row_kernel,
        out_shape=(shape((BLOCKS, PTS), F32), shape((128, 128), F32)),
        in_specs=[SMEM, VMEM, VMEM, VMEM],
        out_specs=(VMEM, VMEM),
        scratch_shapes=[
            pltpu.VMEM((7, TGT, PTS), F32),
            pltpu.VMEM((CL, 16, PTS), F32),
            pltpu.VMEM((2, CL * 16, 128), F32),
            pltpu.VMEM((BLOCKS, PTS), F32),
            pltpu.VMEM((BLOCKS, 128), F32),
        ]
        + stages,
        cost_estimate=pl.CostEstimate(flops=100_000_000, bytes_accessed=10_000_000, transcendentals=5_000_000),
        compiler_params=params,
        name="rows",
    )(order, src_pts, tgt_pts, tgt_mass)
    g, part = pl.pallas_call(
        coarse_kernel,
        out_shape=(shape((8, 256), F32), shape((CL, PTS), F32)),
        in_specs=[VMEM] * 4,
        out_specs=(VMEM, VMEM),
        scratch_shapes=[pltpu.VMEM((512, 256), F32), pltpu.VMEM((4, 128, 256), F32)],
        compiler_params=params,
        name="coarse",
    )(got, own, r, where)
    parts = [part] + [
        lax.ppermute(part, "tgt", [(i, (i + k) % 4) for i in range(4)]) for k in (1, 2, 3)
    ]
    fine_f, sums = pl.pallas_call(
        column_kernel,
        out_shape=(shape((CL, PTS), F32), shape((32, 8, TGT), F32)),
        in_specs=[SMEM, SMEM] + [VMEM] * 8,
        out_specs=(ANY, VMEM),
        scratch_shapes=[
            pltpu.VMEM((7, TGT, PTS), F32),
            pltpu.VMEM((CL, PTS, 16), BF16),
            pltpu.VMEM((2, CL * 16, 128), F32),
            pltpu.VMEM((TGT, PTS), F32),
            pltpu.VMEM((CL, PTS), F32),
            pltpu.SemaphoreType.DMA,
        ],
        compiler_params=params,
        name="columns",
    )(order, g, src_pts, src_mass, tgt_pts, tgt_mass, *parts)
    arrived = lax.all_to_all(sums, "src", split_axis=0, concat_axis=0, tiled=True)
    fine_g = pl.pallas_call(
        final_kernel,
        out_shape=shape((8, TGT), F32),
        in_specs=[VMEM] * 3,
        out_specs=VMEM,
        compiler_params=params,
        name="final",
    )(arrived, mass, g)
    return fine_f, fine_g


def solution(mesh):
    placed = (
        P(None, "src", None),
        P("src", None),
        P(None, None, "tgt"),
        P(None, "tgt"),
        P("src", "tgt", None),
        P("src", "tgt"),
    )
    return jax.shard_map(
        on_device,
        mesh=mesh,
        in_specs=placed,
        out_specs=(P("src", None), P("src", "tgt")),
        check_vma=False,
    )
```

```python
import functools
import math

import jax
import jax.numpy as jnp
from jax import lax
from jax.experimental import pallas as pl
from jax.experimental.pallas import tpu as pltpu
from jax.sharding import PartitionSpec as P

EPS = 0.1
NEG = -1e30
ALPHA = math.log2(math.e) / EPS
UNSCALE = EPS * math.log(2.0)
F32, BF16, I32 = jnp.float32, jnp.bfloat16, jnp.int32
CL, SLOTS, PTS, TGT = 16, 8, 256, 256
BLOCKS = CL * SLOTS
SAMPLE = 32
MARGIN = 90.0
HUGE = 1e36
BATCH = 8
MANY = 16
FEW = 4
PAD = 16
LIST = BLOCKS + 2 * PAD
LIMIT = 16 << 20
VMEM = pl.BlockSpec(memory_space=pltpu.VMEM)
SMEM = pl.BlockSpec(memory_space=pltpu.SMEM)
ANY = pl.BlockSpec(memory_space=pl.ANY)


def iota(shape, dim):
    return lax.broadcasted_iota(I32, shape, dim)


def bf16_part(value):
    big = value * 65537.0
    return big - (big - value)


def split3(value):
    high = bf16_part(value)
    rest = value - high
    mid = bf16_part(rest)
    return high, mid, rest - mid


def fill_order(order, listed, live):
    n = 0
    for c in range(CL):
        for k in range(SLOTS):
            order[n + k] = (k * CL + c) * TGT + listed[k, c]
        n = n + live[0, c]
    for u in range(PAD):
        order[n + u] = order[0]
    order[LIST - 1] = n


def centroid_kernel(sp, sm, tp, tm, row_out, own_out, slice_out):
    s, t = lax.axis_index("src"), lax.axis_index("tgt")
    mass = sm[...]
    total = jnp.sum(mass, axis=1, keepdims=True)
    inv = 1.0 / total
    cols = [jnp.sum(sp[d] * mass, axis=1, keepdims=True) * inv for d in range(3)]
    cols.append(jnp.log2(total))
    lane = iota((CL, 128), 1)
    z = jnp.zeros((CL, 128), F32)
    for q in range(4):
        z = jnp.where(lane == q, cols[q], z)
    zt = jnp.concatenate([z, jnp.zeros((128 - CL, 128), F32)], axis=0).T
    lane = iota((1, 128), 1)
    row = jnp.zeros((1, 128), F32)
    for q in range(4):
        piece = pltpu.roll(zt[q : q + 1, :], lax.rem(128 - 4 * t, 128), 1)
        row = row + pltpu.roll(jnp.where(lane < 4, piece, 0.0), 4 * q, 1)
    slice_out[...] = tm[pl.ds(pl.multiple_of(8 * s, 8), 8), :]
    weight = tm[...]
    total = jnp.sum(weight, axis=0, keepdims=True)
    inv = 1.0 / total
    rows = [jnp.sum(tp[d] * weight, axis=0, keepdims=True) * inv for d in range(3)]
    rows.append(jnp.log2(total))
    for q in range(4):
        own_out[q : q + 1, :] = rows[q]
        half = jnp.where(s >= 16, rows[q][:, 128:], rows[q][:, :128])
        piece = pltpu.roll(half, lax.rem(128 - 8 * lax.rem(s, 16), 128), 1)
        row = row + pltpu.roll(jnp.where(lane < 8, piece, 0.0), 16 + 8 * q, 1)
    row_out[...] = jnp.broadcast_to(row, row_out.shape)


def dup(table, r, piece):
    for h in range(2):
        table[h, pl.ds(r, CL, stride=16), :] = piece[:, 128 * h : 128 * h + 128]


def own_terms(tp, tm):
    return jnp.log2(tm[...]) - (0.5 * ALPHA) * (tp[0] * tp[0] + tp[1] * tp[1] + tp[2] * tp[2])


def fill_tables(tab, tp, tm):
    for d in range(3):
        y = tp[d].T
        high = bf16_part(y)
        tab[2 * d] = high
        tab[2 * d + 1] = bf16_part(y - high)
    tab[6] = own_terms(tp, tm).T


def target_factors(tab, at, extra):
    sub = iota((16, PTS), 0)
    stack = jnp.ones((16, PTS), F32)
    rows = [tab[q, pl.ds(at, 1), :] for q in (0, 0, 1, 2, 2, 3, 4, 4, 5)]
    own = tab[6, pl.ds(at, 1), :]
    for r, row in enumerate((*rows, *split3(own if extra is None else own + extra))):
        stack = jnp.where(sub == r, row, stack)
    return stack.astype(BF16)


def source_factors(table, x, own):
    for d in range(3):
        a, b, _ = split3(x[d])
        for r, piece in enumerate((a, b, a)):
            dup(table, 3 * d + r, piece)
    for r in range(9, 12):
        dup(table, r, jnp.ones((CL, PTS), F32))
    for r, piece in enumerate(own):
        dup(table, 12 + r, piece)


def exp_sum(score):
    total = jnp.zeros((8, PTS), F32)
    for o in range(0, TGT, 8):
        total = total + jnp.exp2(score[o : o + 8, :])
    return jnp.sum(total, axis=0, keepdims=True)


def row_kernel(listed, live, sp, tp, tm, r_out, l_out, order, tab, gt, gf, scol, lrow, *scratch):
    factors = [scratch[2 * u : 2 * u + 2] for u in range(BATCH)]
    fill_order(order, listed, live)
    n = order[LIST - 1]
    zero = jnp.zeros((CL, PTS), F32)
    source_factors(gf, [sp[d] * ALPHA for d in range(3)], [zero] * 4)
    for c in range(CL):
        gt[c] = jnp.concatenate([gf[h, 16 * c : 16 * c + 16, :] for h in range(2)], axis=1)
    fill_tables(tab, tp, tm)
    lrow[...] = jnp.full((BLOCKS, 128), -1.0, F32)
    scol[...] = jnp.zeros((BLOCKS, PTS), F32)
    sub = iota((16, PTS), 0)

    def prepare(i, lhs, rhs):
        b, at = order[i] >> 8, order[i] & (TGT - 1)
        left = target_factors(tab, at, None).T
        right = gt[b & (CL - 1)]
        seen = jnp.dot(left[:SAMPLE, :], right.astype(BF16), preferred_element_type=F32)
        shift = jnp.max(seen, axis=0, keepdims=True) + MARGIN
        for r, piece in enumerate(split3(-shift)):
            right = jnp.where(sub == 12 + r, piece, right)
        lhs[...] = left
        rhs[...] = right.astype(BF16)
        r_out[pl.ds(b, 1), :] = shift
        lrow[pl.ds(b, 1), :] = jnp.broadcast_to(at.astype(F32), (1, 128))

    for u in range(BATCH):
        prepare(u, *factors[u])

    def batch(i, _):
        at = BATCH * i
        scores = [jnp.dot(lhs[...], rhs[...], preferred_element_type=F32) for lhs, rhs in factors]
        for u in range(BATCH):
            prepare(at + BATCH + u, *factors[u])
        for u in range(BATCH):
            scol[pl.ds(order[at + u] >> 8, 1), :] = exp_sum(scores[u])
        return 0

    lax.fori_loop(0, (n + BATCH - 1) // BATCH, batch, 0)

    @pl.when(jnp.max(scol[...]) > HUGE)
    def _():
        def exact(i, _):
            b = order[i] >> 8
            left = target_factors(tab, order[i] & (TGT - 1), None).T
            v = jnp.dot(left, gt[b & (CL - 1)].astype(BF16), preferred_element_type=F32)
            top = jnp.max(v, axis=0, keepdims=True)
            r_out[pl.ds(b, 1), :] = top
            scol[pl.ds(b, 1), :] = jnp.sum(jnp.exp2(v - top), axis=0, keepdims=True)
            return 0

        lax.fori_loop(0, n, exact, 0)

    xn = (-0.5 * ALPHA) * (sp[0] * sp[0] + sp[1] * sp[1] + sp[2] * sp[2])
    r = r_out[...] + jnp.log2(scol[...])
    r = (r.reshape(SLOTS, CL, PTS) + xn[None]).reshape(BLOCKS, PTS)
    r_out[...] = jnp.where(lrow[:, 0:1] >= 0.0, r, NEG)
    l_out[...] = lrow[...]


def coarse_kernel(got, own, r_in, l_in, g_out, l_out, terms, scores):
    table = got[...]
    turned = table.T
    high = bf16_part(ALPHA * table)
    mid = bf16_part(ALPHA * table - high)
    lane = iota((256, 64), 1)
    r = lane & 15
    d = (r >= 3).astype(I32) + (r >= 6).astype(I32)
    wanted = 4 * d + (lane >> 4) + jnp.where(r - 3 * d == 1, 128, 0)
    pick = jnp.where((r < 9) & (iota((256, 64), 0) == wanted), 1.0, 0.0).astype(BF16)
    left = jnp.dot(jnp.concatenate([high, mid], axis=1).astype(BF16), pick, preferred_element_type=F32)
    r = iota((128, 64), 1) & 15
    left = jnp.where((r >= 9) & (r < 12), 1.0, left).astype(BF16)

    def target_rows(y, mass):
        rows = []
        for v in y:
            a = bf16_part(v)
            rows += [a, a, bf16_part(v - a)]
        return rows + list(split3(mass - (0.5 * ALPHA) * (y[0] * y[0] + y[1] * y[1] + y[2] * y[2])))

    def stacked(rows, at):
        stack = jnp.zeros((16, rows[0].shape[1]), F32)
        sub = iota(stack.shape, 0)
        for q, row in enumerate(rows):
            stack = jnp.where(sub == q, row[at : at + 1, :], stack)
        return stack.astype(BF16)

    tiles = target_rows([turned[16 + 8 * d : 24 + 8 * d, :] for d in range(3)], turned[40:48, :])
    rights = [jnp.concatenate([stacked(tiles, 2 * p), stacked(tiles, 2 * p + 1)], axis=1) for p in range(4)]
    mine = stacked(target_rows([own[d : d + 1, :] for d in range(3)], own[3:4, :]), 0)
    zero = jnp.zeros((16, TGT), BF16)
    for ci in range(4):

        def score(right):
            placed = jnp.concatenate([right if k == ci else zero for k in range(4)], axis=0)
            return jnp.dot(left, placed, preferred_element_type=F32)

        peak = None
        for p, right in enumerate(rights):
            v = score(right)
            scores[p] = v
            peak = v if peak is None else jnp.maximum(peak, v)
        terms[128 * ci : 128 * ci + 128, :] = score(mine)
        peak = jnp.max(jnp.maximum(peak[:, :128], peak[:, 128:]), axis=1, keepdims=True)
        total = jnp.exp2(scores[0] - peak)
        for p in range(1, 4):
            total = total + jnp.exp2(scores[p] - peak)
        total = jnp.sum(total[:, :128] + total[:, 128:], axis=1, keepdims=True)
        terms[128 * ci : 128 * ci + 128, :] += table[:, 12 + ci : 13 + ci] - (peak + jnp.log2(total))
    top_g = jnp.full((8, TGT), NEG, F32)
    for i in range(0, 512, 8):
        top_g = jnp.maximum(top_g, terms[i : i + 8, :])
    top = jnp.max(top_g, axis=0, keepdims=True)
    total = jnp.zeros((8, TGT), F32)
    for i in range(0, 512, 8):
        total = total + jnp.exp2(terms[i : i + 8, :] - top)
    g = own[3:4, :] - top - jnp.log2(jnp.sum(total, axis=0, keepdims=True))
    g_out[...] = jnp.broadcast_to(g, g_out.shape)
    at = l_in[...]
    lane = iota((128, 128), 1).astype(F32)
    hit = jnp.where(at == lane, g[:, :128], 0.0) + jnp.where(at == lane + 128.0, g[:, 128:], 0.0)
    picked = jnp.sum(hit, axis=1, keepdims=True)
    r = (r_in[...] + picked).reshape(SLOTS, CL, PTS)
    top = jnp.max(r, axis=0)
    l_out[...] = top + jnp.log2(jnp.sum(jnp.exp2(r - top[None]), axis=0))


def column_kernel(order, g, sp, sm, tp, tm, l0, l1, l2, l3, f_out, s_out, tab, gt, gf, st, fbuf, sem):
    parts = [p[...] for p in (l0, l1, l2, l3)]
    top = functools.reduce(jnp.maximum, parts)
    f = -(top + jnp.log2(sum(jnp.exp2(p - top) for p in parts)))
    fbuf[...] = f * UNSCALE
    send = pltpu.make_async_copy(fbuf, f_out, sem)
    send.start()
    st[...] = jnp.zeros_like(st)
    fill_tables(tab, tp, tm)
    own = f + jnp.log2(sm[...]) - (0.5 * ALPHA) * (sp[0] * sp[0] + sp[1] * sp[1] + sp[2] * sp[2])
    zero = jnp.zeros((CL, PTS), F32)
    source_factors(gf, [sp[d] * ALPHA for d in range(3)], (*split3(own), zero))
    for c in range(CL):
        gt[c] = jnp.concatenate([gf[h, 16 * c : 16 * c + 16, :] for h in range(2)], axis=1).astype(BF16).T
    n = order[LIST - 1]

    def batch(at, size):
        scores = []
        for u in range(size):
            left = gt[(order[at + u] >> 8) & (CL - 1)]
            to = order[at + u] & (TGT - 1)
            scores.append(jnp.dot(left, target_factors(tab, to, g[0, to]), preferred_element_type=F32))
        lines = [jnp.where(at + u < n, exp_sum(scores[u]), 0.0) for u in range(size)]
        for u in range(size):
            to = pl.ds(order[at + u] & (TGT - 1), 1)
            st[to, :] = st[to, :] + lines[u]
        return 0

    whole = n // MANY
    lax.fori_loop(0, whole, lambda i, _: batch(MANY * i, MANY), 0)
    lax.fori_loop(0, (n - MANY * whole + FEW - 1) // FEW, lambda i, _: batch(MANY * whole + FEW * i, FEW), 0)
    s_out[...] = st[...].T.reshape(32, 8, TGT)
    send.wait()


def final_kernel(arrived, mass, g, out):
    total = jnp.sum(arrived[...], axis=0)
    out[...] = (g[...] - jnp.log2(1.0 + total / mass[...])) * UNSCALE


def on_device(src_pts, src_mass, tgt_pts, tgt_mass, listed, live):
    shape = jax.ShapeDtypeStruct
    params = pltpu.CompilerParams(vmem_limit_bytes=LIMIT)
    stages = [pltpu.VMEM((TGT, 16), BF16), pltpu.VMEM((16, PTS), BF16)] * BATCH
    slots = listed.transpose(1, 2, 0).reshape(SLOTS, CL)
    counts = live.transpose(1, 0)
    row, own, mass = pl.pallas_call(
        centroid_kernel,
        out_shape=(shape((128, 128), F32), shape((8, 256), F32), shape((8, 256), F32)),
        in_specs=[VMEM] * 4,
        out_specs=(VMEM, VMEM, VMEM),
        name="centroids",
    )(src_pts, src_mass, tgt_pts, tgt_mass)
    got = lax.all_to_all(row, ("src", "tgt"), split_axis=0, concat_axis=0, tiled=True)
    r, where, order = pl.pallas_call(
        row_kernel,
        out_shape=(shape((BLOCKS, PTS), F32), shape((128, 128), F32), shape((LIST,), I32)),
        in_specs=[SMEM, SMEM, VMEM, VMEM, VMEM],
        out_specs=(VMEM, VMEM, SMEM),
        scratch_shapes=[
            pltpu.VMEM((7, TGT, PTS), F32),
            pltpu.VMEM((CL, 16, PTS), F32),
            pltpu.VMEM((2, CL * 16, 128), F32),
            pltpu.VMEM((BLOCKS, PTS), F32),
            pltpu.VMEM((BLOCKS, 128), F32),
        ]
        + stages,
        cost_estimate=pl.CostEstimate(flops=100_000_000, bytes_accessed=10_000_000, transcendentals=5_000_000),
        compiler_params=params,
        name="rows",
    )(slots, counts, src_pts, tgt_pts, tgt_mass)
    g, part = pl.pallas_call(
        coarse_kernel,
        out_shape=(shape((8, 256), F32), shape((CL, PTS), F32)),
        in_specs=[VMEM] * 4,
        out_specs=(VMEM, VMEM),
        scratch_shapes=[pltpu.VMEM((512, 256), F32), pltpu.VMEM((4, 128, 256), F32)],
        compiler_params=params,
        name="coarse",
    )(got, own, r, where)
    parts = [part] + [
        lax.ppermute(part, "tgt", [(i, (i + k) % 4) for i in range(4)]) for k in (1, 2, 3)
    ]
    fine_f, sums = pl.pallas_call(
        column_kernel,
        out_shape=(shape((CL, PTS), F32), shape((32, 8, TGT), F32)),
        in_specs=[SMEM, SMEM] + [VMEM] * 8,
        out_specs=(ANY, VMEM),
        scratch_shapes=[
            pltpu.VMEM((7, TGT, PTS), F32),
            pltpu.VMEM((CL, PTS, 16), BF16),
            pltpu.VMEM((2, CL * 16, 128), F32),
            pltpu.VMEM((TGT, PTS), F32),
            pltpu.VMEM((CL, PTS), F32),
            pltpu.SemaphoreType.DMA,
        ],
        compiler_params=params,
        name="columns",
    )(order, g, src_pts, src_mass, tgt_pts, tgt_mass, *parts)
    arrived = lax.all_to_all(sums, "src", split_axis=0, concat_axis=0, tiled=True)
    fine_g = pl.pallas_call(
        final_kernel,
        out_shape=shape((8, TGT), F32),
        in_specs=[VMEM] * 3,
        out_specs=VMEM,
        compiler_params=params,
        name="final",
    )(arrived, mass, g)
    return fine_f, fine_g


def solution(mesh):
    placed = (
        P(None, "src", None),
        P("src", None),
        P(None, None, "tgt"),
        P(None, "tgt"),
        P("src", "tgt", None),
        P("src", "tgt"),
    )
    return jax.shard_map(
        on_device,
        mesh=mesh,
        in_specs=placed,
        out_specs=(P("src", None), P("src", "tgt")),
        check_vma=False,
    )
```

```python
import functools
import math

import jax
import jax.numpy as jnp
from jax import lax
from jax.experimental import pallas as pl
from jax.experimental.pallas import tpu as pltpu
from jax.sharding import PartitionSpec as P

EPS = 0.1
NEG = -1e30
ALPHA = math.log2(math.e) / EPS
UNSCALE = EPS * math.log(2.0)
F32, BF16, I32 = jnp.float32, jnp.bfloat16, jnp.int32
CL, SLOTS, PTS, TGT = 16, 8, 256, 256
BLOCKS = CL * SLOTS
AHEAD = 4
MANY = 16
FEW = 4
PAD = 16
LIST = BLOCKS + 2 * PAD
LIMIT = 16 << 20
VMEM = pl.BlockSpec(memory_space=pltpu.VMEM)
SMEM = pl.BlockSpec(memory_space=pltpu.SMEM)
ANY = pl.BlockSpec(memory_space=pl.ANY)


def iota(shape, dim):
    return lax.broadcasted_iota(I32, shape, dim)


def bf16_part(value):
    big = value * 65537.0
    return big - (big - value)


def split3(value):
    high = bf16_part(value)
    rest = value - high
    mid = bf16_part(rest)
    return high, mid, rest - mid


def fill_order(order, listed, live):
    n = 0
    for c in range(CL):
        for k in range(SLOTS):
            order[n + k] = (k * CL + c) * TGT + listed[k, c]
        n = n + live[0, c]
    for u in range(PAD):
        order[n + u] = order[0]
    order[LIST - 1] = n


def centroid_kernel(sp, sm, tp, tm, row_out, own_out, slice_out):
    s, t = lax.axis_index("src"), lax.axis_index("tgt")
    mass = sm[...]
    total = jnp.sum(mass, axis=1, keepdims=True)
    inv = 1.0 / total
    cols = [jnp.sum(sp[d] * mass, axis=1, keepdims=True) * inv for d in range(3)]
    cols.append(jnp.log2(total))
    lane = iota((CL, 128), 1)
    z = jnp.zeros((CL, 128), F32)
    for q in range(4):
        z = jnp.where(lane == q, cols[q], z)
    zt = jnp.concatenate([z, jnp.zeros((128 - CL, 128), F32)], axis=0).T
    lane = iota((1, 128), 1)
    row = jnp.zeros((1, 128), F32)
    for q in range(4):
        piece = pltpu.roll(zt[q : q + 1, :], lax.rem(128 - 4 * t, 128), 1)
        row = row + pltpu.roll(jnp.where(lane < 4, piece, 0.0), 4 * q, 1)
    slice_out[...] = tm[pl.ds(pl.multiple_of(8 * s, 8), 8), :]
    weight = tm[...]
    total = jnp.sum(weight, axis=0, keepdims=True)
    inv = 1.0 / total
    rows = [jnp.sum(tp[d] * weight, axis=0, keepdims=True) * inv for d in range(3)]
    rows.append(jnp.log2(total))
    for q in range(4):
        own_out[q : q + 1, :] = rows[q]
        half = jnp.where(s >= 16, rows[q][:, 128:], rows[q][:, :128])
        piece = pltpu.roll(half, lax.rem(128 - 8 * lax.rem(s, 16), 128), 1)
        row = row + pltpu.roll(jnp.where(lane < 8, piece, 0.0), 16 + 8 * q, 1)
    row_out[...] = jnp.broadcast_to(row, row_out.shape)


def dup(table, r, piece):
    for h in range(2):
        table[h, pl.ds(r, CL, stride=16), :] = piece[:, 128 * h : 128 * h + 128]


def own_terms(tp, tm):
    return jnp.log2(tm[...]) - (0.5 * ALPHA) * (tp[0] * tp[0] + tp[1] * tp[1] + tp[2] * tp[2])


def fill_tables(tab, tp, tm):
    for d in range(3):
        y = tp[d].T
        high = bf16_part(y)
        tab[2 * d] = high
        tab[2 * d + 1] = bf16_part(y - high)
    tab[6] = own_terms(tp, tm).T


def target_factors(tab, at, extra):
    sub = iota((16, PTS), 0)
    stack = jnp.ones((16, PTS), F32)
    rows = [tab[q, pl.ds(at, 1), :] for q in (0, 0, 1, 2, 2, 3, 4, 4, 5)]
    own = tab[6, pl.ds(at, 1), :]
    for r, row in enumerate((*rows, *split3(own if extra is None else own + extra))):
        stack = jnp.where(sub == r, row, stack)
    return stack.astype(BF16)


def source_factors(table, x, own):
    for d in range(3):
        a, b, _ = split3(x[d])
        for r, piece in enumerate((a, b, a)):
            dup(table, 3 * d + r, piece)
    for r in range(9, 12):
        dup(table, r, jnp.ones((CL, PTS), F32))
    for r, piece in enumerate(own):
        dup(table, 12 + r, piece)


def exp_sum(score):
    total = jnp.zeros((8, PTS), F32)
    for o in range(0, TGT, 8):
        total = total + jnp.exp2(score[o : o + 8, :])
    return jnp.sum(total, axis=0, keepdims=True)


def row_kernel(listed, live, sp, tp, tm, r_out, l_out, order, tab, gt, gf, scol, lrow, *sets):
    sets = [sets[3 * u : 3 * u + 3] for u in range(AHEAD)]
    fill_order(order, listed, live)
    n = order[LIST - 1]
    zero = jnp.zeros((CL, PTS), F32)
    source_factors(gf, [sp[d] * ALPHA for d in range(3)], [zero] * 4)
    for c in range(CL):
        gt[c] = jnp.concatenate([gf[h, 16 * c : 16 * c + 16, :] for h in range(2)], axis=1).astype(BF16)
    fill_tables(tab, tp, tm)
    lrow[...] = jnp.full((BLOCKS, 128), -1.0, F32)

    def prepare(i, lhs):
        at = order[i] & (TGT - 1)
        lhs[...] = target_factors(tab, at, None).T
        lrow[pl.ds(order[i] >> 8, 1), :] = jnp.broadcast_to(at.astype(F32), (1, 128))

    for u in range(AHEAD):
        prepare(u, sets[u][0])

    def batch(i, _):
        at = AHEAD * i
        v = [jnp.dot(sets[u][0][...], gt[(order[at + u] >> 8) & (CL - 1)], preferred_element_type=F32) for u in range(AHEAD)]
        for u in range(AHEAD):
            prepare(at + AHEAD + u, sets[u][0])
        for u in range(AHEAD):
            lhs, score, tops = sets[u]
            top_old = tops[...]
            total = jnp.zeros((8, PTS), F32)
            top = jnp.full((8, PTS), NEG, F32)
            for j in range(0, TGT, 8):
                total = total + jnp.exp2(score[j : j + 8, :] - top_old)
                score[j : j + 8, :] = v[u][j : j + 8, :]
                top = jnp.maximum(top, v[u][j : j + 8, :])
            tops[...] = jnp.broadcast_to(jnp.max(top, axis=0, keepdims=True), (8, PTS))
            old = order[jnp.maximum(at - AHEAD + u, 0)] >> 8
            r_out[pl.ds(old, 1), :] = top_old[0:1, :]
            scol[pl.ds(old, 1), :] = jnp.sum(total, axis=0, keepdims=True)
        return 0

    lax.fori_loop(0, (n + AHEAD - 1) // AHEAD + 1, batch, 0)
    xn = (-0.5 * ALPHA) * (sp[0] * sp[0] + sp[1] * sp[1] + sp[2] * sp[2])
    r = r_out[...] + jnp.log2(scol[...])
    r = (r.reshape(SLOTS, CL, PTS) + xn[None]).reshape(BLOCKS, PTS)
    r_out[...] = jnp.where(lrow[:, 0:1] >= 0.0, r, NEG)
    l_out[...] = lrow[...]


def coarse_kernel(got, own, r_in, l_in, g_out, l_out, terms, scores):
    table = got[...]
    turned = table.T
    high = bf16_part(ALPHA * table)
    mid = bf16_part(ALPHA * table - high)
    lane = iota((256, 64), 1)
    r = lane & 15
    d = (r >= 3).astype(I32) + (r >= 6).astype(I32)
    wanted = 4 * d + (lane >> 4) + jnp.where(r - 3 * d == 1, 128, 0)
    pick = jnp.where((r < 9) & (iota((256, 64), 0) == wanted), 1.0, 0.0).astype(BF16)
    left = jnp.dot(jnp.concatenate([high, mid], axis=1).astype(BF16), pick, preferred_element_type=F32)
    r = iota((128, 64), 1) & 15
    left = jnp.where((r >= 9) & (r < 12), 1.0, left).astype(BF16)

    def target_rows(y, mass):
        rows = []
        for v in y:
            a = bf16_part(v)
            rows += [a, a, bf16_part(v - a)]
        return rows + list(split3(mass - (0.5 * ALPHA) * (y[0] * y[0] + y[1] * y[1] + y[2] * y[2])))

    def stacked(rows, at):
        stack = jnp.zeros((16, rows[0].shape[1]), F32)
        sub = iota(stack.shape, 0)
        for q, row in enumerate(rows):
            stack = jnp.where(sub == q, row[at : at + 1, :], stack)
        return stack.astype(BF16)

    tiles = target_rows([turned[16 + 8 * d : 24 + 8 * d, :] for d in range(3)], turned[40:48, :])
    rights = [jnp.concatenate([stacked(tiles, 2 * p), stacked(tiles, 2 * p + 1)], axis=1) for p in range(4)]
    mine = stacked(target_rows([own[d : d + 1, :] for d in range(3)], own[3:4, :]), 0)
    zero = jnp.zeros((16, TGT), BF16)
    for ci in range(4):

        def score(right):
            placed = jnp.concatenate([right if k == ci else zero for k in range(4)], axis=0)
            return jnp.dot(left, placed, preferred_element_type=F32)

        peak = None
        for p, right in enumerate(rights):
            v = score(right)
            scores[p] = v
            peak = v if peak is None else jnp.maximum(peak, v)
        terms[128 * ci : 128 * ci + 128, :] = score(mine)
        peak = jnp.max(jnp.maximum(peak[:, :128], peak[:, 128:]), axis=1, keepdims=True)
        total = jnp.exp2(scores[0] - peak)
        for p in range(1, 4):
            total = total + jnp.exp2(scores[p] - peak)
        total = jnp.sum(total[:, :128] + total[:, 128:], axis=1, keepdims=True)
        terms[128 * ci : 128 * ci + 128, :] += table[:, 12 + ci : 13 + ci] - (peak + jnp.log2(total))
    top_g = jnp.full((8, TGT), NEG, F32)
    for i in range(0, 512, 8):
        top_g = jnp.maximum(top_g, terms[i : i + 8, :])
    top = jnp.max(top_g, axis=0, keepdims=True)
    total = jnp.zeros((8, TGT), F32)
    for i in range(0, 512, 8):
        total = total + jnp.exp2(terms[i : i + 8, :] - top)
    g = own[3:4, :] - top - jnp.log2(jnp.sum(total, axis=0, keepdims=True))
    g_out[...] = jnp.broadcast_to(g, g_out.shape)
    at = l_in[...]
    lane = iota((128, 128), 1).astype(F32)
    hit = jnp.where(at == lane, g[:, :128], 0.0) + jnp.where(at == lane + 128.0, g[:, 128:], 0.0)
    picked = jnp.sum(hit, axis=1, keepdims=True)
    r = (r_in[...] + picked).reshape(SLOTS, CL, PTS)
    top = jnp.max(r, axis=0)
    l_out[...] = top + jnp.log2(jnp.sum(jnp.exp2(r - top[None]), axis=0))


def column_kernel(order, g, sp, sm, tp, tm, l0, l1, l2, l3, f_out, s_out, tab, gt, gf, st, fbuf, sem):
    parts = [p[...] for p in (l0, l1, l2, l3)]
    top = functools.reduce(jnp.maximum, parts)
    f = -(top + jnp.log2(sum(jnp.exp2(p - top) for p in parts)))
    fbuf[...] = f * UNSCALE
    send = pltpu.make_async_copy(fbuf, f_out, sem)
    send.start()
    st[...] = jnp.zeros_like(st)
    fill_tables(tab, tp, tm)
    own = f + jnp.log2(sm[...]) - (0.5 * ALPHA) * (sp[0] * sp[0] + sp[1] * sp[1] + sp[2] * sp[2])
    zero = jnp.zeros((CL, PTS), F32)
    source_factors(gf, [sp[d] * ALPHA for d in range(3)], (*split3(own), zero))
    for c in range(CL):
        gt[c] = jnp.concatenate([gf[h, 16 * c : 16 * c + 16, :] for h in range(2)], axis=1).astype(BF16).T
    n = order[LIST - 1]

    def batch(at, size):
        scores = []
        for u in range(size):
            left = gt[(order[at + u] >> 8) & (CL - 1)]
            to = order[at + u] & (TGT - 1)
            scores.append(jnp.dot(left, target_factors(tab, to, g[0, to]), preferred_element_type=F32))
        lines = [jnp.where(at + u < n, exp_sum(scores[u]), 0.0) for u in range(size)]
        for u in range(size):
            to = pl.ds(order[at + u] & (TGT - 1), 1)
            st[to, :] = st[to, :] + lines[u]
        return 0

    whole = n // MANY
    lax.fori_loop(0, whole, lambda i, _: batch(MANY * i, MANY), 0)
    lax.fori_loop(0, (n - MANY * whole + FEW - 1) // FEW, lambda i, _: batch(MANY * whole + FEW * i, FEW), 0)
    s_out[...] = st[...].T.reshape(32, 8, TGT)
    send.wait()


def final_kernel(arrived, mass, g, out):
    total = jnp.sum(arrived[...], axis=0)
    out[...] = (g[...] - jnp.log2(1.0 + total / mass[...])) * UNSCALE


def on_device(src_pts, src_mass, tgt_pts, tgt_mass, listed, live):
    shape = jax.ShapeDtypeStruct
    params = pltpu.CompilerParams(vmem_limit_bytes=LIMIT)
    stages = [pltpu.VMEM((TGT, 16), BF16), pltpu.VMEM((TGT, PTS), F32), pltpu.VMEM((8, PTS), F32)] * AHEAD
    slots = listed.transpose(1, 2, 0).reshape(SLOTS, CL)
    counts = live.transpose(1, 0)
    row, own, mass = pl.pallas_call(
        centroid_kernel,
        out_shape=(shape((128, 128), F32), shape((8, 256), F32), shape((8, 256), F32)),
        in_specs=[VMEM] * 4,
        out_specs=(VMEM, VMEM, VMEM),
        name="centroids",
    )(src_pts, src_mass, tgt_pts, tgt_mass)
    got = lax.all_to_all(row, ("src", "tgt"), split_axis=0, concat_axis=0, tiled=True)
    r, where, order = pl.pallas_call(
        row_kernel,
        out_shape=(shape((BLOCKS, PTS), F32), shape((128, 128), F32), shape((LIST,), I32)),
        in_specs=[SMEM, SMEM, VMEM, VMEM, VMEM],
        out_specs=(VMEM, VMEM, SMEM),
        scratch_shapes=[
            pltpu.VMEM((7, TGT, PTS), F32),
            pltpu.VMEM((CL, 16, PTS), BF16),
            pltpu.VMEM((2, CL * 16, 128), F32),
            pltpu.VMEM((BLOCKS, PTS), F32),
            pltpu.VMEM((BLOCKS, 128), F32),
        ]
        + stages,
        cost_estimate=pl.CostEstimate(flops=100_000_000, bytes_accessed=10_000_000, transcendentals=5_000_000),
        compiler_params=params,
        name="rows",
    )(slots, counts, src_pts, tgt_pts, tgt_mass)
    g, part = pl.pallas_call(
        coarse_kernel,
        out_shape=(shape((8, 256), F32), shape((CL, PTS), F32)),
        in_specs=[VMEM] * 4,
        out_specs=(VMEM, VMEM),
        scratch_shapes=[pltpu.VMEM((512, 256), F32), pltpu.VMEM((4, 128, 256), F32)],
        compiler_params=params,
        name="coarse",
    )(got, own, r, where)
    parts = [part] + [
        lax.ppermute(part, "tgt", [(i, (i + k) % 4) for i in range(4)]) for k in (1, 2, 3)
    ]
    fine_f, sums = pl.pallas_call(
        column_kernel,
        out_shape=(shape((CL, PTS), F32), shape((32, 8, TGT), F32)),
        in_specs=[SMEM, SMEM] + [VMEM] * 8,
        out_specs=(ANY, VMEM),
        scratch_shapes=[
            pltpu.VMEM((7, TGT, PTS), F32),
            pltpu.VMEM((CL, PTS, 16), BF16),
            pltpu.VMEM((2, CL * 16, 128), F32),
            pltpu.VMEM((TGT, PTS), F32),
            pltpu.VMEM((CL, PTS), F32),
            pltpu.SemaphoreType.DMA,
        ],
        compiler_params=params,
        name="columns",
    )(order, g, src_pts, src_mass, tgt_pts, tgt_mass, *parts)
    arrived = lax.all_to_all(sums, "src", split_axis=0, concat_axis=0, tiled=True)
    fine_g = pl.pallas_call(
        final_kernel,
        out_shape=shape((8, TGT), F32),
        in_specs=[VMEM] * 3,
        out_specs=VMEM,
        compiler_params=params,
        name="final",
    )(arrived, mass, g)
    return fine_f, fine_g


def solution(mesh):
    placed = (
        P(None, "src", None),
        P("src", None),
        P(None, None, "tgt"),
        P(None, "tgt"),
        P("src", "tgt", None),
        P("src", "tgt"),
    )
    return jax.shard_map(
        on_device,
        mesh=mesh,
        in_specs=placed,
        out_specs=(P("src", None), P("src", "tgt")),
        check_vma=False,
    )
```

```python
import functools
import math

import jax
import jax.numpy as jnp
from jax import lax
from jax.experimental import pallas as pl
from jax.experimental.pallas import tpu as pltpu
from jax.sharding import PartitionSpec as P

EPS = 0.1
NEG = -1e30
ALPHA = math.log2(math.e) / EPS
UNSCALE = EPS * math.log(2.0)
F32, BF16, I32 = jnp.float32, jnp.bfloat16, jnp.int32
CL, SLOTS, PTS, TGT = 16, 8, 256, 256
BLOCKS = CL * SLOTS
AHEAD = 4
MANY = 16
FEW = 4
PAD = 16
LIST = BLOCKS + 2 * PAD
LIMIT = 16 << 20
VMEM = pl.BlockSpec(memory_space=pltpu.VMEM)
SMEM = pl.BlockSpec(memory_space=pltpu.SMEM)
ANY = pl.BlockSpec(memory_space=pl.ANY)


def iota(shape, dim):
    return lax.broadcasted_iota(I32, shape, dim)


def bf16_part(value):
    big = value * 65537.0
    return big - (big - value)


def split3(value):
    high = bf16_part(value)
    rest = value - high
    mid = bf16_part(rest)
    return high, mid, rest - mid


def fill_order(order, listed, live):
    n = 0
    for c in range(CL):
        for k in range(SLOTS):
            order[n + k] = (k * CL + c) * TGT + listed[k, c]
        n = n + live[0, c]
    for u in range(PAD):
        order[n + u] = order[0]
    order[LIST - 1] = n


def centroid_kernel(sp, sm, tp, tm, row_out, own_out, slice_out):
    s, t = lax.axis_index("src"), lax.axis_index("tgt")
    mass = sm[...]
    total = jnp.sum(mass, axis=1, keepdims=True)
    inv = 1.0 / total
    cols = [jnp.sum(sp[d] * mass, axis=1, keepdims=True) * inv for d in range(3)]
    cols.append(jnp.log2(total))
    lane = iota((CL, 128), 1)
    z = jnp.zeros((CL, 128), F32)
    for q in range(4):
        z = jnp.where(lane == q, cols[q], z)
    zt = jnp.concatenate([z, jnp.zeros((128 - CL, 128), F32)], axis=0).T
    lane = iota((1, 128), 1)
    row = jnp.zeros((1, 128), F32)
    for q in range(4):
        piece = pltpu.roll(zt[q : q + 1, :], lax.rem(128 - 4 * t, 128), 1)
        row = row + pltpu.roll(jnp.where(lane < 4, piece, 0.0), 4 * q, 1)
    slice_out[...] = tm[pl.ds(pl.multiple_of(8 * s, 8), 8), :]
    weight = tm[...]
    total = jnp.sum(weight, axis=0, keepdims=True)
    inv = 1.0 / total
    rows = [jnp.sum(tp[d] * weight, axis=0, keepdims=True) * inv for d in range(3)]
    rows.append(jnp.log2(total))
    for q in range(4):
        own_out[q : q + 1, :] = rows[q]
        half = jnp.where(s >= 16, rows[q][:, 128:], rows[q][:, :128])
        piece = pltpu.roll(half, lax.rem(128 - 8 * lax.rem(s, 16), 128), 1)
        row = row + pltpu.roll(jnp.where(lane < 8, piece, 0.0), 16 + 8 * q, 1)
    row_out[...] = jnp.broadcast_to(row, row_out.shape)


def dup(table, r, piece):
    for h in range(2):
        table[h, pl.ds(r, CL, stride=16), :] = piece[:, 128 * h : 128 * h + 128]


def own_terms(tp, tm):
    return jnp.log2(tm[...]) - (0.5 * ALPHA) * (tp[0] * tp[0] + tp[1] * tp[1] + tp[2] * tp[2])


def fill_tables(tab, tp, tm):
    for d in range(3):
        y = tp[d].T
        high = bf16_part(y)
        tab[2 * d] = high
        tab[2 * d + 1] = bf16_part(y - high)
    tab[6] = own_terms(tp, tm).T


def target_factors(tab, at, extra):
    sub = iota((16, PTS), 0)
    stack = jnp.ones((16, PTS), F32)
    rows = [tab[q, pl.ds(at, 1), :] for q in (0, 0, 1, 2, 2, 3, 4, 4, 5)]
    own = tab[6, pl.ds(at, 1), :]
    for r, row in enumerate((*rows, *split3(own if extra is None else own + extra))):
        stack = jnp.where(sub == r, row, stack)
    return stack.astype(BF16)


def source_factors(table, x, own):
    for d in range(3):
        a, b, _ = split3(x[d])
        for r, piece in enumerate((a, b, a)):
            dup(table, 3 * d + r, piece)
    for r in range(9, 12):
        dup(table, r, jnp.ones((CL, PTS), F32))
    for r, piece in enumerate(own):
        dup(table, 12 + r, piece)


def exp_sum(score):
    total = jnp.zeros((8, PTS), F32)
    for o in range(0, TGT, 8):
        total = total + jnp.exp2(score[o : o + 8, :])
    return jnp.sum(total, axis=0, keepdims=True)


def row_kernel(listed, live, sp, tp, tm, r_out, l_out, order, tab, gt, gf, scol, lrow, *sets):
    sets = [sets[3 * u : 3 * u + 3] for u in range(AHEAD)]
    fill_order(order, listed, live)
    n = order[LIST - 1]
    zero = jnp.zeros((CL, PTS), F32)
    source_factors(gf, [sp[d] * ALPHA for d in range(3)], [zero] * 4)
    for c in range(CL):
        gt[c] = jnp.concatenate([gf[h, 16 * c : 16 * c + 16, :] for h in range(2)], axis=1).astype(BF16)
    fill_tables(tab, tp, tm)
    lrow[...] = jnp.full((BLOCKS, 128), -1.0, F32)

    def prepare(i, lhs):
        at = order[i] & (TGT - 1)
        lhs[...] = target_factors(tab, at, None).T
        lrow[pl.ds(order[i] >> 8, 1), :] = jnp.broadcast_to(at.astype(F32), (1, 128))

    for u in range(AHEAD):
        prepare(u, sets[u][0])

    def batch(i, _):
        at = AHEAD * i
        v = [jnp.dot(sets[u][0][...], gt[(order[at + u] >> 8) & (CL - 1)], preferred_element_type=F32) for u in range(AHEAD)]
        for u in range(AHEAD):
            prepare(at + AHEAD + u, sets[u][0])
        for u in range(AHEAD):
            lhs, score, tops = sets[u]
            top_old = tops[...]
            total = jnp.zeros((8, PTS), F32)
            top = jnp.full((8, PTS), NEG, F32)
            for j in range(0, TGT, 8):
                total = total + jnp.exp2(score[j : j + 8, :] - top_old)
                score[j : j + 8, :] = v[u][j : j + 8, :]
                top = jnp.maximum(top, v[u][j : j + 8, :])
            tops[...] = jnp.broadcast_to(jnp.max(top, axis=0, keepdims=True), (8, PTS))
            old = order[jnp.maximum(at - AHEAD + u, 0)] >> 8
            r_out[pl.ds(old, 1), :] = top_old[0:1, :]
            scol[pl.ds(old, 1), :] = jnp.sum(total, axis=0, keepdims=True)
        return 0

    lax.fori_loop(0, (n + AHEAD - 1) // AHEAD + 1, batch, 0)
    xn = (-0.5 * ALPHA) * (sp[0] * sp[0] + sp[1] * sp[1] + sp[2] * sp[2])
    r = r_out[...] + jnp.log2(scol[...])
    r = (r.reshape(SLOTS, CL, PTS) + xn[None]).reshape(BLOCKS, PTS)
    r_out[...] = jnp.where(lrow[:, 0:1] >= 0.0, r, NEG)
    l_out[...] = lrow[...]


def coarse_kernel(got, own, r_in, l_in, g_out, l_out, terms, scores):
    table = got[...]
    turned = table.T
    high = bf16_part(ALPHA * table)
    mid = bf16_part(ALPHA * table - high)
    lane = iota((256, 128), 1)
    r = lane & 15
    d = (r >= 3).astype(I32) + (r >= 6).astype(I32)
    wanted = 4 * d + (lane >> 4) + jnp.where(r - 3 * d == 1, 128, 0)
    pick = jnp.where((r < 9) & (lane < 64) & (iota((256, 128), 0) == wanted), 1.0, 0.0).astype(BF16)
    left = jnp.dot(jnp.concatenate([high, mid], axis=1).astype(BF16), pick, preferred_element_type=F32)
    r = iota((128, 128), 1) & 15
    left = jnp.where((r >= 9) & (r < 12), 1.0, left)

    def target_rows(y, mass):
        rows = []
        for v in y:
            a = bf16_part(v)
            rows += [a, a, bf16_part(v - a)]
        return rows + list(split3(mass - (0.5 * ALPHA) * (y[0] * y[0] + y[1] * y[1] + y[2] * y[2])))

    def stacked(rows, at):
        stack = jnp.zeros((16, rows[0].shape[1]), F32)
        sub = iota(stack.shape, 0)
        for q, row in enumerate(rows):
            stack = jnp.where(sub == q, row[at : at + 1, :], stack)
        return stack.astype(BF16)

    tiles = target_rows([turned[16 + 8 * d : 24 + 8 * d, :] for d in range(3)], turned[40:48, :])
    rights = [jnp.concatenate([stacked(tiles, 2 * p), stacked(tiles, 2 * p + 1)], axis=1) for p in range(4)]
    mine = stacked(target_rows([own[d : d + 1, :] for d in range(3)], own[3:4, :]), 0)
    for ci in range(4):
        own_lanes = (left if ci == 0 else pltpu.roll(left, 128 - 16 * ci, 1))[:, :16].astype(BF16)

        def score(right, own_lanes=own_lanes):
            return jnp.dot(own_lanes, right, preferred_element_type=F32)

        peak = None
        for p, right in enumerate(rights):
            v = score(right)
            scores[p] = v
            peak = v if peak is None else jnp.maximum(peak, v)
        terms[128 * ci : 128 * ci + 128, :] = score(mine)
        peak = jnp.max(jnp.maximum(peak[:, :128], peak[:, 128:]), axis=1, keepdims=True)
        total = jnp.exp2(scores[0] - peak)
        for p in range(1, 4):
            total = total + jnp.exp2(scores[p] - peak)
        total = jnp.sum(total[:, :128] + total[:, 128:], axis=1, keepdims=True)
        terms[128 * ci : 128 * ci + 128, :] += table[:, 12 + ci : 13 + ci] - (peak + jnp.log2(total))
    top_g = jnp.full((8, TGT), NEG, F32)
    for i in range(0, 512, 8):
        top_g = jnp.maximum(top_g, terms[i : i + 8, :])
    top = jnp.max(top_g, axis=0, keepdims=True)
    total = jnp.zeros((8, TGT), F32)
    for i in range(0, 512, 8):
        total = total + jnp.exp2(terms[i : i + 8, :] - top)
    g = own[3:4, :] - top - jnp.log2(jnp.sum(total, axis=0, keepdims=True))
    g_out[...] = jnp.broadcast_to(g, g_out.shape)
    at = l_in[...]
    lane = iota((128, 128), 1).astype(F32)
    hit = jnp.where(at == lane, g[:, :128], 0.0) + jnp.where(at == lane + 128.0, g[:, 128:], 0.0)
    picked = jnp.sum(hit, axis=1, keepdims=True)
    r = (r_in[...] + picked).reshape(SLOTS, CL, PTS)
    top = jnp.max(r, axis=0)
    l_out[...] = top + jnp.log2(jnp.sum(jnp.exp2(r - top[None]), axis=0))


def column_kernel(order, g, sp, sm, tp, tm, l0, l1, l2, l3, f_out, s_out, tab, gt, gf, st, fbuf, sem):
    parts = [p[...] for p in (l0, l1, l2, l3)]
    top = functools.reduce(jnp.maximum, parts)
    f = -(top + jnp.log2(sum(jnp.exp2(p - top) for p in parts)))
    fbuf[...] = f * UNSCALE
    send = pltpu.make_async_copy(fbuf, f_out, sem)
    send.start()
    st[...] = jnp.zeros_like(st)
    fill_tables(tab, tp, tm)
    own = f + jnp.log2(sm[...]) - (0.5 * ALPHA) * (sp[0] * sp[0] + sp[1] * sp[1] + sp[2] * sp[2])
    zero = jnp.zeros((CL, PTS), F32)
    source_factors(gf, [sp[d] * ALPHA for d in range(3)], (*split3(own), zero))
    for c in range(CL):
        gt[c] = jnp.concatenate([gf[h, 16 * c : 16 * c + 16, :] for h in range(2)], axis=1).astype(BF16).T
    n = order[LIST - 1]

    def batch(at, size):
        scores = []
        for u in range(size):
            left = gt[(order[at + u] >> 8) & (CL - 1)]
            to = order[at + u] & (TGT - 1)
            scores.append(jnp.dot(left, target_factors(tab, to, g[0, to]), preferred_element_type=F32))
        lines = [jnp.where(at + u < n, exp_sum(scores[u]), 0.0) for u in range(size)]
        for u in range(size):
            to = pl.ds(order[at + u] & (TGT - 1), 1)
            st[to, :] = st[to, :] + lines[u]
        return 0

    whole = n // MANY
    lax.fori_loop(0, whole, lambda i, _: batch(MANY * i, MANY), 0)
    lax.fori_loop(0, (n - MANY * whole + FEW - 1) // FEW, lambda i, _: batch(MANY * whole + FEW * i, FEW), 0)
    s_out[...] = st[...].T.reshape(32, 8, TGT)
    send.wait()


def final_kernel(arrived, mass, g, out):
    total = jnp.sum(arrived[...], axis=0)
    out[...] = (g[...] - jnp.log2(1.0 + total / mass[...])) * UNSCALE


def on_device(src_pts, src_mass, tgt_pts, tgt_mass, listed, live):
    shape = jax.ShapeDtypeStruct
    params = pltpu.CompilerParams(vmem_limit_bytes=LIMIT)
    stages = [pltpu.VMEM((TGT, 16), BF16), pltpu.VMEM((TGT, PTS), F32), pltpu.VMEM((8, PTS), F32)] * AHEAD
    slots = listed.transpose(1, 2, 0).reshape(SLOTS, CL)
    counts = live.transpose(1, 0)
    row, own, mass = pl.pallas_call(
        centroid_kernel,
        out_shape=(shape((128, 128), F32), shape((8, 256), F32), shape((8, 256), F32)),
        in_specs=[VMEM] * 4,
        out_specs=(VMEM, VMEM, VMEM),
        name="centroids",
    )(src_pts, src_mass, tgt_pts, tgt_mass)
    got = lax.all_to_all(row, ("src", "tgt"), split_axis=0, concat_axis=0, tiled=True)
    r, where, order = pl.pallas_call(
        row_kernel,
        out_shape=(shape((BLOCKS, PTS), F32), shape((128, 128), F32), shape((LIST,), I32)),
        in_specs=[SMEM, SMEM, VMEM, VMEM, VMEM],
        out_specs=(VMEM, VMEM, SMEM),
        scratch_shapes=[
            pltpu.VMEM((7, TGT, PTS), F32),
            pltpu.VMEM((CL, 16, PTS), BF16),
            pltpu.VMEM((2, CL * 16, 128), F32),
            pltpu.VMEM((BLOCKS, PTS), F32),
            pltpu.VMEM((BLOCKS, 128), F32),
        ]
        + stages,
        cost_estimate=pl.CostEstimate(flops=100_000_000, bytes_accessed=10_000_000, transcendentals=5_000_000),
        compiler_params=params,
        name="rows",
    )(slots, counts, src_pts, tgt_pts, tgt_mass)
    g, part = pl.pallas_call(
        coarse_kernel,
        out_shape=(shape((8, 256), F32), shape((CL, PTS), F32)),
        in_specs=[VMEM] * 4,
        out_specs=(VMEM, VMEM),
        scratch_shapes=[pltpu.VMEM((512, 256), F32), pltpu.VMEM((4, 128, 256), F32)],
        compiler_params=params,
        name="coarse",
    )(got, own, r, where)
    parts = [part] + [
        lax.ppermute(part, "tgt", [(i, (i + k) % 4) for i in range(4)]) for k in (1, 2, 3)
    ]
    fine_f, sums = pl.pallas_call(
        column_kernel,
        out_shape=(shape((CL, PTS), F32), shape((32, 8, TGT), F32)),
        in_specs=[SMEM, SMEM] + [VMEM] * 8,
        out_specs=(ANY, VMEM),
        scratch_shapes=[
            pltpu.VMEM((7, TGT, PTS), F32),
            pltpu.VMEM((CL, PTS, 16), BF16),
            pltpu.VMEM((2, CL * 16, 128), F32),
            pltpu.VMEM((TGT, PTS), F32),
            pltpu.VMEM((CL, PTS), F32),
            pltpu.SemaphoreType.DMA,
        ],
        compiler_params=params,
        name="columns",
    )(order, g, src_pts, src_mass, tgt_pts, tgt_mass, *parts)
    arrived = lax.all_to_all(sums, "src", split_axis=0, concat_axis=0, tiled=True)
    fine_g = pl.pallas_call(
        final_kernel,
        out_shape=shape((8, TGT), F32),
        in_specs=[VMEM] * 3,
        out_specs=VMEM,
        compiler_params=params,
        name="final",
    )(arrived, mass, g)
    return fine_f, fine_g


def solution(mesh):
    placed = (
        P(None, "src", None),
        P("src", None),
        P(None, None, "tgt"),
        P(None, "tgt"),
        P("src", "tgt", None),
        P("src", "tgt"),
    )
    return jax.shard_map(
        on_device,
        mesh=mesh,
        in_specs=placed,
        out_specs=(P("src", None), P("src", "tgt")),
        check_vma=False,
    )
```
